32 devices in a mesh: shard: 4 (over z), ctx: 4 (over x, core), tp: 2 (over y).
Axes of the slice: x: 2, y: 2, z: 4, core: 2. Of those that a mesh axis runs over, the one named last changes fastest.
Arguments:
- hidden_in: bfloat16 [2, 4, 1024, 2048], P(None, 'shard', 'ctx'), may hold values from -6 to 6
- attn_gain: bfloat16 [2048], P('shard'), may hold values from 0.099609375 to 1.8984375
- query_weight: bfloat16 [2048, 2048], P('shard', 'tp'), may hold values from -0.125 to 0.125
- key_weight: bfloat16 [2048, 2048], P('shard', 'tp'), may hold values from -0.125 to 0.125
- value_weight: bfloat16 [2048, 2048], P('shard', 'tp'), may hold values from -0.125 to 0.125
- conv_weight: bfloat16 [4, 3, 16, 128], P(None, None, 'tp', 'shard'), may hold values from -3 to 3
- beta_weight: bfloat16 [2048, 16], P('shard', 'tp'), may hold values from -0.125 to 0.125
- out_gain: bfloat16 [128], P('shard'), may hold values from 0.099609375 to 1.8984375
- out_weight: bfloat16 [2048, 2048], P('tp', 'shard'), may hold values from -0.125 to 0.125
- ffn_gain: bfloat16 [2048], P('shard'), may hold values from 0.099609375 to 1.8984375
- gate_weight: bfloat16 [2048, 5632], P('shard', 'tp'), may hold values from -0.125 to 0.125
- up_weight: bfloat16 [2048, 5632], P('shard', 'tp'), may hold values from -0.125 to 0.125
- down_weight: bfloat16 [5632, 2048], P('tp', 'shard'), may hold values from -0.078125 to 0.078125
- cotangent: bfloat16 [2, 4, 1024, 2048], P(None, 'shard', 'ctx'), may hold values from -6 to 6
- segment_ids: int32 [2, 4, 1024], P(None, 'shard', 'ctx'), may hold values from 0 to 3, never falling along the last dimension, each value on 1 to 512 neighbouring positions
Outputs:
- hidden_out: bfloat16 [2, 4, 1024, 2048], P(None, 'shard', 'ctx')
- grad_input: bfloat16 [2, 4, 1024, 2048], P(None, 'shard', 'ctx')
- grad_attn_gain: float32 [2048], P('shard')
- grad_query: float32 [2048, 2048], P('shard', 'tp')
- grad_key: float32 [2048, 2048], P('shard', 'tp')
- grad_value: float32 [2048, 2048], P('shard', 'tp')
- grad_conv: float32 [4, 3, 16, 128], P(None, None, 'tp', 'shard')
- grad_beta: float32 [2048, 16], P('shard', 'tp')
- grad_out_gain: float32 [128], P('shard')
- grad_out_weight: float32 [2048, 2048], P('tp', 'shard')
- grad_ffn_gain: float32 [2048], P('shard')
- grad_gate: float32 [2048, 5632], P('shard', 'tp')
- grad_up: float32 [2048, 5632], P('shard', 'tp')
- grad_down: float32 [5632, 2048], P('tp', 'shard')
The draws below stay inside these ranges and needn't reach their ends.
Inputs may be any that keep to these rules, and one draw needn't show every extreme that they name: `segment_ids`: in each sequence of 1024 tokens the ids never fall from one token to the next, begin at 0, and each id covers one to 512 consecutive tokens; each id is one document.
All inputs are finite; a program needn't handle non-finite values.
Results may differ from the reference program's by a relative error of at most 0.023.
Values may be sent and summed in bfloat16 or wider, within the bound.
No kernel may reach another device: no remote copies, remote signals or barrier semaphores. Data moves between devices by JAX's collectives and lax.ppermute only.
A program may use at most 320 MiB of HBM per device.

```python
import math
import jax
import jax.numpy as jnp
import numpy as np
from jax import lax

D = 2048
HEADS = 16
HD = 128
FF = 5632
CONV = 4
BLOCK = 64
SEGS = 4
MB = 2
LEN = 1024
BATCH = 4
MOST_DOC = 512


def block_levels(own_key, shape, shards, least, top_value):
    def one(axis_at, parts):
        steps = jax.random.uniform(jax.random.fold_in(jax.random.fold_in(own_key, 6), axis_at), (parts,), jnp.float32, least / len(shards), top_value / len(shards))
        return jnp.repeat(jnp.exp(steps), shape[axis_at] // parts).reshape((-1,) + (1,) * (len(shape) - axis_at - 1))

    level = one(*shards[0])
    for cut in shards[1:]:
        level = level * one(*cut)
    return level


def split_up(count, total, reach, lean):
    weights = [(1 << 20) // math.isqrt(grade ** lean) + 1 for grade in range(2, count + 1)]
    rest, counts = total - reach - (count - 1), [1] * (count - 1)
    while rest > 0:
        free = [i for i in range(count - 1) if counts[i] < reach]
        pool, left = sum([weights[i] for i in free]), rest
        for i in free:
            addition = min(reach - counts[i], max(1, left * weights[i] // pool), rest)
            counts[i] = counts[i] + addition
            rest = rest - addition
    return np.array([reach] + counts)


def uneven(stream_key, amount, total, limit, lean):
    if amount == 2:
        one = jax.random.randint(stream_key, (), max(1, total - limit), min(limit, total - 1) + 1)
        return jnp.stack([one, total - one])
    sizes = jnp.asarray(split_up(amount, total, limit, lean), jnp.int32)
    pairs = (amount - 1) // 2
    donor, sink = sizes[1:1 + 2 * pairs:2], sizes[2:2 + 2 * pairs:2]
    margin = jnp.minimum(donor - 1, limit - sink)
    shifted = jax.random.randint(jax.random.fold_in(stream_key, 1), (pairs,), 0, 1 << 20) % (margin + 1)
    sizes = sizes.at[1:1 + 2 * pairs:2].set(donor - shifted).at[2:2 + 2 * pairs:2].set(sink + shifted)
    return sizes[jax.random.permutation(jax.random.fold_in(stream_key, 2), amount)]


def normal_values(own_key, shape, spread, most, cuts=(), kind=jnp.bfloat16):
    values = spread * jax.random.normal(own_key, shape, jnp.float32)
    if cuts:
        values = values * block_levels(own_key, shape, cuts, -0.22, 0.18)
    return jnp.clip(values, -most, most).astype(kind)


def setup_inputs(seed: int = 0) -> dict:
    keys = jax.random.split(jax.random.key(seed), 16)
    return {
        "hidden_in": normal_values(keys[0], (MB, BATCH, LEN, D), 1.0, 6.0, ((1, 4), (2, 4))),
        "attn_gain": jnp.clip(1.0 + 0.18 * jax.random.normal(keys[1], (D,), jnp.float32), 0.099609375, 1.8984375).astype(jnp.bfloat16),
        "query_weight": normal_values(keys[2], (D, D), D ** -0.5, 0.125, ((0, 4), (1, 2))),
        "key_weight": normal_values(keys[3], (D, D), D ** -0.5, 0.125, ((0, 4), (1, 2))),
        "value_weight": normal_values(keys[4], (D, D), D ** -0.5, 0.125, ((0, 4), (1, 2))),
        "conv_weight": normal_values(keys[5], (CONV, 3, HEADS, HD), 0.5, 3.0, ((2, 2), (3, 4))),
        "beta_weight": normal_values(keys[6], (D, HEADS), D ** -0.5, 0.125, ((0, 4), (1, 2))),
        "out_gain": jnp.clip(1.0 + 0.18 * jax.random.normal(keys[7], (HD,), jnp.float32), 0.099609375, 1.8984375).astype(jnp.bfloat16),
        "out_weight": normal_values(keys[8], (D, D), D ** -0.5, 0.125, ((0, 2), (1, 4))),
        "ffn_gain": jnp.clip(1.0 + 0.18 * jax.random.normal(keys[9], (D,), jnp.float32), 0.099609375, 1.8984375).astype(jnp.bfloat16),
        "gate_weight": normal_values(keys[10], (D, FF), D ** -0.5, 0.125, ((0, 4), (1, 2))),
        "up_weight": normal_values(keys[11], (D, FF), D ** -0.5, 0.125, ((0, 4), (1, 2))),
        "down_weight": normal_values(keys[12], (FF, D), FF ** -0.5, 0.078125, ((0, 2), (1, 4))),
        "cotangent": normal_values(keys[13], (MB, BATCH, LEN, D), 1.0, 6.0, ((1, 4), (2, 4))),
        "segment_ids": jax.vmap(lambda own: jnp.searchsorted(jnp.cumsum(uneven(own, SEGS, LEN, MOST_DOC, 2)), jnp.arange(LEN), side="right"))(jax.random.split(keys[14], MB * BATCH)).reshape((MB, BATCH, LEN)).astype(jnp.int32),
    }


EPSILON = 1e-06
HIGHEST = lax.Precision.HIGHEST

@jax.custom_vjp
def low(v):
    return lax.optimization_barrier(v.astype(jnp.bfloat16)).astype(jnp.float32)

@jax.custom_vjp
def low_back(v):
    return v

def low_keep(v):
    return (low(v), None)

def low_pass(kept, grad):
    return (grad,)

def back_keep(v):
    return (v, None)

def back_low(kept, grad):
    return (low(grad),)
low.defvjp(low_keep, low_pass)
low_back.defvjp(back_keep, back_low)

def rounded(values):
    return low_back(low(values))

def matmul(left, right):
    return jnp.dot(left, right, precision=HIGHEST, preferred_element_type=jnp.float32)

def rms_scale(values, gain):
    return values * lax.rsqrt(lax.optimization_barrier(jnp.mean(values * values, axis=-1, keepdims=True)) + EPSILON) * gain

def unit_rows(values):
    return values * lax.rsqrt(lax.optimization_barrier(jnp.sum(values * values, axis=-1, keepdims=True)) + EPSILON)

def delta_block(state, block):

    def token(carry, item):
        query_row, key_row, value_row, rate_row, start_row = item
        carry = carry * (1.0 - start_row)
        error = value_row - jnp.einsum('hvk,hk->hv', carry, key_row, precision=HIGHEST)
        carry = carry + rate_row[:, None, None] * error[:, :, None] * key_row[:, None, :]
        result = jnp.einsum('hvk,hk->hv', carry, query_row, precision=HIGHEST)
        return (carry, result)
    return lax.scan(token, state, block)

def recurrence(queries, key_rows, value_rows, rates, starts):
    length = queries.shape[0]
    count = length // BLOCK
    blocks = (queries.reshape(count, BLOCK, HEADS, HD), key_rows.reshape(count, BLOCK, HEADS, HD), value_rows.reshape(count, BLOCK, HEADS, HD), rates.reshape(count, BLOCK, HEADS), starts.reshape(count, BLOCK))
    initial = jnp.zeros((HEADS, HD, HD), jnp.float32)
    final_state, results = lax.scan(jax.checkpoint(delta_block), initial, blocks)
    return results.reshape(length, HEADS, HD) * (1.0 / math.sqrt(HD))

def short_conv(raw, taps, segments):
    length, channels = raw.shape
    padded = jnp.concatenate([jnp.zeros((CONV - 1, channels), raw.dtype), raw], axis=0)
    padded_ids = jnp.concatenate([jnp.full((CONV - 1,), -1, jnp.int32), segments.astype(jnp.int32)])
    total = jnp.zeros((length, channels), raw.dtype)
    for tap_index in range(CONV):
        same_doc = (padded_ids[tap_index:tap_index + length] == segments).astype(raw.dtype)
        total = total + taps[tap_index] * padded[tap_index:tap_index + length] * same_doc[:, None]
    return total

def forward(hidden, attn_gain, query_weight, key_weight, value_weight, conv_weight, beta_weight, out_gain, out_weight, ffn_gain, gate_weight, up_weight, down_weight, segments):
    length = hidden.shape[0]
    normed_in = low(rms_scale(hidden, attn_gain))
    raws = [rounded(matmul(normed_in, weight)) for weight in (query_weight, key_weight, value_weight)]
    rates = jax.nn.sigmoid(low_back(matmul(normed_in, beta_weight)))
    previous = jnp.concatenate([jnp.full((1,), -1, jnp.int32), segments[:-1].astype(jnp.int32)])
    starts = (segments != previous).astype(hidden.dtype)
    acts = [jax.nn.silu(short_conv(raws[index], conv_weight[:, index].reshape(CONV, D), segments)) for index in range(3)]
    queries = rounded(unit_rows(acts[0].reshape(length, HEADS, HD)))
    key_rows = rounded(unit_rows(acts[1].reshape(length, HEADS, HD)))
    value_rows = rounded(acts[2].reshape(length, HEADS, HD))
    mixed = recurrence(queries, key_rows, value_rows, rates, starts)
    head_normed = rounded(rms_scale(mixed, out_gain)).reshape(length, D)
    resid = hidden + low_back(matmul(head_normed, out_weight))
    normed_ffn = low(rms_scale(resid, ffn_gain))
    gate = low_back(matmul(normed_ffn, gate_weight))
    upward = low_back(matmul(normed_ffn, up_weight))
    act_ffn = rounded(jax.nn.silu(gate) * upward)
    return resid + low_back(matmul(act_ffn, down_weight))

def reference(hidden_in, attn_gain, query_weight, key_weight, value_weight, conv_weight, beta_weight, out_gain, out_weight, ffn_gain, gate_weight, up_weight, down_weight, cotangent, segment_ids):
    weights = tuple((weight.astype(jnp.float32) for weight in (attn_gain, query_weight, key_weight, value_weight, conv_weight, beta_weight, out_gain, out_weight, ffn_gain, gate_weight, up_weight, down_weight)))
    inputs = hidden_in.reshape(-1, LEN, D).astype(jnp.float32)
    grads_in = cotangent.reshape(-1, LEN, D).astype(jnp.float32)
    documents = segment_ids.reshape(-1, LEN)

    def one_sequence(totals, item):
        hidden, incoming, segments = item

        def layer(values, *params):
            return forward(values, *params, segments)
        result, pullback = jax.vjp(layer, hidden, *weights)
        grads = pullback(incoming)
        return (tuple((total + grad for total, grad in zip(totals, grads[1:]))), (result, grads[0]))
    initial = tuple((jnp.zeros_like(weight) for weight in weights))
    totals, (results, input_grads) = lax.scan(one_sequence, initial, (inputs, grads_in, documents))
    shape = hidden_in.shape
    return (results.reshape(shape).astype(jnp.bfloat16), input_grads.reshape(shape).astype(jnp.bfloat16), totals[0], totals[1], totals[2], totals[3], totals[4], totals[5], totals[6], totals[7], totals[8], totals[9], totals[10], totals[11])
```

```python
import functools

import jax
import jax.numpy as jnp
from jax import lax
from jax.experimental import pallas as pl
from jax.experimental.pallas import tpu as pltpu
from jax.sharding import Mesh
from jax.sharding import PartitionSpec as P

EPSILON = 1e-06
F32 = jnp.float32
BF16 = jnp.bfloat16
LANES = 128
HALO = 16
SWAP = [(0, 1), (1, 0)]


def mm(left, right, left_dim, right_dim):
    return lax.dot_general(
        left.astype(BF16),
        right.astype(BF16),
        (((left_dim,), (right_dim,)), ((), ())),
        preferred_element_type=F32,
    )


def nn(left, right):
    return mm(left, right, 1, 0)


def nt(left, right):
    return mm(left, right, 1, 1)


def tn(left, right):
    return mm(left, right, 0, 0)


def place_scalars():
    return jnp.stack([lax.axis_index("core"), lax.axis_index("cx")]).astype(jnp.int32)


def call(kernel, grid, in_specs, out_specs, out_shape, scratch=(), flops=0, moved=0):
    return pl.pallas_call(
        kernel,
        grid_spec=pltpu.PrefetchScalarGridSpec(
            num_scalar_prefetch=1,
            grid=grid,
            in_specs=in_specs,
            out_specs=out_specs,
            scratch_shapes=list(scratch),
        ),
        out_shape=out_shape,
        compiler_params=pltpu.CompilerParams(
            dimension_semantics=("arbitrary",) * len(grid), vmem_limit_bytes=48 << 20
        ),
        cost_estimate=pl.CostEstimate(flops=flops, transcendentals=0, bytes_accessed=moved),
    )


def split_rows(places, values, count):
    rows, width = values.shape
    half = width // (2 * count)
    if half % LANES:
        cut = values.reshape(rows, count, 2, half)
        cut = jnp.where(places[1] == 0, cut, cut[:, :, ::-1])
        return cut.transpose(2, 0, 1, 3).reshape(2, rows, width // 2)
    tile = max(t for t in range(16, 400, 16) if rows % t == 0)

    def kernel(where, source, target):
        for side in range(2):
            for shard in range(count):
                at = shard * 2 * half + (where[1] if side == 0 else 1 - where[1]) * half
                target[side, :, shard * half : (shard + 1) * half] = source[
                    :, pl.ds(pl.multiple_of(at, LANES), half)
                ]

    return call(
        kernel,
        (rows // tile,),
        [pl.BlockSpec((tile, width), lambda i, w: (i, 0))],
        pl.BlockSpec((2, tile, width // 2), lambda i, w: (0, i, 0)),
        jax.ShapeDtypeStruct((2, rows, width // 2), values.dtype),
        moved=2 * values.size * values.dtype.itemsize,
    )(places, values)


def join_rows(places, values, count):
    rows, width = values.shape[1], 2 * values.shape[2]
    half = width // (2 * count)
    if half % LANES:
        cut = values.reshape(2, rows, count, half).transpose(1, 2, 0, 3)
        cut = jnp.where(places[1] == 0, cut, cut[:, :, ::-1])
        return cut.reshape(rows, width)
    tile = max(t for t in range(16, 400, 16) if rows % t == 0)

    def kernel(where, source, target):
        for side in range(2):
            for shard in range(count):
                at = shard * 2 * half + (where[1] if side == 0 else 1 - where[1]) * half
                target[:, pl.ds(pl.multiple_of(at, LANES), half)] = source[
                    side, :, shard * half : (shard + 1) * half
                ]

    return call(
        kernel,
        (rows // tile,),
        [pl.BlockSpec((2, tile, width // 2), lambda i, w: (0, i, 0))],
        pl.BlockSpec((tile, width), lambda i, w: (i, 0)),
        jax.ShapeDtypeStruct((rows, width), values.dtype),
        moved=2 * values.size * values.dtype.itemsize,
    )(places, values)


def split_small(places, values, count):
    cut = values.reshape((count, 2, values.shape[0] // (2 * count)) + values.shape[1:])
    cut = jnp.where(places[1] == 0, cut, cut[:, ::-1])
    cut = jnp.swapaxes(cut, 0, 1)
    return cut.reshape((2, values.shape[0] // 2) + values.shape[1:])


def join_small(places, values, count):
    cut = values.reshape((2, count, values.shape[1] // count) + values.shape[2:])
    cut = jnp.swapaxes(cut, 0, 1)
    cut = jnp.where(places[1] == 0, cut, cut[:, ::-1])
    return cut.reshape((2 * values.shape[1],) + values.shape[2:])


def pack_heads(places, query, key, value, heads):
    half = query.shape[0] // 2

    def kernel(where, query_ref, key_ref, value_ref, out):
        out[:, :LANES] = query_ref[...]
        out[:, LANES : 2 * LANES] = key_ref[...]
        out[:, 2 * LANES :] = value_ref[...]

    spec = pl.BlockSpec((half, LANES), lambda h, w: (w[1], w[0] * heads + h))
    return call(
        kernel,
        (heads,),
        [spec] * 3,
        pl.BlockSpec((half, 3 * LANES), lambda h, w: (0, h)),
        jax.ShapeDtypeStruct((half, 3 * LANES * heads), query.dtype),
    )(places, query, key, value)


def own_block(places, weight):
    half, columns = weight.shape[0] // 2, weight.shape[1] // 2
    return lax.dynamic_slice(weight, (places[1] * half, places[0] * columns), (half, columns))


def own_block_turned(places, weight):
    rows, half = weight.shape[0] // 2, weight.shape[1] // 2
    return lax.dynamic_slice(weight, (places[0] * rows, places[1] * half), (rows, half)).T


def pieces_of(own):
    across = lax.ppermute(own, "cx", SWAP)
    return [own, across, lax.ppermute(own, "core", SWAP), lax.ppermute(across, "core", SWAP)]


def pick(where, core, cx, refs, store):
    which = 2 * jnp.bitwise_xor(where[0], core) + jnp.bitwise_xor(where[1], cx)
    for index in range(4):

        @pl.when(which == index)
        def _():
            store(refs[index][...].astype(F32))


def lay_heads(places, pieces, heads):
    half = pieces[0].shape[0]
    width = heads * LANES

    def kernel(where, a, b, c, d, *outs):
        def store(values):
            for head in range(heads):
                for index in range(3):
                    at = (head * 3 + index) * LANES
                    outs[index][:, head * LANES : (head + 1) * LANES] = values[:, at : at + LANES]

        pick(where, pl.program_id(1), pl.program_id(0), (a, b, c, d), store)

    return call(
        kernel,
        (2, 2),
        [pl.BlockSpec(pieces[0].shape, lambda i, j, w: (0, 0))] * 4,
        [pl.BlockSpec((half, width), lambda i, j, w: (i, j))] * 3,
        [jax.ShapeDtypeStruct((2 * half, 2 * width), F32)] * 3,
        moved=10 * pieces[0].size * 4,
    )(places, *pieces)


def lay_block(places, pieces):
    half, columns = pieces[0].shape

    def kernel(where, a, b, c, d, out):
        def store(values):
            out[...] = values

        pick(where, pl.program_id(1), pl.program_id(0), (a, b, c, d), store)

    return call(
        kernel,
        (2, 2),
        [pl.BlockSpec((half, columns), lambda i, j, w: (0, 0))] * 4,
        pl.BlockSpec((half, columns), lambda i, j, w: (i, j)),
        jax.ShapeDtypeStruct((2 * half, 2 * columns), F32),
        moved=6 * pieces[0].size * 4,
    )(places, *pieces)


def lay_block_turned(places, pieces):
    half, rows = pieces[0].shape

    def kernel(where, a, b, c, d, out):
        for side in range(2):

            def store(values):
                out[:, side * half : (side + 1) * half] = values.T

            pick(where, pl.program_id(0), side, (a, b, c, d), store)

    return call(
        kernel,
        (2,),
        [pl.BlockSpec((half, rows), lambda i, w: (0, 0))] * 4,
        pl.BlockSpec((rows, 2 * half), lambda i, w: (i, 0)),
        jax.ShapeDtypeStruct((2 * rows, 2 * half), F32),
        moved=6 * pieces[0].size * 4,
    )(places, *pieces)


def fill_ext(ext, index, halo, first, second, size):
    ext[index, :HALO, :] = halo[...].astype(F32)
    ext[index, HALO : HALO + size, :] = first[...].astype(F32)
    ext[index, HALO + size :, :] = second[...].astype(F32)


def links_of(ids, total):
    own = ids[0, HALO : HALO + total, :]
    return [
        (ids[0, HALO - 3 + tap : HALO - 3 + tap + total, :] == own).astype(F32) for tap in range(4)
    ]


def conv_of(ext, index, taps, links, total):
    result = None
    for tap in range(4):
        term = (
            taps[index, 0, tap : tap + 1, :]
            * ext[index, HALO - 3 + tap : HALO - 3 + tap + total, :]
            * links[tap]
        )
        result = term if result is None else result + term
    return result


def sigmoid(values):
    return 1.0 / (1.0 + jnp.exp(-values))


def column_of(values, head):
    lane = lax.broadcasted_iota(jnp.int32, values.shape, 1)
    return jnp.sum(jnp.where(lane == head, values, 0.0), axis=1, keepdims=True)


def marks(ids, rows, chunk, size):
    start = HALO + chunk * size
    column = ids[0, start : start + size, :]
    before = ids[0, start - 1 : start, :]
    last = ids[0, start + size - 1 : start + size, :]
    first = (column == before).astype(F32)
    tail = (column == last).astype(F32)
    whole = (last == before).astype(F32)
    same = column == rows[0, chunk : chunk + 1, :]
    row = lax.broadcasted_iota(jnp.int32, (size, size), 0)
    col = lax.broadcasted_iota(jnp.int32, (size, size), 1)
    return first, tail, whole, same & (row > col), same & (row >= col)


def inverse_unit(strict, size):
    row = lax.broadcasted_iota(jnp.int32, (size, size), 0)
    col = lax.broadcasted_iota(jnp.int32, (size, size), 1)
    mixed = jnp.bitwise_xor(row, col)
    result = jnp.where(row == col, 1.0, jnp.where(mixed == 1, -strict, 0.0))
    block = 2
    while block < size:
        part = jnp.where((mixed >= block) & (mixed < 2 * block), strict, 0.0).astype(BF16)
        low = result.astype(BF16)
        result = result - nn(low, nn(part, low))
        block *= 2
    return result


def forward_one(where, q0, k0, v0, q1, k1, v1, qh, kh, vh, taps, ids, rows, r0, r1, *rest, size):
    query, key, value, inverse, final, ext = rest
    head = pl.program_id(1)
    total = 2 * size
    for index, group in enumerate(((qh, q0, q1), (kh, k0, k1), (vh, v0, v1))):
        fill_ext(ext, index, *group, size)
    links = links_of(ids, total)
    out = []
    for index in range(3):
        conv = conv_of(ext, index, taps, links, total)
        act = conv * sigmoid(conv)
        if index < 2:
            act = act * lax.rsqrt(jnp.sum(act * act, axis=1, keepdims=True) + EPSILON)
        out.append(act.astype(BF16))
    for target, values in zip((query, key, value), out):
        target[0, 0] = values[:size]
        target[0, 1] = values[size:]
    state = None
    for chunk, rates in enumerate((r0, r1)):
        first, tail, whole, strict, _ = marks(ids, rows, chunk, size)
        rate = column_of(rates[...], head)
        keys = out[1][chunk * size : (chunk + 1) * size]
        fresh = out[2][chunk * size : (chunk + 1) * size].astype(F32)
        inv = inverse_unit(jnp.where(strict, rate * nt(keys, keys), 0.0), size).astype(BF16)
        inverse[0, 0, chunk] = inv
        if chunk:
            fresh = fresh - first * nt(keys, state)
        fresh = nn(inv, rate * fresh)
        added = tn(tail * fresh, keys)
        state = added if state is None else whole * state + added
    final[0, 0] = state.astype(BF16)


def forward_two(where, query, key, value, inverse, ids, rows, r0, r1, incoming, gain, *rest, size, scale):
    head_low, mixed_out, fresh_out, middle = rest
    head = pl.program_id(1)
    state = incoming[0, 0].astype(F32)
    for chunk, rates in enumerate((r0, r1)):
        first, tail, whole, _, lower = marks(ids, rows, chunk, size)
        rate = column_of(rates[...], head)
        keys, queries = key[0, chunk], query[0, chunk]
        if chunk:
            middle[0, 0] = state.astype(BF16)
        rest_rows = value[0, chunk].astype(F32) - first * nt(keys, state)
        fresh = nn(inverse[0, 0, chunk], rate * rest_rows)
        fresh_out[0, chunk] = fresh.astype(BF16)
        inner = jnp.where(lower, nt(queries, keys), 0.0)
        mixed = scale * (first * nt(queries, state) + nn(inner, fresh))
        mixed_out[0, chunk] = mixed
        normed = mixed * lax.rsqrt(jnp.mean(mixed * mixed, axis=1, keepdims=True) + EPSILON)
        slot = where[0] if chunk == 0 else 1 - where[0]
        head_low[slot, 0] = (normed * gain[...]).astype(BF16)
        if chunk == 0:
            state = whole * state + tn(tail * fresh, keys)


def backward_one(where, d_head, mixed, query, key, inverse, ids, rows, r0, r1, gain, *rest, size, scale):
    d_out, d_state_out, d_gain = rest
    head = pl.program_id(1)
    total = jnp.zeros((1, LANES), F32)
    d_state = None
    for chunk in (1, 0):
        first, tail, whole, _, lower = marks(ids, rows, chunk, size)
        rate = column_of((r0, r1)[chunk][...], head)
        keys, queries = key[0, chunk], query[0, chunk]
        slot = where[0] if chunk == 0 else 1 - where[0]
        grad = d_head[slot, 0].astype(F32)
        values = mixed[0, chunk]
        inv_rms = lax.rsqrt(jnp.mean(values * values, axis=1, keepdims=True) + EPSILON)
        normed = values * inv_rms
        total = total + jnp.sum(grad * normed, axis=0, keepdims=True)
        scaled = grad * gain[...]
        d_mixed = inv_rms * (scaled - normed * jnp.mean(scaled * normed, axis=1, keepdims=True))
        d_low = (scale * d_mixed).astype(BF16)
        d_out[0, chunk] = d_low
        inner = jnp.where(lower, nt(queries, keys), 0.0)
        d_fresh = tn(inner, d_low)
        if d_state is not None:
            d_fresh = d_fresh + tail * nt(keys, d_state)
        d_rest = rate * tn(inverse[0, 0, chunk], d_fresh)
        change = tn(first * d_low.astype(F32), queries) - tn(first * d_rest, keys)
        d_state = change if d_state is None else whole * d_state + change
    d_state_out[0, 0] = d_state.astype(BF16)
    d_gain[0, 0] = jnp.broadcast_to(total, (8, LANES))


def backward_two(where, q0, k0, v0, q1, k1, v1, qh, kh, vh, taps, ids, rows, r0, r1, *rest, size):
    query, key, value, inverse, fresh_in, d_in, incoming, middle, d_final = rest[:9]
    d_raw, d_edge, d_rates, d_taps = rest[9:13]
    ext, d_ext, d_rows = rest[13:]
    head = pl.program_id(1)
    total = 2 * size
    for index, group in enumerate(((qh, q0, q1), (kh, k0, k1), (vh, v0, v1))):
        fill_ext(ext, index, *group, size)
    d_state = d_final[0, 0].astype(F32)

    @pl.when(head == 0)
    def _():
        d_rates[...] = jnp.zeros_like(d_rates)

    for chunk in (1, 0):
        first, tail, whole, strict, lower = marks(ids, rows, chunk, size)
        rate = column_of((r0, r1)[chunk][...], head)
        keys, queries, fresh = key[0, chunk], query[0, chunk], fresh_in[0, chunk]
        inv, d_low = inverse[0, 0, chunk], d_in[0, chunk]
        state = (middle if chunk else incoming)[0, 0]
        d_mix = d_low.astype(F32)
        inner = jnp.where(lower, nt(queries, keys), 0.0)
        gram = jnp.where(strict, nt(keys, keys), 0.0)
        d_fresh = tn(inner, d_low) + tail * nt(keys, d_state)
        turned = tn(inv, d_fresh)
        d_rest = rate * turned
        rest_rows = value[0, chunk].astype(F32) - first * nt(keys, state)
        error = rest_rows - nn(gram, fresh)
        d_rate = jnp.sum(turned * error, axis=1, keepdims=True) * rate * (1.0 - rate)
        d_inner = jnp.where(lower, nt(d_low, fresh), 0.0)
        d_gram = rate * jnp.where(strict, -nt(turned, fresh), 0.0)
        d_query = first * nn(d_low, state) + nn(d_inner, keys)
        d_key = (
            tn(d_inner, queries)
            + tail * nn(fresh, d_state)
            - nn(first * d_rest, state)
            + nn(d_gram, keys)
            + tn(d_gram, keys)
        )
        for index, values in enumerate((d_query, d_key, d_rest)):
            d_rows[index, chunk * size : (chunk + 1) * size, :] = values
        lane = lax.broadcasted_iota(jnp.int32, (size, LANES), 1)
        d_rates[0, chunk] = d_rates[0, chunk] + jnp.where(lane == head, d_rate, 0.0)
        if chunk:
            d_state = (
                whole * d_state + tn(first * d_mix, queries) - tn(first * d_rest, keys)
            )
    links = links_of(ids, total)
    for index in range(3):
        conv = conv_of(ext, index, taps, links, total)
        sig = sigmoid(conv)
        d_act = d_rows[index].astype(BF16).astype(F32)
        if index < 2:
            act = conv * sig
            inv_norm = lax.rsqrt(jnp.sum(act * act, axis=1, keepdims=True) + EPSILON)
            unit = act * inv_norm
            d_act = (d_act - unit * jnp.sum(unit * d_act, axis=1, keepdims=True)) * inv_norm
        d_conv = d_act * sig * (1.0 + conv * (1.0 - sig))
        d_ext[...] = jnp.zeros_like(d_ext)
        for tap in range(4):
            window = slice(HALO - 3 + tap, HALO - 3 + tap + total)
            linked = d_conv * links[tap]
            d_taps[0, index, 0, tap : tap + 1, :] = jnp.sum(
                linked * ext[index, window, :], axis=0, keepdims=True
            )
            d_ext[window, :] = d_ext[window, :] + taps[index, 0, tap : tap + 1, :] * linked
        lanes = slice(index * LANES, (index + 1) * LANES)
        d_edge[0, :, lanes] = d_ext[:HALO, :].astype(BF16)
        d_raw[where[0], 0, :, lanes] = d_ext[HALO : HALO + size, :].astype(BF16)
        d_raw[1 - where[0], 0, :, lanes] = d_ext[HALO + size :, :].astype(BF16)


def mixer_calls(places, raw, rates, ids, rows, taps, gain, heads, seqs, size, scale):
    width = heads * LANES
    columns = 3 * width

    def raw_spec(chunk, part):
        def index(b, h, w):
            slot = w[0] if chunk == 0 else 1 - w[0]
            return (slot * seqs + b, 3 * h + part)

        return pl.BlockSpec((size, LANES), index)

    def rate_spec(chunk):
        def index(b, h, w):
            slot = w[0] if chunk == 0 else 1 - w[0]
            return (slot * seqs + b, 0)

        return pl.BlockSpec((size, LANES), index)

    halo_base = 2 * seqs * size // HALO

    def halo_spec(part):
        return pl.BlockSpec((HALO, LANES), lambda b, h, w: (halo_base + b, 3 * h + part))

    raw_specs = [raw_spec(c, p) for c in range(2) for p in range(3)] + [halo_spec(p) for p in range(3)]
    conv_specs = raw_specs + [
        pl.BlockSpec((3, 1, 4, LANES), lambda b, h, w: (0, h, 0, 0)),
        pl.BlockSpec((1, HALO + 2 * size, 1), lambda b, h, w: (b, 0, 0)),
        pl.BlockSpec((1, 2, size), lambda b, h, w: (b, 0, 0)),
        rate_spec(0),
        rate_spec(1),
    ]
    conv_args = (raw,) * 9 + (taps, ids, rows, rates, rates)
    id_specs, id_args = conv_specs[10:], conv_args[10:]
    act_spec = pl.BlockSpec((1, 2, size, LANES), lambda b, h, w: (b, 0, 0, h))
    act_shape = (seqs, 2, size, width)
    state_spec = pl.BlockSpec((1, 1, LANES, LANES), lambda b, h, w: (b, h, 0, 0))
    state_shape = jax.ShapeDtypeStruct((seqs, heads, LANES, LANES), BF16)
    inv_spec = pl.BlockSpec((1, 1, 2, size, size), lambda b, h, w: (b, h, 0, 0, 0))
    slot_spec = pl.BlockSpec((2, 1, size, LANES), lambda b, h, w: (0, b, 0, h))
    slot_shape = (2, seqs, size, width)
    gain_spec = pl.BlockSpec((1, LANES), lambda b, h, w: (0, 0))
    low = jax.ShapeDtypeStruct(act_shape, BF16)
    grid = (seqs, heads)
    steps = seqs * heads
    unit = 2 * size * size * LANES

    def one():
        return call(
            functools.partial(forward_one, size=size),
            grid,
            conv_specs,
            [act_spec] * 3 + [inv_spec, state_spec],
            [low] * 3
            + [jax.ShapeDtypeStruct((seqs, heads, 2, size, size), BF16), state_shape],
            [pltpu.VMEM((3, HALO + 2 * size, LANES), F32)],
            flops=steps * 64 * unit,
            moved=12 << 20,
        )(places, *conv_args)

    def two(query, key, value, inverse, incoming):
        return call(
            functools.partial(forward_two, size=size, scale=scale),
            grid,
            [act_spec] * 3 + [inv_spec] + id_specs + [state_spec, gain_spec],
            [slot_spec, act_spec, act_spec, state_spec],
            [
                jax.ShapeDtypeStruct(slot_shape, BF16),
                jax.ShapeDtypeStruct(act_shape, F32),
                low,
                state_shape,
            ],
            flops=steps * 10 * unit,
            moved=10 << 20,
        )(places, query, key, value, inverse, *id_args, incoming, gain)

    def three(d_head, mixed, query, key, inverse):
        return call(
            functools.partial(backward_one, size=size, scale=scale),
            grid,
            [slot_spec, act_spec, act_spec, act_spec, inv_spec] + id_specs + [gain_spec],
            [act_spec, state_spec, pl.BlockSpec((1, 1, 8, LANES), lambda b, h, w: (b, h, 0, 0))],
            [low, state_shape, jax.ShapeDtypeStruct((seqs, heads, 8, LANES), F32)],
            flops=steps * 16 * unit,
            moved=10 << 20,
        )(places, d_head, mixed, query, key, inverse, *id_args, gain)

    def four(query, key, value, inverse, fresh, d_low, incoming, middle, d_final):
        return call(
            functools.partial(backward_two, size=size),
            grid,
            conv_specs + [act_spec] * 3 + [inv_spec, act_spec, act_spec] + [state_spec] * 3,
            [
                pl.BlockSpec((2, 1, size, 3 * LANES), lambda b, h, w: (0, b, 0, h)),
                pl.BlockSpec((1, HALO, 3 * LANES), lambda b, h, w: (b, 0, h)),
                pl.BlockSpec((1, 2, size, LANES), lambda b, h, w: (b, 0, 0, 0)),
                pl.BlockSpec((1, 3, 1, 4, LANES), lambda b, h, w: (b, 0, h, 0, 0)),
            ],
            [
                jax.ShapeDtypeStruct((2, seqs, size, columns), BF16),
                jax.ShapeDtypeStruct((seqs, HALO, columns), BF16),
                jax.ShapeDtypeStruct((seqs, 2, size, LANES), F32),
                jax.ShapeDtypeStruct((seqs, 3, heads, 4, LANES), F32),
            ],
            [
                pltpu.VMEM((3, HALO + 2 * size, LANES), F32),
                pltpu.VMEM((HALO + 2 * size, LANES), F32),
                pltpu.VMEM((3, 2 * size, LANES), F32),
            ],
            flops=steps * 40 * unit,
            moved=20 << 20,
        )(
            places,
            *conv_args,
            query,
            key,
            value,
            inverse,
            fresh,
            d_low,
            incoming,
            middle,
            d_final,
        )

    return one, two, three, four


def dot_nn(left, right):
    return lax.dot_general(left, right, (((1,), (0,)), ((), ())), preferred_element_type=F32)


def dot_nt(left, right):
    return lax.dot_general(left, right, (((1,), (1,)), ((), ())), preferred_element_type=F32)


def dot_tn(left, right):
    return lax.dot_general(left, right, (((0,), (0,)), ((), ())), preferred_element_type=F32)


def rms_split(values, gain):
    mean = jnp.mean(values * values, axis=(0, 2), keepdims=True)
    return values * lax.rsqrt(mean + EPSILON) * gain


def sum_heads(mine, other):
    arrived = lax.ppermute(other.astype(BF16), "core", SWAP)
    part = (mine + arrived.astype(F32)).astype(BF16)
    return part.astype(F32) + lax.ppermute(part, "tp", SWAP).astype(F32)


def shards(
    hidden_in,
    attn_gain,
    query_weight,
    key_weight,
    value_weight,
    conv_weight,
    beta_weight,
    out_gain,
    out_weight,
    ffn_gain,
    gate_weight,
    up_weight,
    down_weight,
    cotangent,
    segment_ids,
):
    count = lax.axis_size("shard")
    places = place_scalars()
    core, cx = places[0], places[1]
    micro, local, size, width = hidden_in.shape
    seqs = micro * local
    own_rows = seqs * size
    heads_tp = conv_weight.shape[2]
    heads = heads_tp // 2
    scale = LANES ** (-0.5)

    pieces = [
        pack_heads(places, query_weight, key_weight, value_weight, heads),
        own_block_turned(places, out_weight),
        own_block(places, gate_weight),
        own_block(places, up_weight),
        own_block_turned(places, down_weight),
    ]
    full = []
    for piece in pieces:
        own = lax.all_gather(piece, "shard", axis=0, tiled=True)
        full.append((own, lax.ppermute(own, "cx", SWAP)))
    joint, outer, gates, ups, downs = full

    small = jnp.concatenate(
        [
            attn_gain,
            ffn_gain,
            out_gain,
            conv_weight.reshape(-1),
            beta_weight.reshape(-1),
        ]
    )
    small = lax.all_gather(small, "shard", axis=0)
    piece_d = attn_gain.shape[0]
    entry = out_gain.shape[0]
    at = 2 * piece_d + entry
    gain_in = split_small(places, small[:, :piece_d].reshape(-1), count).astype(F32)
    gain_ffn = split_small(places, small[:, piece_d : 2 * piece_d].reshape(-1), count).astype(F32)
    gain_head = small[:, 2 * piece_d : at].reshape(1, LANES).astype(F32)
    conv_size = conv_weight.size
    taps = small[:, at : at + conv_size].reshape(count, 4, 3, heads_tp, entry)
    taps = taps.transpose(2, 3, 1, 0, 4).reshape(3, heads_tp, 4, LANES)
    taps = lax.dynamic_slice_in_dim(taps, core * heads, heads, axis=1).astype(F32)
    beta = small[:, at + conv_size :].reshape(width, heads_tp)
    beta = lax.dynamic_slice_in_dim(beta, core * heads, heads, axis=1)
    beta = jnp.pad(beta, ((0, 0), (0, LANES - heads)))
    beta = split_small(places, beta, count)
    gain_in, gain_ffn = gain_in[:, None, :], gain_ffn[:, None, :]

    hidden_own = hidden_in.reshape(own_rows, width)
    hidden_other = lax.ppermute(hidden_own, "core", SWAP)
    grad_own = cotangent.reshape(own_rows, width)
    grad_all = split_rows(
        places, jnp.concatenate([grad_own, lax.ppermute(grad_own, "core", SWAP)]), count
    )
    ids_own = segment_ids.reshape(seqs, size)
    ids_other = lax.ppermute(ids_own, "core", SWAP)
    late = jnp.where(core == 1, hidden_own, hidden_other).reshape(seqs, size, width)[:, size - HALO :]
    early_ids = jnp.where(core == 0, ids_own, ids_other)
    late_ids = jnp.where(core == 1, ids_own, ids_other)
    halo = lax.ppermute(late, "cx", [(0, 1)]).reshape(seqs * HALO, width)
    halo_ids = lax.ppermute(late_ids[:, size - HALO :], "cx", [(0, 1)])
    halo_ids = jnp.where(cx == 0, -1, halo_ids)
    ids = jnp.concatenate([halo_ids, early_ids, late_ids], axis=1)[..., None]
    id_rows = jnp.stack([early_ids, late_ids], axis=1)
    hidden_all = split_rows(
        places, jnp.concatenate([hidden_own, hidden_other, halo]), count
    )

    normed_low = rms_split(hidden_all.astype(F32), gain_in).astype(BF16)
    raw = (dot_nn(normed_low[0], joint[0]) + dot_nn(normed_low[1], joint[1])).astype(BF16)
    rates = sigmoid(dot_nn(normed_low[0], beta[0]) + dot_nn(normed_low[1], beta[1]))
    one, two, three, four = mixer_calls(
        places, raw, rates, ids, id_rows, taps, gain_head, heads, seqs, size, scale
    )
    query, key, value, inverse, final = one()
    incoming = lax.ppermute(final, "cx", [(0, 1)])
    head_low, mixed, fresh, middle = two(query, key, value, inverse, incoming)

    head_rows = head_low.reshape(2 * own_rows, heads * LANES)

    def out_rows(rows):
        return jnp.stack([dot_nt(rows, outer[0]), dot_nt(rows, outer[1])])

    hidden_f32 = hidden_all[:, :own_rows].astype(F32)
    resid = hidden_f32 + sum_heads(out_rows(head_rows[:own_rows]), out_rows(head_rows[own_rows:]))
    normed_ffn, ffn_pull = jax.vjp(rms_split, resid, gain_ffn)
    ffn_own = normed_ffn.astype(BF16)
    ffn_low = jnp.concatenate([ffn_own, lax.ppermute(ffn_own, "core", SWAP)], axis=1)

    gate = dot_nn(ffn_low[0], gates[0]) + dot_nn(ffn_low[1], gates[1])
    up = dot_nn(ffn_low[0], ups[0]) + dot_nn(ffn_low[1], ups[1])
    sig = jax.nn.sigmoid(gate)
    act = (gate * sig * up).astype(BF16)

    def reduced(rows, grads):
        across = lax.ppermute(dot_tn(rows[1], grads).astype(BF16), "cx", SWAP)
        total = (dot_tn(rows[0], grads) + across.astype(F32)).astype(BF16)
        return lax.psum_scatter(total, "shard", scatter_dimension=0, tiled=True)

    grad_down = reduced(grad_all, act)
    d_act = (dot_nn(grad_all[0], downs[0]) + dot_nn(grad_all[1], downs[1])).astype(BF16).astype(F32)
    d_gate = (d_act * up * sig * (1.0 + gate * (1.0 - sig))).astype(BF16)
    d_up = (d_act * gate * sig).astype(BF16)
    grad_gate = reduced(ffn_low, d_gate)
    grad_up = reduced(ffn_low, d_up)

    def ffn_back(rows):
        return jnp.stack(
            [dot_nt(d_gate[rows], gates[i]) + dot_nt(d_up[rows], ups[i]) for i in range(2)]
        )

    first_rows, other_rows = slice(0, own_rows), slice(own_rows, 2 * own_rows)
    d_ffn = sum_heads(ffn_back(first_rows), ffn_back(other_rows))
    d_resid, sum_ffn_gain = ffn_pull(d_ffn)
    d_resid = grad_all[:, :own_rows].astype(F32) + d_resid
    resid_own = d_resid.astype(BF16)
    resid_low = jnp.concatenate([resid_own, lax.ppermute(resid_own, "core", SWAP)], axis=1)

    def down_rows(rows):
        return jnp.stack([dot_nt(act[rows], downs[0]), dot_nt(act[rows], downs[1])])

    result = resid + sum_heads(down_rows(first_rows), down_rows(other_rows))
    result_rows = join_rows(places, result.astype(BF16), count)

    d_head = (dot_nn(resid_low[0], outer[0]) + dot_nn(resid_low[1], outer[1])).astype(BF16)
    grad_outer = reduced(resid_low, head_rows)
    d_low, d_incoming, d_gain = three(
        d_head.reshape(head_low.shape), mixed, query, key, inverse
    )
    d_final = lax.ppermute(d_incoming, "cx", [(1, 0)])
    d_raw, d_edge, d_rates, d_taps = four(
        query, key, value, inverse, fresh, d_low, incoming, middle, d_final
    )
    d_edge = lax.ppermute(d_edge, "cx", [(1, 0)])
    window = (1 - core, 0, size - HALO, 0)
    edge_rows = lax.dynamic_slice(d_raw, window, (1,) + d_edge.shape)
    d_raw = lax.dynamic_update_slice(
        d_raw, (edge_rows.astype(F32) + d_edge.astype(F32)[None]).astype(BF16), window
    ).reshape(2 * own_rows, -1)
    d_logit = jnp.where(core == 0, d_rates, d_rates[:, ::-1]).transpose(1, 0, 2, 3)
    d_logit = d_logit.reshape(2 * own_rows, LANES).astype(BF16)
    normed_rows = normed_low[:, : 2 * own_rows]
    grad_joint = reduced(normed_rows, d_raw)
    sum_rate = jnp.stack([dot_tn(normed_rows[i], d_logit)[:, :heads] for i in range(2)])

    def normed_back(rows):
        return jnp.stack(
            [dot_nt(d_raw[rows], joint[i]) + dot_nt(d_logit[rows], beta[i]) for i in range(2)]
        )

    d_normed = sum_heads(normed_back(first_rows), normed_back(other_rows))
    _, norm_pull = jax.vjp(rms_split, hidden_f32, gain_in)
    d_hidden, sum_attn_gain = norm_pull(d_normed)
    input_rows = join_rows(places, (d_resid + d_hidden).astype(BF16), count)

    sum_taps = jnp.sum(d_taps, axis=0).transpose(2, 0, 1, 3)
    sum_taps = lax.dynamic_update_slice_in_dim(
        jnp.zeros((4, 3, heads_tp, LANES), F32), sum_taps, core * heads, axis=2
    )
    sum_rate = join_small(places, sum_rate, count)
    sum_rate = lax.dynamic_update_slice_in_dim(
        jnp.zeros((width, heads_tp), F32), sum_rate, core * heads, axis=1
    )
    sum_head_gain = jnp.sum(d_gain[:, :, 0, :], axis=(0, 1))
    sum_head_gain = lax.psum(sum_head_gain.astype(BF16), "tp").astype(F32)
    own = lax.axis_index("shard")
    packed = jnp.concatenate(
        [
            join_small(places, sum_attn_gain[:, 0], count),
            join_small(places, sum_ffn_gain[:, 0], count),
            sum_head_gain,
            sum_taps.reshape(-1),
            sum_rate.reshape(-1),
        ]
    ).astype(BF16)
    packed = lax.psum(packed, ("shard", "cx", "core")).astype(F32)
    ends = [width, 2 * width, 2 * width + LANES, 2 * width + LANES + sum_taps.size]
    grad_attn_gain = lax.dynamic_slice_in_dim(packed[: ends[0]], own * piece_d, piece_d)
    grad_ffn_gain = lax.dynamic_slice_in_dim(packed[ends[0] : ends[1]], own * piece_d, piece_d)
    grad_out_gain = lax.dynamic_slice_in_dim(packed[ends[1] : ends[2]], own * entry, entry)
    grad_conv = lax.dynamic_slice_in_dim(
        packed[ends[2] : ends[3]].reshape(4, 3, heads_tp, LANES), own * entry, entry, axis=3
    )
    grad_beta = lax.dynamic_slice_in_dim(
        packed[ends[3] :].reshape(width, heads_tp), own * piece_d, piece_d, axis=0
    )

    grad_query, grad_key, grad_value = lay_heads(places, pieces_of(grad_joint), heads)
    return (
        result_rows.reshape(hidden_in.shape),
        input_rows.reshape(hidden_in.shape),
        grad_attn_gain,
        grad_query,
        grad_key,
        grad_value,
        grad_conv,
        grad_beta,
        grad_out_gain,
        lay_block_turned(places, pieces_of(grad_outer)),
        grad_ffn_gain,
        lay_block(places, pieces_of(grad_gate)),
        lay_block(places, pieces_of(grad_up)),
        lay_block_turned(places, pieces_of(grad_down)),
    )


def solution(mesh):
    shard, ctx, tp = (mesh.shape[name] for name in ("shard", "ctx", "tp"))
    cores = Mesh(
        mesh.devices.reshape(shard, ctx // 2, 2, tp), ("shard", "cx", "core", "tp")
    )
    tokens = P(None, "shard", ("cx", "core"), None)
    outer = P("shard", "tp")
    turned = P("tp", "shard")
    conv = P(None, None, "tp", "shard")
    split = P("shard")
    return jax.shard_map(
        shards,
        mesh=cores,
        in_specs=(
            tokens,
            split,
            outer,
            outer,
            outer,
            conv,
            outer,
            split,
            turned,
            split,
            outer,
            outer,
            turned,
            tokens,
            P(None, "shard", ("cx", "core")),
        ),
        out_specs=(
            tokens,
            tokens,
            split,
            outer,
            outer,
            outer,
            conv,
            outer,
            split,
            turned,
            split,
            outer,
            outer,
            turned,
        ),
        check_vma=False,
    )
```

```python
import functools

import jax
import jax.numpy as jnp
from jax import lax
from jax.experimental import pallas as pl
from jax.experimental.pallas import tpu as pltpu
from jax.sharding import Mesh
from jax.sharding import PartitionSpec as P

EPSILON = 1e-06
F32 = jnp.float32
BF16 = jnp.bfloat16
LANES = 128
HALO = 16
SWAP = [(0, 1), (1, 0)]


def mm(left, right, left_dim, right_dim):
    return lax.dot_general(
        left.astype(BF16),
        right.astype(BF16),
        (((left_dim,), (right_dim,)), ((), ())),
        preferred_element_type=F32,
    )


def nn(left, right):
    return mm(left, right, 1, 0)


def nt(left, right):
    return mm(left, right, 1, 1)


def tn(left, right):
    return mm(left, right, 0, 0)


def place_scalars():
    return jnp.stack([lax.axis_index("core"), lax.axis_index("cx")]).astype(jnp.int32)


def call(kernel, grid, in_specs, out_specs, out_shape, scratch=(), aliases=None):
    return pl.pallas_call(
        kernel,
        grid_spec=pltpu.PrefetchScalarGridSpec(
            num_scalar_prefetch=1,
            grid=grid,
            in_specs=in_specs,
            out_specs=out_specs,
            scratch_shapes=list(scratch),
        ),
        out_shape=out_shape,
        input_output_aliases=aliases or {},
        compiler_params=pltpu.CompilerParams(
            dimension_semantics=("arbitrary",) * len(grid), vmem_limit_bytes=48 << 20
        ),
        cost_estimate=pl.CostEstimate(
            flops=1000, transcendentals=0, bytes_accessed=1000
        ),
    )


def split_rows(places, values, count):
    rows, width = values.shape
    half = width // (2 * count)
    if half % LANES:
        cut = values.reshape(rows, count, 2, half)
        cut = jnp.where(places[1] == 0, cut, cut[:, :, ::-1])
        return [cut[:, :, side].reshape(rows, width // 2) for side in range(2)]
    tile = max(t for t in range(16, 400, 16) if rows % t == 0)

    def kernel(where, source, *targets):
        for side in range(2):
            for shard in range(count):
                at = shard * 2 * half + (where[1] if side == 0 else 1 - where[1]) * half
                targets[side][:, shard * half : (shard + 1) * half] = source[
                    :, pl.ds(pl.multiple_of(at, LANES), half)
                ]

    return call(
        kernel,
        (rows // tile,),
        [pl.BlockSpec((tile, width), lambda i, w: (i, 0))],
        [pl.BlockSpec((tile, width // 2), lambda i, w: (i, 0))] * 2,
        [jax.ShapeDtypeStruct((rows, width // 2), values.dtype)] * 2,
    )(places, values)


def join_rows(places, values, count):
    rows, width = values[0].shape[0], 2 * values[0].shape[1]
    half = width // (2 * count)
    if half % LANES:
        cut = jnp.stack([part.reshape(rows, count, half) for part in values], axis=2)
        cut = jnp.where(places[1] == 0, cut, cut[:, :, ::-1])
        return cut.reshape(rows, width)
    tile = max(t for t in range(16, 400, 16) if rows % t == 0)

    def kernel(where, own, other, target):
        for side, source in enumerate((own, other)):
            for shard in range(count):
                at = shard * 2 * half + (where[1] if side == 0 else 1 - where[1]) * half
                target[:, pl.ds(pl.multiple_of(at, LANES), half)] = source[
                    :, shard * half : (shard + 1) * half
                ]

    return call(
        kernel,
        (rows // tile,),
        [pl.BlockSpec((tile, width // 2), lambda i, w: (i, 0))] * 2,
        pl.BlockSpec((tile, width), lambda i, w: (i, 0)),
        jax.ShapeDtypeStruct((rows, width), values[0].dtype),
    )(places, *values)


def split_small(places, values, count):
    cut = values.reshape((count, 2, values.shape[0] // (2 * count)) + values.shape[1:])
    cut = jnp.where(places[1] == 0, cut, cut[:, ::-1])
    cut = jnp.swapaxes(cut, 0, 1)
    return cut.reshape((2, values.shape[0] // 2) + values.shape[1:])


def join_small(places, values, count):
    cut = values.reshape((2, count, values.shape[1] // count) + values.shape[2:])
    cut = jnp.swapaxes(cut, 0, 1)
    cut = jnp.where(places[1] == 0, cut, cut[:, ::-1])
    return cut.reshape((2 * values.shape[1],) + values.shape[2:])


def pack_heads(places, query, key, value, heads, pair):
    half = query.shape[0] // 2

    def kernel(where, query_ref, key_ref, value_ref, out):
        out[:, :LANES] = query_ref[...]
        out[:, LANES : 2 * LANES] = key_ref[...]
        out[:, 2 * LANES :] = value_ref[...]

    spec = pl.BlockSpec((half, LANES), lambda h, w: (w[1], w[0] * heads + 2 * pair + h))
    return call(
        kernel,
        (2,),
        [spec] * 3,
        pl.BlockSpec((half, 3 * LANES), lambda h, w: (0, h)),
        jax.ShapeDtypeStruct((half, 6 * LANES), query.dtype),
    )(places, query, key, value)


def own_block(places, weight):
    half, columns = weight.shape[0] // 2, weight.shape[1] // 2
    return lax.dynamic_slice(weight, (places[1] * half, places[0] * columns), (half, columns))


def own_block_turned(places, weight):
    rows, half = weight.shape[0] // 2, weight.shape[1] // 2
    return lax.dynamic_slice(weight, (places[0] * rows, places[1] * half), (rows, half)).T


def pieces_of(own):
    across = lax.ppermute(own, "cx", SWAP)
    return [own, across, lax.ppermute(own, "core", SWAP), lax.ppermute(across, "core", SWAP)]


def pick(where, core, cx, refs, store):
    which = 2 * jnp.bitwise_xor(where[0], core) + jnp.bitwise_xor(where[1], cx)
    for index in range(4):

        @pl.when(which == index)
        def _():
            store(refs[index][...].astype(F32))


def lay_heads(places, pairs):
    half = pairs[0][0].shape[0]
    heads = 2 * len(pairs)
    width = heads * LANES

    def kernel(where, *refs):
        outs = refs[-3:]
        for pair in range(len(pairs)):

            def store(values):
                for inner in range(2):
                    head = 2 * pair + inner
                    for index in range(3):
                        at = (inner * 3 + index) * LANES
                        outs[index][:, head * LANES : (head + 1) * LANES] = values[
                            :, at : at + LANES
                        ]

            pick(
                where, pl.program_id(1), pl.program_id(0), refs[4 * pair : 4 * pair + 4], store
            )

    return call(
        kernel,
        (2, 2),
        [pl.BlockSpec(pairs[0][0].shape, lambda i, j, w: (0, 0))] * (4 * len(pairs)),
        [pl.BlockSpec((half, width), lambda i, j, w: (i, j))] * 3,
        [jax.ShapeDtypeStruct((2 * half, 2 * width), F32)] * 3,
    )(places, *(piece for pair in pairs for piece in pair))


def lay_block(places, pieces):
    half, columns = pieces[0].shape

    def kernel(where, a, b, c, d, out):
        def store(values):
            out[...] = values

        pick(where, pl.program_id(1), pl.program_id(0), (a, b, c, d), store)

    return call(
        kernel,
        (2, 2),
        [pl.BlockSpec((half, columns), lambda i, j, w: (0, 0))] * 4,
        pl.BlockSpec((half, columns), lambda i, j, w: (i, j)),
        jax.ShapeDtypeStruct((2 * half, 2 * columns), F32),
    )(places, *pieces)


def lay_block_turned(places, pieces):
    half, rows = pieces[0].shape

    def kernel(where, a, b, c, d, out):
        for side in range(2):

            def store(values):
                out[:, side * half : (side + 1) * half] = values.T

            pick(where, pl.program_id(0), side, (a, b, c, d), store)

    return call(
        kernel,
        (2,),
        [pl.BlockSpec((half, rows), lambda i, w: (0, 0))] * 4,
        pl.BlockSpec((rows, 2 * half), lambda i, w: (i, 0)),
        jax.ShapeDtypeStruct((2 * rows, 2 * half), F32),
    )(places, *pieces)


def fill_ext(ext, index, halo, first, second, size):
    ext[index, :HALO, :] = halo[...].astype(F32)
    ext[index, HALO : HALO + size, :] = first[...].astype(F32)
    ext[index, HALO + size :, :] = second[...].astype(F32)


def links_of(ids, total):
    own = ids[0, HALO : HALO + total, :]
    return [
        (ids[0, HALO - 3 + tap : HALO - 3 + tap + total, :] == own).astype(F32) for tap in range(4)
    ]


def conv_of(ext, index, taps, links, total):
    result = None
    for tap in range(4):
        term = (
            taps[index, 0, tap : tap + 1, :]
            * ext[index, HALO - 3 + tap : HALO - 3 + tap + total, :]
            * links[tap]
        )
        result = term if result is None else result + term
    return result


def sigmoid(values):
    return 1.0 / (1.0 + jnp.exp(-values))


def column_of(values, head):
    lane = lax.broadcasted_iota(jnp.int32, values.shape, 1)
    return jnp.sum(jnp.where(lane == head, values, 0.0), axis=1, keepdims=True)


def marks(ids, rows, chunk, size):
    start = HALO + chunk * size
    column = ids[0, start : start + size, :]
    before = ids[0, start - 1 : start, :]
    last = ids[0, start + size - 1 : start + size, :]
    first = (column == before).astype(F32)
    tail = (column == last).astype(F32)
    whole = (last == before).astype(F32)
    same = column == rows[0, chunk : chunk + 1, :]
    row = lax.broadcasted_iota(jnp.int32, (size, size), 0)
    col = lax.broadcasted_iota(jnp.int32, (size, size), 1)
    return first, tail, whole, same & (row > col), same & (row >= col)


def inverse_units(stricts, size):
    row = lax.broadcasted_iota(jnp.int32, (size, size), 0)
    col = lax.broadcasted_iota(jnp.int32, (size, size), 1)
    mixed = jnp.bitwise_xor(row, col)
    results = [
        jnp.where(row == col, 1.0, jnp.where(mixed == 1, -strict, 0.0)) for strict in stricts
    ]
    stricts = [strict.astype(BF16) for strict in stricts]
    block = 2
    while block < size:
        pair = (mixed >= block) & (mixed < 2 * block)
        lows = [result.astype(BF16) for result in results]
        parts = [jnp.where(pair, strict, 0.0) for strict in stricts]
        steps = [nn(part, low).astype(BF16) for part, low in zip(parts, lows)]
        results = [
            result - nn(low, step) for result, low, step in zip(results, lows, steps)
        ]
        block *= 2
    return [result.astype(BF16) for result in results]


def forward_one(where, q0, k0, v0, q1, k1, v1, qh, kh, vh, taps, ids, rows, r0, r1, *rest, size, base):
    query, key, value, inverse, final, ext = rest
    head = base + pl.program_id(1)
    total = 2 * size
    for index, group in enumerate(((qh, q0, q1), (kh, k0, k1), (vh, v0, v1))):
        fill_ext(ext, index, *group, size)
    links = links_of(ids, total)
    out = []
    for index in range(3):
        conv = conv_of(ext, index, taps, links, total)
        act = conv * sigmoid(conv)
        if index < 2:
            act = act * lax.rsqrt(jnp.sum(act * act, axis=1, keepdims=True) + EPSILON)
        out.append(act.astype(BF16))
    for target, values in zip((query, key, value), out):
        target[0, 0] = values[:size]
        target[0, 1] = values[size:]
    chunks = []
    for chunk, rates in enumerate((r0, r1)):
        first, tail, whole, strict, _ = marks(ids, rows, chunk, size)
        rate = column_of(rates[...], head)
        keys = out[1][chunk * size : (chunk + 1) * size]
        chunks.append((first, tail, whole, rate, keys, jnp.where(strict, rate * nt(keys, keys), 0.0)))
    inverses = inverse_units([item[-1] for item in chunks], size)
    state = None
    for chunk, (first, tail, whole, rate, keys, _) in enumerate(chunks):
        fresh = out[2][chunk * size : (chunk + 1) * size].astype(F32)
        inverse[0, 0, chunk] = inverses[chunk]
        if chunk:
            fresh = fresh - first * nt(keys, state)
        fresh = nn(inverses[chunk], rate * fresh)
        added = tn(tail * fresh, keys)
        state = added if state is None else whole * state + added
    final[0, 0] = state.astype(BF16)


def forward_two(where, query, key, value, inverse, ids, rows, r0, r1, incoming, gain, *rest, size, scale, base):
    head_low, mixed_out, fresh_out, middle = rest[-4:]
    head = base + pl.program_id(1)
    state = incoming[0, 0].astype(F32)
    for chunk, rates in enumerate((r0, r1)):
        first, tail, whole, _, lower = marks(ids, rows, chunk, size)
        rate = column_of(rates[...], head)
        keys, queries = key[0, chunk], query[0, chunk]
        if chunk:
            middle[0, 0] = state.astype(BF16)
        rest_rows = value[0, chunk].astype(F32) - first * nt(keys, state)
        fresh = nn(inverse[0, 0, chunk], rate * rest_rows)
        fresh_out[0, chunk] = fresh.astype(BF16)
        inner = jnp.where(lower, nt(queries, keys), 0.0)
        mixed = scale * (first * nt(queries, state) + nn(inner, fresh))
        mixed_out[0, chunk] = mixed
        normed = mixed * lax.rsqrt(jnp.mean(mixed * mixed, axis=1, keepdims=True) + EPSILON)
        slot = where[0] if chunk == 0 else 1 - where[0]
        head_low[slot, 0] = (normed * gain[...]).astype(BF16)
        if chunk == 0:
            state = whole * state + tn(tail * fresh, keys)


def backward_one(where, d_head, mixed, query, key, inverse, ids, rows, r0, r1, gain, *rest, size, scale, base):
    d_out, d_state_out, d_gain = rest
    head = base + pl.program_id(1)
    total = jnp.zeros((1, LANES), F32)
    d_state = None
    for chunk in (1, 0):
        first, tail, whole, _, lower = marks(ids, rows, chunk, size)
        rate = column_of((r0, r1)[chunk][...], head)
        keys, queries = key[0, chunk], query[0, chunk]
        slot = where[0] if chunk == 0 else 1 - where[0]
        grad = d_head[slot, 0].astype(F32)
        values = mixed[0, chunk]
        inv_rms = lax.rsqrt(jnp.mean(values * values, axis=1, keepdims=True) + EPSILON)
        normed = values * inv_rms
        total = total + jnp.sum(grad * normed, axis=0, keepdims=True)
        scaled = grad * gain[...]
        d_mixed = inv_rms * (scaled - normed * jnp.mean(scaled * normed, axis=1, keepdims=True))
        d_low = (scale * d_mixed).astype(BF16)
        d_out[0, chunk] = d_low
        inner = jnp.where(lower, nt(queries, keys), 0.0)
        d_fresh = tn(inner, d_low)
        if d_state is not None:
            d_fresh = d_fresh + tail * nt(keys, d_state)
        d_rest = rate * tn(inverse[0, 0, chunk], d_fresh)
        change = tn(first * d_low.astype(F32), queries) - tn(first * d_rest, keys)
        d_state = change if d_state is None else whole * d_state + change
    d_state_out[0, 0] = d_state.astype(BF16)
    d_gain[0, 0] = jnp.broadcast_to(total, (8, LANES))


def backward_two(where, q0, k0, v0, q1, k1, v1, qh, kh, vh, taps, ids, rows, r0, r1, *rest, size, base):
    query, key, value, inverse, fresh_in, d_in, incoming, middle, d_final = rest[:9]
    d_raw, d_edge, d_rates, d_taps = rest[9:13]
    ext, d_ext, d_rows = rest[13:]
    head = base + pl.program_id(1)
    total = 2 * size
    for index, group in enumerate(((qh, q0, q1), (kh, k0, k1), (vh, v0, v1))):
        fill_ext(ext, index, *group, size)
    d_state = d_final[0, 0].astype(F32)

    @pl.when(pl.program_id(1) == 0)
    def _():
        d_rates[...] = jnp.zeros_like(d_rates)

    for chunk in (1, 0):
        first, tail, whole, strict, lower = marks(ids, rows, chunk, size)
        rate = column_of((r0, r1)[chunk][...], head)
        keys, queries, fresh = key[0, chunk], query[0, chunk], fresh_in[0, chunk]
        inv, d_low = inverse[0, 0, chunk], d_in[0, chunk]
        state = (middle if chunk else incoming)[0, 0]
        d_mix = d_low.astype(F32)
        inner = jnp.where(lower, nt(queries, keys), 0.0)
        gram = jnp.where(strict, nt(keys, keys), 0.0)
        d_fresh = tn(inner, d_low) + tail * nt(keys, d_state)
        turned = tn(inv, d_fresh)
        d_rest = rate * turned
        rest_rows = value[0, chunk].astype(F32) - first * nt(keys, state)
        error = rest_rows - nn(gram, fresh)
        d_rate = jnp.sum(turned * error, axis=1, keepdims=True) * rate * (1.0 - rate)
        d_inner = jnp.where(lower, nt(d_low, fresh), 0.0)
        d_gram = rate * jnp.where(strict, -nt(turned, fresh), 0.0)
        d_query = first * nn(d_low, state) + nn(d_inner, keys)
        d_key = (
            tn(d_inner, queries)
            + tail * nn(fresh, d_state)
            - nn(first * d_rest, state)
            + nn(d_gram, keys)
            + tn(d_gram, keys)
        )
        for index, values in enumerate((d_query, d_key, d_rest)):
            d_rows[index, chunk * size : (chunk + 1) * size, :] = values
        lane = lax.broadcasted_iota(jnp.int32, (size, LANES), 1)
        d_rates[0, chunk] = d_rates[0, chunk] + jnp.where(lane == head, d_rate, 0.0)
        if chunk:
            d_state = (
                whole * d_state + tn(first * d_mix, queries) - tn(first * d_rest, keys)
            )
    links = links_of(ids, total)
    for index in range(3):
        conv = conv_of(ext, index, taps, links, total)
        sig = sigmoid(conv)
        d_act = d_rows[index].astype(BF16).astype(F32)
        if index < 2:
            act = conv * sig
            inv_norm = lax.rsqrt(jnp.sum(act * act, axis=1, keepdims=True) + EPSILON)
            unit = act * inv_norm
            d_act = (d_act - unit * jnp.sum(unit * d_act, axis=1, keepdims=True)) * inv_norm
        d_conv = d_act * sig * (1.0 + conv * (1.0 - sig))
        d_ext[...] = jnp.zeros_like(d_ext)
        for tap in range(4):
            window = slice(HALO - 3 + tap, HALO - 3 + tap + total)
            linked = d_conv * links[tap]
            d_taps[0, index, 0, tap : tap + 1, :] = jnp.sum(
                linked * ext[index, window, :], axis=0, keepdims=True
            )
            d_ext[window, :] = d_ext[window, :] + taps[index, 0, tap : tap + 1, :] * linked
        lanes = slice(index * LANES, (index + 1) * LANES)
        d_edge[0, :, lanes] = d_ext[:HALO, :].astype(BF16)
        d_raw[where[0], 0, :, lanes] = d_ext[HALO : HALO + size, :].astype(BF16)
        d_raw[1 - where[0], 0, :, lanes] = d_ext[HALO + size :, :].astype(BF16)


def mixer_calls(places, pair, raw, rates, ids, rows, taps, gain, heads, seqs, size, scale):
    base = 2 * pair

    def slot_of(chunk, w):
        return w[0] if chunk == 0 else 1 - w[0]

    def raw_spec(chunk, part):
        return pl.BlockSpec(
            (size, LANES), lambda b, h, w: (slot_of(chunk, w) * seqs + b, 3 * h + part)
        )

    def rate_spec(chunk):
        return pl.BlockSpec((size, LANES), lambda b, h, w: (slot_of(chunk, w) * seqs + b, 0))

    halo_base = 2 * seqs * size // HALO

    def halo_spec(part):
        return pl.BlockSpec((HALO, LANES), lambda b, h, w: (halo_base + b, 3 * h + part))

    conv_specs = (
        [raw_spec(c, p) for c in range(2) for p in range(3)]
        + [halo_spec(p) for p in range(3)]
        + [
            pl.BlockSpec((3, 1, 4, LANES), lambda b, h, w: (0, base + h, 0, 0)),
            pl.BlockSpec((1, HALO + 2 * size, 1), lambda b, h, w: (b, 0, 0)),
            pl.BlockSpec((1, 2, size), lambda b, h, w: (b, 0, 0)),
            rate_spec(0),
            rate_spec(1),
        ]
    )
    conv_args = (raw,) * 9 + (taps, ids, rows, rates, rates)
    id_specs, id_args = conv_specs[10:], conv_args[10:]
    act_spec = pl.BlockSpec((1, 2, size, LANES), lambda b, h, w: (b, 0, 0, h))
    act_shape = (seqs, 2, size, 2 * LANES)
    state_spec = pl.BlockSpec((1, 1, LANES, LANES), lambda b, h, w: (b, h, 0, 0))
    state_shape = jax.ShapeDtypeStruct((seqs, 2, LANES, LANES), BF16)
    inv_spec = pl.BlockSpec((1, 1, 2, size, size), lambda b, h, w: (b, h, 0, 0, 0))
    inv_shape = jax.ShapeDtypeStruct((seqs, 2, 2, size, size), BF16)
    slot_spec = pl.BlockSpec((2, 1, size, LANES), lambda b, h, w: (0, b, 0, base + h))
    slot_shape = jax.ShapeDtypeStruct((2, seqs, size, heads * LANES), BF16)
    gain_spec = pl.BlockSpec((1, LANES), lambda b, h, w: (0, 0))
    low = jax.ShapeDtypeStruct(act_shape, BF16)
    grid = (seqs, 2)

    def one():
        return call(
            functools.partial(forward_one, size=size, base=base),
            grid,
            conv_specs,
            [act_spec] * 3 + [inv_spec, state_spec],
            [low] * 3 + [inv_shape, state_shape],
            [pltpu.VMEM((3, HALO + 2 * size, LANES), F32)],
        )(places, *conv_args)

    def two(query, key, value, inverse, incoming, before=()):
        args = (query, key, value, inverse, *id_args, incoming, gain)
        return call(
            functools.partial(forward_two, size=size, scale=scale, base=base),
            grid,
            [act_spec] * 3
            + [inv_spec]
            + id_specs
            + [state_spec, gain_spec]
            + [pl.BlockSpec(memory_space=pl.ANY)] * len(before),
            [slot_spec, act_spec, act_spec, state_spec],
            [slot_shape, jax.ShapeDtypeStruct(act_shape, F32), low, state_shape],
            aliases={1 + len(args): 0} if before else None,
        )(places, *args, *before)

    def three(d_head, mixed, query, key, inverse):
        return call(
            functools.partial(backward_one, size=size, scale=scale, base=base),
            grid,
            [slot_spec, act_spec, act_spec, act_spec, inv_spec] + id_specs + [gain_spec],
            [act_spec, state_spec, pl.BlockSpec((1, 1, 8, LANES), lambda b, h, w: (b, h, 0, 0))],
            [low, state_shape, jax.ShapeDtypeStruct((seqs, 2, 8, LANES), F32)],
        )(places, d_head, mixed, query, key, inverse, *id_args, gain)

    def four(query, key, value, inverse, fresh, d_low, incoming, middle, d_final):
        return call(
            functools.partial(backward_two, size=size, base=base),
            grid,
            conv_specs + [act_spec] * 3 + [inv_spec, act_spec, act_spec] + [state_spec] * 3,
            [
                pl.BlockSpec((2, 1, size, 3 * LANES), lambda b, h, w: (0, b, 0, h)),
                pl.BlockSpec((1, HALO, 3 * LANES), lambda b, h, w: (b, 0, h)),
                pl.BlockSpec((1, 2, size, LANES), lambda b, h, w: (b, 0, 0, 0)),
                pl.BlockSpec((1, 3, 1, 4, LANES), lambda b, h, w: (b, 0, h, 0, 0)),
            ],
            [
                jax.ShapeDtypeStruct((2, seqs, size, 6 * LANES), BF16),
                jax.ShapeDtypeStruct((seqs, HALO, 6 * LANES), BF16),
                jax.ShapeDtypeStruct((seqs, 2, size, LANES), F32),
                jax.ShapeDtypeStruct((seqs, 3, 2, 4, LANES), F32),
            ],
            [
                pltpu.VMEM((3, HALO + 2 * size, LANES), F32),
                pltpu.VMEM((HALO + 2 * size, LANES), F32),
                pltpu.VMEM((3, 2 * size, LANES), F32),
            ],
        )(
            places,
            *conv_args,
            query,
            key,
            value,
            inverse,
            fresh,
            d_low,
            incoming,
            middle,
            d_final,
        )

    return one, two, three, four


def dot_nn(left, right):
    return lax.dot_general(left, right, (((1,), (0,)), ((), ())), preferred_element_type=F32)


def dot_nt(left, right):
    return lax.dot_general(left, right, (((1,), (1,)), ((), ())), preferred_element_type=F32)


def dot_tn(left, right):
    return lax.dot_general(left, right, (((0,), (0,)), ((), ())), preferred_element_type=F32)


def rms_split(values, gain):
    total = sum(jnp.sum(part * part, axis=1, keepdims=True) for part in values)
    factor = lax.rsqrt(total / (2 * values[0].shape[1]) + EPSILON)
    return [part * factor * own for part, own in zip(values, gain)]


def tie(value, *after):
    return lax.optimization_barrier((value, after))[0]


class Steps:
    def __init__(self):
        self.last = ()

    def wait(self, *values):
        self.last = (self.last, values)

    def __call__(self, fn, *args):
        traced, static = [], []
        for arg in args:
            leaves = jax.tree.leaves(arg)
            static.append(not leaves or not all(hasattr(leaf, "dtype") for leaf in leaves))
            if not static[-1]:
                traced.append(arg)
        traced = iter(tie(tuple(traced), self.last))
        result = fn(*(arg if fixed else next(traced) for arg, fixed in zip(args, static)))
        self.last = result
        return result


def across_cores(values):
    return [jnp.concatenate([part, lax.ppermute(part, "core", SWAP)]) for part in values]


def sum_cores(mine, other):
    arrived = [lax.ppermute(away.astype(BF16), "core", SWAP) for away in other]
    return [(own + more.astype(F32)).astype(BF16) for own, more in zip(mine, arrived)]


def sum_heads(mine, other):
    return [(part, lax.ppermute(part, "tp", SWAP)) for part in sum_cores(mine, other)]


def sum_over(values, axis, hop):
    partners = [(index, index ^ hop) for index in range(lax.axis_size(axis))]
    return (values.astype(F32) + lax.ppermute(values, axis, partners).astype(F32)).astype(BF16)


def add_pairs(pairs, values):
    return [base + (a.astype(F32) + b.astype(F32)) for (a, b), base in zip(pairs, values)]


def dots(dot, left, right):
    return dot(left[0], right[0]) + dot(left[1], right[1])


def shards(
    hidden_in,
    attn_gain,
    query_weight,
    key_weight,
    value_weight,
    conv_weight,
    beta_weight,
    out_gain,
    out_weight,
    ffn_gain,
    gate_weight,
    up_weight,
    down_weight,
    cotangent,
    segment_ids,
):
    count = lax.axis_size("shard")
    places = place_scalars()
    core, cx = places[0], places[1]
    micro, local, size, width = hidden_in.shape
    seqs = micro * local
    own_rows = seqs * size
    heads_tp = conv_weight.shape[2]
    heads = heads_tp // 2
    scale = LANES ** (-0.5)

    first_rows, other_rows = slice(0, own_rows), slice(own_rows, 2 * own_rows)

    small = jnp.concatenate(
        [
            attn_gain,
            ffn_gain,
            out_gain,
            conv_weight.reshape(-1),
            beta_weight.reshape(-1),
        ]
    )
    unpadded = small.size
    small = jnp.pad(small, (0, -unpadded % (16 * LANES))).reshape(-1, LANES)
    small = lax.all_gather(small, "shard", axis=0).reshape(count, -1)
    piece_d = attn_gain.shape[0]
    entry = out_gain.shape[0]
    at = 2 * piece_d + entry
    gain_in = split_small(places, small[:, :piece_d].reshape(-1), count).astype(F32)
    gain_ffn = split_small(places, small[:, piece_d : 2 * piece_d].reshape(-1), count).astype(F32)
    gain_head = small[:, 2 * piece_d : at].reshape(1, LANES).astype(F32)
    conv_size = conv_weight.size
    taps = small[:, at : at + conv_size].reshape(count, 4, 3, heads_tp, entry)
    taps = taps.transpose(2, 3, 1, 0, 4).reshape(3, heads_tp, 4, LANES)
    taps = lax.dynamic_slice_in_dim(taps, core * heads, heads, axis=1).astype(F32)
    beta = small[:, at + conv_size : unpadded].reshape(width, heads_tp)
    beta = lax.dynamic_slice_in_dim(beta, core * heads, heads, axis=1)
    beta = jnp.pad(beta, ((0, 0), (0, LANES - heads)))
    beta = split_small(places, beta, count)
    gain_in = [gain_in[side : side + 1] for side in range(2)]
    gain_ffn = [gain_ffn[side : side + 1] for side in range(2)]

    hidden_own = hidden_in.reshape(own_rows, width)
    hidden_other = lax.ppermute(hidden_own, "core", SWAP)
    grad_own = cotangent.reshape(own_rows, width)
    grad_all = split_rows(
        places, jnp.concatenate([grad_own, lax.ppermute(grad_own, "core", SWAP)]), count
    )
    ids_own = segment_ids.reshape(seqs, size)
    ids_other = lax.ppermute(ids_own, "core", SWAP)
    late = jnp.where(core == 1, hidden_own, hidden_other).reshape(seqs, size, width)[:, size - HALO :]
    early_ids = jnp.where(core == 0, ids_own, ids_other)
    late_ids = jnp.where(core == 1, ids_own, ids_other)
    halo = lax.ppermute(late, "cx", [(0, 1)]).reshape(seqs * HALO, width)
    halo_ids = lax.ppermute(late_ids[:, size - HALO :], "cx", [(0, 1)])
    halo_ids = jnp.where(cx == 0, -1, halo_ids)
    ids = jnp.concatenate([halo_ids, early_ids, late_ids], axis=1)[..., None]
    id_rows = jnp.stack([early_ids, late_ids], axis=1)
    hidden_all = split_rows(places, jnp.concatenate([hidden_own, hidden_other, halo]), count)

    hidden_wide = [part.astype(F32) for part in hidden_all]
    normed_low = [part.astype(BF16) for part in rms_split(hidden_wide, gain_in)]
    rates = sigmoid(dots(dot_nn, normed_low, beta))

    def gathered(piece):
        return lax.all_gather(piece, "shard", axis=0, tiled=True)

    def with_other(own, *after):
        return [own, lax.ppermute(tie(own, *after), "cx", SWAP)]

    pairs = range(heads // 2)
    weights = (query_weight, key_weight, value_weight)
    packs = [pack_heads(places, *weights, heads, pair) for pair in pairs]
    joint = []
    for piece in packs:
        joint.append(with_other(gathered(piece), *(part[1] for part in joint)))
    outer_own = gathered(tie(own_block_turned(places, out_weight), packs[-1]))
    gates_own = gathered(tie(own_block(places, gate_weight), hidden_all))
    ups_own = gathered(tie(own_block(places, up_weight), normed_low, rates))
    downs_own = gathered(tie(own_block_turned(places, down_weight), grad_all, joint[0][1]))
    outer = with_other(outer_own, joint[-1][1])

    raws = [dots(dot_nn, normed_low, part).astype(BF16) for part in joint]
    calls = [
        mixer_calls(
            places, pair, raws[pair], rates, ids, id_rows, taps, gain_head, heads, seqs, size, scale
        )
        for pair in pairs
    ]
    firsts = [one() for one, *_ in calls]
    incomings = [lax.ppermute(first[-1], "cx", [(0, 1)]) for first in firsts]
    seconds = []
    for pair in pairs:
        before = (seconds[-1][0],) if seconds else ()
        seconds.append(calls[pair][1](*firsts[pair][:4], incomings[pair], before))
    head_low = seconds[-1][0]

    head_rows = head_low.reshape(2 * own_rows, heads * LANES)

    def out_rows(rows):
        return [dot_nt(rows, part) for part in outer]

    hidden_f32 = [part[:own_rows].astype(F32) for part in hidden_all]
    mixer_pairs = sum_heads(out_rows(head_rows[:own_rows]), out_rows(head_rows[own_rows:]))
    gates = with_other(gates_own, outer[1], [pair[0] for pair in mixer_pairs])
    ups = with_other(ups_own, gates[1])
    downs = with_other(downs_own, ups[1])
    resid = add_pairs(mixer_pairs, hidden_f32)
    normed_ffn, ffn_pull = jax.vjp(rms_split, resid, gain_ffn)
    ffn_low = across_cores([part.astype(BF16) for part in normed_ffn])

    def across(part):
        return lax.ppermute(part, "cx", SWAP)

    def over_shard(total):
        return lax.psum_scatter(total, "shard", scatter_dimension=0, tiled=True)

    def grad_of(rows, grads):
        return dot_tn(rows, grads).astype(BF16)

    def grad_with(rows, grads, arrived):
        return (dot_tn(rows, grads) + arrived.astype(F32)).astype(BF16)

    steps = Steps()
    gate = steps(dots, dot_nn, ffn_low, gates)

    def activate(ffn_low, ups, gate):
        up = dots(dot_nn, ffn_low, ups)
        return up, (jax.nn.silu(gate) * up).astype(BF16)

    up, act = steps(activate, ffn_low, ups, gate)
    down_own = over_shard(steps(grad_of, grad_all[0], act))
    down_other = over_shard(steps(grad_of, grad_all[1], act))

    def ffn_grads(grad_all, downs, gate, up):
        d_act = dots(dot_nn, grad_all, downs).astype(BF16).astype(F32)
        sig = jax.nn.sigmoid(gate)
        d_gate = (d_act * up * sig * (1.0 + gate * (1.0 - sig))).astype(BF16)
        return d_gate, (d_act * gate * sig).astype(BF16)

    steps.wait(down_own)
    d_gate, d_up = steps(ffn_grads, grad_all, downs, gate, up)
    gate_sent = across(steps(grad_of, ffn_low[1], d_gate))

    def ffn_back(d_gate, d_up, gates, ups, rows):
        return [dot_nt(d_gate[rows], gates[i]) + dot_nt(d_up[rows], ups[i]) for i in range(2)]

    def away(fn, *args):
        values = steps(lambda *args: [part.astype(BF16) for part in fn(*args, other_rows)], *args)
        return [lax.ppermute(part, "core", SWAP) for part in values]

    def here(fn, arrived, *args):
        def total(arrived, *args):
            return [
                (own + more.astype(F32)).astype(BF16)
                for own, more in zip(fn(*args, first_rows), arrived)
            ]

        return steps(total, arrived, *args)

    def with_tp(parts):
        return [(part, lax.ppermute(part, "tp", SWAP)) for part in parts]

    args = (d_gate, d_up, gates, ups)
    arrived = away(ffn_back, *args)
    d_ffn_pairs = with_tp(here(ffn_back, arrived, *args))
    up_dot = steps(grad_of, ffn_low[1], d_up)

    def down_rows(act, downs, rows):
        return [dot_nt(act[rows], part) for part in downs]

    arrived = away(down_rows, act, downs)
    down_parts = here(down_rows, arrived, act, downs)
    gate_total = steps(grad_with, ffn_low[0], d_gate, gate_sent)
    steps.wait(down_other)
    grad_gate = over_shard(gate_total)

    def resid_back(d_ffn_pairs, grad_all):
        d_ffn = add_pairs(d_ffn_pairs, [jnp.zeros(part[0].shape, F32) for part in d_ffn_pairs])
        d_resid, sum_ffn_gain = ffn_pull(d_ffn)
        d_resid = [part[:own_rows].astype(F32) + more for part, more in zip(grad_all, d_resid)]
        return d_resid, sum_ffn_gain, [part.astype(BF16) for part in d_resid]

    d_resid, sum_ffn_gain, resid_own = steps(resid_back, d_ffn_pairs, grad_all)
    down_pairs = with_tp(tie(down_parts, resid_own))
    resid_other = [lax.ppermute(part, "core", SWAP) for part in resid_own]
    resid_low = steps(
        lambda own, other: [jnp.concatenate(parts) for parts in zip(own, other)],
        resid_own,
        resid_other,
    )
    outer_sent = across(steps(grad_of, resid_low[1], head_rows))
    d_head = steps(lambda rows, outer: dots(dot_nn, rows, outer).astype(BF16), resid_low, outer)
    d_head = d_head.reshape(head_low.shape)
    thirds = []
    for pair in pairs:
        thirds.append(
            steps(calls[pair][2], d_head, seconds[pair][1], *firsts[pair][:2], firsts[pair][3])
        )
    d_finals = [lax.ppermute(third[1], "cx", [(1, 0)]) for third in thirds]
    up_sent = across(tie(up_dot, d_finals, outer_sent))
    outer_total = steps(grad_with, resid_low[0], head_rows, outer_sent)
    grad_outer = over_shard(outer_total)

    def with_edge(d_raw, d_edge):
        window = (1 - core, 0, size - HALO, 0)
        edge_rows = lax.dynamic_slice(d_raw, window, (1,) + d_edge.shape)
        return lax.dynamic_update_slice(
            d_raw, (edge_rows.astype(F32) + d_edge.astype(F32)[None]).astype(BF16), window
        ).reshape(2 * own_rows, -1)

    def joint_step(d_raw, d_edge, rows):
        d_raw = with_edge(d_raw, d_edge)
        return d_raw, grad_of(rows, d_raw)

    normed_rows = [part[: 2 * own_rows] for part in normed_low]
    steps.wait(grad_gate)
    fourths, edges = [], []
    for pair in pairs:
        query, key, value, inverse, _ = firsts[pair]
        _, _, fresh, middle = seconds[pair]
        fourth = steps(
            calls[pair][3],
            query,
            key,
            value,
            inverse,
            fresh,
            thirds[pair][0],
            incomings[pair],
            middle,
            d_finals[pair],
        )
        edges.append(lax.ppermute(fourth[1], "cx", [(1, 0)]))
        fourths.append(fourth)
    steps.wait(grad_outer)
    d_raws, joint_sents = [], []
    for pair in pairs:
        d_raw, joint_dot = steps(joint_step, fourths[pair][0], edges[pair], normed_rows[1])
        d_raws.append(d_raw)
        joint_sents.append(across(joint_dot))
    up_total = steps(grad_with, ffn_low[0], d_up, up_sent)
    grad_up = over_shard(up_total)

    def logit_step(rates, rows):
        d_rates = sum(rates)
        d_logit = jnp.where(core == 0, d_rates, d_rates[:, ::-1]).transpose(1, 0, 2, 3)
        d_logit = d_logit.reshape(2 * own_rows, LANES).astype(BF16)
        return d_logit, jnp.stack([dot_tn(part, d_logit)[:, :heads] for part in rows])

    d_logit, sum_rate = steps(logit_step, [fourth[2] for fourth in fourths], normed_rows)

    def normed_back(d_raws, d_logit, joint, beta, rows):
        return [
            sum(dot_nt(d_raw[rows], part[i]) for d_raw, part in zip(d_raws, joint))
            + dot_nt(d_logit[rows], beta[i])
            for i in range(2)
        ]

    args = (d_raws, d_logit, joint, beta)
    arrived = away(normed_back, *args)
    d_normed_pairs = with_tp(here(normed_back, arrived, *args))
    result = steps(add_pairs, down_pairs, resid)
    result_rows = steps(
        lambda result: join_rows(places, [part.astype(BF16) for part in result], count), result
    )
    sum_head_gain = sum(jnp.sum(third[2][:, :, 0, :], axis=(0, 1)) for third in thirds)
    sum_head_gain = sum_over(sum_head_gain.astype(BF16), "tp", 1).astype(F32)
    grad_joint = [over_shard(steps(grad_with, normed_rows[0], d_raws[0], joint_sents[0]))]
    grad_down = steps(
        lambda own, other: (own.astype(F32) + other.astype(F32)).astype(BF16),
        down_own,
        across(tie(down_other, joint_sents[0])),
    )

    def input_back(d_normed_pairs, d_resid):
        d_normed = add_pairs(d_normed_pairs, [jnp.zeros(part.shape, F32) for part in d_resid])
        _, norm_pull = jax.vjp(rms_split, hidden_f32, gain_in)
        d_hidden, sum_attn_gain = norm_pull(d_normed)
        return sum_attn_gain, [(a + b).astype(BF16) for a, b in zip(d_resid, d_hidden)]

    steps.wait(grad_up)
    sum_attn_gain, input_halves = steps(input_back, d_normed_pairs, d_resid)
    grad_joint += [
        over_shard(steps(grad_with, normed_rows[0], d_raws[pair], joint_sents[pair]))
        for pair in pairs[1:]
    ]
    input_rows = steps(lambda halves: join_rows(places, halves, count), input_halves)
    out_down = lay_block_turned(places, pieces_of(grad_down))
    out_gate = lay_block(places, pieces_of(grad_gate))
    out_up = lay_block(places, pieces_of(grad_up))

    d_taps = jnp.concatenate([fourth[3] for fourth in fourths], axis=2)
    sum_taps = jnp.sum(d_taps, axis=0).transpose(2, 0, 1, 3)
    sum_rate = join_small(places, sum_rate, count)
    gains = jnp.concatenate(
        [
            join_small(places, jnp.concatenate(sum_attn_gain), count),
            join_small(places, jnp.concatenate(sum_ffn_gain), count),
            sum_head_gain,
        ]
    ).astype(BF16)
    gains = sum_over(gains, "core", 1)
    packed = jnp.concatenate(
        [gains, sum_taps.reshape(-1).astype(BF16), sum_rate.reshape(-1).astype(BF16)]
    )
    packed = sum_over(packed, "cx", 1)
    hop = 1
    while hop < count:
        packed = sum_over(packed, "shard", hop)
        hop *= 2
    own = lax.axis_index("shard")
    ends = [width, 2 * width, 2 * width + LANES, 2 * width + LANES + sum_taps.size]
    grad_attn_gain = lax.dynamic_slice_in_dim(packed[: ends[0]], own * piece_d, piece_d)
    grad_ffn_gain = lax.dynamic_slice_in_dim(packed[ends[0] : ends[1]], own * piece_d, piece_d)
    grad_out_gain = lax.dynamic_slice_in_dim(packed[ends[1] : ends[2]], own * entry, entry)
    own_conv = lax.dynamic_slice_in_dim(
        packed[ends[2] : ends[3]].reshape(4, 3, heads, LANES), own * entry, entry, axis=3
    )
    own_beta = lax.dynamic_slice_in_dim(
        packed[ends[3] :].reshape(width, heads), own * piece_d, piece_d, axis=0
    )

    def both_cores(values, axis):
        other = lax.ppermute(values, "core", SWAP)
        return jnp.where(
            core == 0,
            jnp.concatenate([values, other], axis=axis),
            jnp.concatenate([other, values], axis=axis),
        ).astype(F32)

    grad_out_weight = lay_block_turned(places, pieces_of(grad_outer))
    grad_query, grad_key, grad_value = lay_heads(places, [pieces_of(part) for part in grad_joint])
    return (
        result_rows.reshape(hidden_in.shape),
        input_rows.reshape(hidden_in.shape),
        grad_attn_gain.astype(F32),
        grad_query,
        grad_key,
        grad_value,
        both_cores(own_conv, 2),
        both_cores(own_beta, 1),
        grad_out_gain.astype(F32),
        grad_out_weight,
        grad_ffn_gain.astype(F32),
        out_gate,
        out_up,
        out_down,
    )


def solution(mesh):
    shard, ctx, tp = (mesh.shape[name] for name in ("shard", "ctx", "tp"))
    cores = Mesh(
        mesh.devices.reshape(shard, ctx // 2, 2, tp), ("shard", "cx", "core", "tp")
    )
    tokens = P(None, "shard", ("cx", "core"), None)
    outer = P("shard", "tp")
    turned = P("tp", "shard")
    conv = P(None, None, "tp", "shard")
    split = P("shard")
    return jax.shard_map(
        shards,
        mesh=cores,
        in_specs=(
            tokens,
            split,
            outer,
            outer,
            outer,
            conv,
            outer,
            split,
            turned,
            split,
            outer,
            outer,
            turned,
            tokens,
            P(None, "shard", ("cx", "core")),
        ),
        out_specs=(
            tokens,
            tokens,
            split,
            outer,
            outer,
            outer,
            conv,
            outer,
            split,
            turned,
            split,
            outer,
            outer,
            turned,
        ),
        check_vma=False,
    )
```

```python
import functools

import jax
import jax.numpy as jnp
from jax import lax
from jax.experimental import pallas as pl
from jax.experimental.pallas import tpu as pltpu
from jax.sharding import Mesh
from jax.sharding import PartitionSpec as P

EPSILON = 1e-06
F32 = jnp.float32
BF16 = jnp.bfloat16
LANES = 128
HALO = 16
SWAP = [(0, 1), (1, 0)]
LONG = 6 * 10**10


def mm(left, right, left_dim, right_dim):
    return lax.dot_general(
        left.astype(BF16),
        right.astype(BF16),
        (((left_dim,), (right_dim,)), ((), ())),
        preferred_element_type=F32,
    )


def nn(left, right):
    return mm(left, right, 1, 0)


def nt(left, right):
    return mm(left, right, 1, 1)


def tn(left, right):
    return mm(left, right, 0, 0)


def place_scalars():
    return jnp.stack([lax.axis_index("core"), lax.axis_index("cx")]).astype(jnp.int32)


def call(kernel, grid, in_specs, out_specs, out_shape, scratch=(), flops=1000):
    return pl.pallas_call(
        kernel,
        grid_spec=pltpu.PrefetchScalarGridSpec(
            num_scalar_prefetch=1,
            grid=grid,
            in_specs=in_specs,
            out_specs=out_specs,
            scratch_shapes=list(scratch),
        ),
        out_shape=out_shape,
        compiler_params=pltpu.CompilerParams(
            dimension_semantics=("arbitrary",) * len(grid), vmem_limit_bytes=48 << 20
        ),
        cost_estimate=pl.CostEstimate(flops=flops, transcendentals=0, bytes_accessed=1000),
    )


def pack_heads(places, query, key, value, heads):
    rows = query.shape[0]

    def kernel(where, query_ref, key_ref, value_ref, out):
        out[:, :LANES] = query_ref[...]
        out[:, LANES : 2 * LANES] = key_ref[...]
        out[:, 2 * LANES :] = value_ref[...]

    spec = pl.BlockSpec((rows, LANES), lambda h, w: (0, w[0] * heads + 2 * w[1] + h))
    return call(
        kernel,
        (2,),
        [spec] * 3,
        pl.BlockSpec((rows, 3 * LANES), lambda h, w: (0, h)),
        jax.ShapeDtypeStruct((rows, 6 * LANES), query.dtype),
    )(places, query, key, value)


def own_parts(units):
    wide = units // 2
    main = wide // (2 * LANES) * LANES
    return wide, main, wide - 2 * main


def own_units(places, weight, axis):
    wide, main, rest = own_parts(weight.shape[axis])
    first = lax.dynamic_slice_in_dim(weight, places[0] * wide + places[1] * main, main, axis)
    last = lax.dynamic_slice_in_dim(weight, places[0] * wide + 2 * main, rest, axis)
    low, high = jnp.split(last, 2, axis)
    return jnp.concatenate([first, jnp.where(places[1] == 0, low, high)], axis)


def own_heads(places, weight):
    rows = weight.shape[0] // 4
    return lax.dynamic_slice_in_dim(weight, (2 * places[0] + places[1]) * rows, rows, 0)


def pieces_of(own, *after):
    across = lax.ppermute(own, "cx", SWAP)
    late = tie(across, after)
    return [own, across, lax.ppermute(own, "core", SWAP), lax.ppermute(late, "core", SWAP)]


def pick(where, core, cx, refs, store):
    which = 2 * jnp.bitwise_xor(where[0], core) + jnp.bitwise_xor(where[1], cx)
    for index in range(4):

        @pl.when(which == index)
        def _():
            store(refs[index][...].astype(F32))


def lay_heads(places, heads):
    rows = heads[0][0].shape[0]

    def kernel(where, *refs):
        outs = refs[-3:]
        for head in range(2):

            def store(values):
                for index in range(3):
                    outs[index][:, head * LANES : (head + 1) * LANES] = values[
                        :, index * LANES : (index + 1) * LANES
                    ]

            pick(where, pl.program_id(0), pl.program_id(1), refs[4 * head : 4 * head + 4], store)

    return call(
        kernel,
        (2, 2),
        [pl.BlockSpec(heads[0][0].shape, lambda i, j, w: (0, 0))] * 8,
        [pl.BlockSpec((rows, 2 * LANES), lambda i, j, w: (0, 2 * i + j))] * 3,
        [jax.ShapeDtypeStruct((rows, 8 * LANES), F32)] * 3,
    )(places, *heads[0], *heads[1])


def lay_units(places, pieces):
    rows, units = pieces[0].shape
    wide, main, rest = own_parts(4 * units)
    half = rest // 2

    def kernel(where, a, b, c, d, out):
        for side in range(2):

            def store(values):
                out[:, side * main : (side + 1) * main] = values[:, :main]
                at = 2 * main + side * half
                out[:, at : at + half] = values[:, main:]

            pick(where, pl.program_id(0), side, (a, b, c, d), store)

    return call(
        kernel,
        (2,),
        [pl.BlockSpec((rows, units), lambda i, w: (0, 0))] * 4,
        pl.BlockSpec((rows, wide), lambda i, w: (0, i)),
        jax.ShapeDtypeStruct((rows, 2 * wide), F32),
    )(places, *pieces)


def lay_units_turned(places, pieces):
    rows, units = pieces[0].shape
    wide, main, rest = own_parts(4 * units)
    half = rest // 2

    def kernel(where, a, b, c, d, out):
        for side in range(2):

            def store(values):
                turned = values.T
                out[side * main : (side + 1) * main, :] = turned[:main]
                at = 2 * main + side * half
                out[at : at + half, :] = turned[main:]

            pick(where, pl.program_id(0), side, (a, b, c, d), store)

    return call(
        kernel,
        (2,),
        [pl.BlockSpec((rows, units), lambda i, w: (0, 0))] * 4,
        pl.BlockSpec((wide, rows), lambda i, w: (i, 0)),
        jax.ShapeDtypeStruct((2 * wide, rows), F32),
    )(places, *pieces)


def lay_heads_turned(places, pieces):
    rows, columns = pieces[0].shape

    def kernel(where, a, b, c, d, out):
        def store(values):
            out[...] = values.T

        pick(where, pl.program_id(0), pl.program_id(1), (a, b, c, d), store)

    return call(
        kernel,
        (2, 2),
        [pl.BlockSpec((rows, columns), lambda i, j, w: (0, 0))] * 4,
        pl.BlockSpec((columns, rows), lambda i, j, w: (2 * i + j, 0)),
        jax.ShapeDtypeStruct((4 * columns, rows), F32),
    )(places, *pieces)


def fill_ext(ext, index, halo, first, second, size):
    ext[index, :HALO, :] = halo[...].astype(F32)
    ext[index, HALO : HALO + size, :] = first[...].astype(F32)
    ext[index, HALO + size :, :] = second[...].astype(F32)


def links_of(ids, total):
    own = ids[0, HALO : HALO + total, :]
    return [
        (ids[0, HALO - 3 + tap : HALO - 3 + tap + total, :] == own).astype(F32) for tap in range(4)
    ]


def conv_of(ext, index, taps, links, total):
    result = None
    for tap in range(4):
        term = (
            taps[index, 0, tap : tap + 1, :]
            * ext[index, HALO - 3 + tap : HALO - 3 + tap + total, :]
            * links[tap]
        )
        result = term if result is None else result + term
    return result


def sigmoid(values):
    return 1.0 / (1.0 + jnp.exp(-values))


def first_head(where, own):
    return 2 * (where[1] if own else 1 - where[1])


def head_of(where, own):
    return first_head(where, own) + pl.program_id(1)


def column_of(values, head):
    lane = lax.broadcasted_iota(jnp.int32, values.shape, 1)
    return jnp.sum(jnp.where(lane == head, values, 0.0), axis=1, keepdims=True)


def marks(ids, rows, chunk, size):
    start = HALO + chunk * size
    column = ids[0, start : start + size, :]
    before = ids[0, start - 1 : start, :]
    last = ids[0, start + size - 1 : start + size, :]
    first = (column == before).astype(F32)
    tail = (column == last).astype(F32)
    whole = (last == before).astype(F32)
    same = column == rows[0, chunk : chunk + 1, :]
    row = lax.broadcasted_iota(jnp.int32, (size, size), 0)
    col = lax.broadcasted_iota(jnp.int32, (size, size), 1)
    return first, tail, whole, same & (row > col), same & (row >= col)


def inverse_units(stricts, size):
    row = lax.broadcasted_iota(jnp.int32, (size, size), 0)
    col = lax.broadcasted_iota(jnp.int32, (size, size), 1)
    mixed = jnp.bitwise_xor(row, col)
    results = [
        jnp.where(row == col, 1.0, jnp.where(mixed == 1, -strict, 0.0)) for strict in stricts
    ]
    stricts = [strict.astype(BF16) for strict in stricts]
    block = 2
    while block < size:
        pair = (mixed >= block) & (mixed < 2 * block)
        lows = [result.astype(BF16) for result in results]
        parts = [jnp.where(pair, strict, 0.0) for strict in stricts]
        steps = [nn(part, low).astype(BF16) for part, low in zip(parts, lows)]
        results = [
            result - nn(low, step) for result, low, step in zip(results, lows, steps)
        ]
        block *= 2
    return [result.astype(BF16) for result in results]


def forward_one(where, q0, k0, v0, q1, k1, v1, qh, kh, vh, taps, ids, rows, r0, r1, *rest, size, own):
    query, key, value, inverse, final, ext = rest
    head = head_of(where, own)
    total = 2 * size
    for index, group in enumerate(((qh, q0, q1), (kh, k0, k1), (vh, v0, v1))):
        fill_ext(ext, index, *group, size)
    links = links_of(ids, total)
    out = []
    for index in range(3):
        conv = conv_of(ext, index, taps, links, total)
        act = conv * sigmoid(conv)
        if index < 2:
            act = act * lax.rsqrt(jnp.sum(act * act, axis=1, keepdims=True) + EPSILON)
        out.append(act.astype(BF16))
    for target, values in zip((query, key, value), out):
        target[0, 0] = values[:size]
        target[0, 1] = values[size:]
    chunks = []
    for chunk, rates in enumerate((r0, r1)):
        first, tail, whole, strict, _ = marks(ids, rows, chunk, size)
        rate = column_of(rates[...], head)
        keys = out[1][chunk * size : (chunk + 1) * size]
        chunks.append((first, tail, whole, rate, keys, jnp.where(strict, rate * nt(keys, keys), 0.0)))
    inverses = inverse_units([item[-1] for item in chunks], size)
    state = None
    for chunk, (first, tail, whole, rate, keys, _) in enumerate(chunks):
        fresh = out[2][chunk * size : (chunk + 1) * size].astype(F32)
        inverse[0, 0, chunk] = inverses[chunk]
        if chunk:
            fresh = fresh - first * nt(keys, state)
        fresh = nn(inverses[chunk], rate * fresh)
        added = tn(tail * fresh, keys)
        state = added if state is None else whole * state + added
    final[0, 0] = state.astype(BF16)


def forward_two(where, query, key, value, inverse, ids, rows, r0, r1, incoming, gain, *rest, size, scale, own):
    head_low, mixed_out, fresh_out, middle = rest
    head = head_of(where, own)
    state = incoming[0, 0].astype(F32)
    for chunk, rates in enumerate((r0, r1)):
        first, tail, whole, _, lower = marks(ids, rows, chunk, size)
        rate = column_of(rates[...], head)
        keys, queries = key[0, chunk], query[0, chunk]
        if chunk:
            middle[0, 0] = state.astype(BF16)
        rest_rows = value[0, chunk].astype(F32) - first * nt(keys, state)
        fresh = nn(inverse[0, 0, chunk], rate * rest_rows)
        fresh_out[0, chunk] = fresh.astype(BF16)
        inner = jnp.where(lower, nt(queries, keys), 0.0)
        mixed = scale * (first * nt(queries, state) + nn(inner, fresh))
        mixed_out[0, chunk] = mixed
        normed = mixed * lax.rsqrt(jnp.mean(mixed * mixed, axis=1, keepdims=True) + EPSILON)
        slot = where[0] if chunk == 0 else 1 - where[0]
        head_low[slot, 0] = (normed * gain[...]).astype(BF16)
        if chunk == 0:
            state = whole * state + tn(tail * fresh, keys)


def backward_one(where, d_head, mixed, query, key, inverse, ids, rows, r0, r1, gain, *rest, size, scale, own):
    d_out, d_state_out, d_gain = rest
    head = head_of(where, own)
    total = jnp.zeros((1, LANES), F32)
    d_state = None
    for chunk in (1, 0):
        first, tail, whole, _, lower = marks(ids, rows, chunk, size)
        rate = column_of((r0, r1)[chunk][...], head)
        keys, queries = key[0, chunk], query[0, chunk]
        slot = where[0] if chunk == 0 else 1 - where[0]
        grad = d_head[slot, 0].astype(F32)
        values = mixed[0, chunk]
        inv_rms = lax.rsqrt(jnp.mean(values * values, axis=1, keepdims=True) + EPSILON)
        normed = values * inv_rms
        total = total + jnp.sum(grad * normed, axis=0, keepdims=True)
        scaled = grad * gain[...]
        d_mixed = inv_rms * (scaled - normed * jnp.mean(scaled * normed, axis=1, keepdims=True))
        d_low = (scale * d_mixed).astype(BF16)
        d_out[0, chunk] = d_low
        inner = jnp.where(lower, nt(queries, keys), 0.0)
        d_fresh = tn(inner, d_low)
        if d_state is not None:
            d_fresh = d_fresh + tail * nt(keys, d_state)
        d_rest = rate * tn(inverse[0, 0, chunk], d_fresh)
        change = tn(first * d_low.astype(F32), queries) - tn(first * d_rest, keys)
        d_state = change if d_state is None else whole * d_state + change
    d_state_out[0, 0] = d_state.astype(BF16)
    d_gain[0, 0] = jnp.broadcast_to(total, (8, LANES))


def backward_two(where, q0, k0, v0, q1, k1, v1, qh, kh, vh, taps, ids, rows, r0, r1, *rest, size, own):
    query, key, value, inverse, fresh_in, d_in, incoming, middle, d_final = rest[:9]
    d_raw, d_edge, d_rates, d_taps = rest[9:13]
    ext, d_ext, d_rows = rest[13:]
    head = head_of(where, own)
    total = 2 * size
    for index, group in enumerate(((qh, q0, q1), (kh, k0, k1), (vh, v0, v1))):
        fill_ext(ext, index, *group, size)
    d_state = d_final[0, 0].astype(F32)

    @pl.when(pl.program_id(1) == 0)
    def _():
        d_rates[...] = jnp.zeros_like(d_rates)

    for chunk in (1, 0):
        first, tail, whole, strict, lower = marks(ids, rows, chunk, size)
        rate = column_of((r0, r1)[chunk][...], head)
        keys, queries, fresh = key[0, chunk], query[0, chunk], fresh_in[0, chunk]
        inv, d_low = inverse[0, 0, chunk], d_in[0, chunk]
        state = (middle if chunk else incoming)[0, 0]
        d_mix = d_low.astype(F32)
        inner = jnp.where(lower, nt(queries, keys), 0.0)
        gram = jnp.where(strict, nt(keys, keys), 0.0)
        d_fresh = tn(inner, d_low) + tail * nt(keys, d_state)
        turned = tn(inv, d_fresh)
        d_rest = rate * turned
        rest_rows = value[0, chunk].astype(F32) - first * nt(keys, state)
        error = rest_rows - nn(gram, fresh)
        d_rate = jnp.sum(turned * error, axis=1, keepdims=True) * rate * (1.0 - rate)
        d_inner = jnp.where(lower, nt(d_low, fresh), 0.0)
        d_gram = rate * jnp.where(strict, -nt(turned, fresh), 0.0)
        d_query = first * nn(d_low, state) + nn(d_inner, keys)
        d_key = (
            tn(d_inner, queries)
            + tail * nn(fresh, d_state)
            - nn(first * d_rest, state)
            + nn(d_gram, keys)
            + tn(d_gram, keys)
        )
        for index, values in enumerate((d_query, d_key, d_rest)):
            d_rows[index, chunk * size : (chunk + 1) * size, :] = values
        lane = lax.broadcasted_iota(jnp.int32, (size, LANES), 1)
        d_rates[0, chunk] = d_rates[0, chunk] + jnp.where(lane == head, d_rate, 0.0)
        if chunk:
            d_state = (
                whole * d_state + tn(first * d_mix, queries) - tn(first * d_rest, keys)
            )
    links = links_of(ids, total)
    for index in range(3):
        conv = conv_of(ext, index, taps, links, total)
        sig = sigmoid(conv)
        d_act = d_rows[index].astype(BF16).astype(F32)
        if index < 2:
            act = conv * sig
            inv_norm = lax.rsqrt(jnp.sum(act * act, axis=1, keepdims=True) + EPSILON)
            unit = act * inv_norm
            d_act = (d_act - unit * jnp.sum(unit * d_act, axis=1, keepdims=True)) * inv_norm
        d_conv = d_act * sig * (1.0 + conv * (1.0 - sig))
        d_ext[...] = jnp.zeros_like(d_ext)
        for tap in range(4):
            window = slice(HALO - 3 + tap, HALO - 3 + tap + total)
            linked = d_conv * links[tap]
            d_taps[0, index, 0, tap : tap + 1, :] = jnp.sum(
                linked * ext[index, window, :], axis=0, keepdims=True
            )
            d_ext[window, :] = d_ext[window, :] + taps[index, 0, tap : tap + 1, :] * linked
        lanes = slice(index * LANES, (index + 1) * LANES)
        d_edge[0, :, lanes] = d_ext[:HALO, :].astype(BF16)
        d_raw[where[0], 0, :, lanes] = d_ext[HALO : HALO + size, :].astype(BF16)
        d_raw[1 - where[0], 0, :, lanes] = d_ext[HALO + size :, :].astype(BF16)


def mixer_calls(places, own, rates, ids, rows, taps, gain, seqs, size, scale):
    def slot_of(chunk, w):
        return w[0] if chunk == 0 else 1 - w[0]

    def raw_spec(chunk, part):
        return pl.BlockSpec(
            (size, LANES), lambda b, h, w: (slot_of(chunk, w) * seqs + b, 3 * h + part)
        )

    def rate_spec(chunk):
        return pl.BlockSpec((size, LANES), lambda b, h, w: (slot_of(chunk, w) * seqs + b, 0))

    halo_base = 2 * seqs * size // HALO

    def halo_spec(part):
        return pl.BlockSpec((HALO, LANES), lambda b, h, w: (halo_base + b, 3 * h + part))

    conv_specs = (
        [raw_spec(c, p) for c in range(2) for p in range(3)]
        + [halo_spec(p) for p in range(3)]
        + [
            pl.BlockSpec((3, 1, 4, LANES), lambda b, h, w: (0, first_head(w, own) + h, 0, 0)),
            pl.BlockSpec((1, HALO + 2 * size, 1), lambda b, h, w: (b, 0, 0)),
            pl.BlockSpec((1, 2, size), lambda b, h, w: (b, 0, 0)),
            rate_spec(0),
            rate_spec(1),
        ]
    )
    rest_args = (taps, ids, rows, rates, rates)
    id_specs, id_args = conv_specs[10:], rest_args[1:]
    act_spec = pl.BlockSpec((1, 2, size, LANES), lambda b, h, w: (b, 0, 0, h))
    act_shape = (seqs, 2, size, 2 * LANES)
    state_spec = pl.BlockSpec((1, 1, LANES, LANES), lambda b, h, w: (b, h, 0, 0))
    state_shape = jax.ShapeDtypeStruct((seqs, 2, LANES, LANES), BF16)
    inv_spec = pl.BlockSpec((1, 1, 2, size, size), lambda b, h, w: (b, h, 0, 0, 0))
    inv_shape = jax.ShapeDtypeStruct((seqs, 2, 2, size, size), BF16)
    slot_spec = pl.BlockSpec((2, 1, size, LANES), lambda b, h, w: (0, b, 0, h))
    slot_shape = jax.ShapeDtypeStruct((2, seqs, size, 2 * LANES), BF16)
    gain_spec = pl.BlockSpec((1, LANES), lambda b, h, w: (0, 0))
    low = jax.ShapeDtypeStruct(act_shape, BF16)
    grid = (seqs, 2)

    def one(raw):
        return call(
            functools.partial(forward_one, size=size, own=own),
            grid,
            conv_specs,
            [act_spec] * 3 + [inv_spec, state_spec],
            [low] * 3 + [inv_shape, state_shape],
            [pltpu.VMEM((3, HALO + 2 * size, LANES), F32)],
        )(places, *(raw,) * 9, *rest_args)

    def two(query, key, value, inverse, incoming):
        args = (query, key, value, inverse, *id_args, incoming, gain)
        return call(
            functools.partial(forward_two, size=size, scale=scale, own=own),
            grid,
            [act_spec] * 3
            + [inv_spec]
            + id_specs
            + [state_spec, gain_spec],
            [slot_spec, act_spec, act_spec, state_spec],
            [slot_shape, jax.ShapeDtypeStruct(act_shape, F32), low, state_shape],
        )(places, *args)

    def three(d_head, mixed, query, key, inverse):
        return call(
            functools.partial(backward_one, size=size, scale=scale, own=own),
            grid,
            [slot_spec, act_spec, act_spec, act_spec, inv_spec] + id_specs + [gain_spec],
            [act_spec, state_spec, pl.BlockSpec((1, 1, 8, LANES), lambda b, h, w: (b, h, 0, 0))],
            [low, state_shape, jax.ShapeDtypeStruct((seqs, 2, 8, LANES), F32)],
            flops=LONG,
        )(places, d_head, mixed, query, key, inverse, *id_args, gain)

    def four(raw, query, key, value, inverse, fresh, d_low, incoming, middle, d_final):
        return call(
            functools.partial(backward_two, size=size, own=own),
            grid,
            conv_specs + [act_spec] * 3 + [inv_spec, act_spec, act_spec] + [state_spec] * 3,
            [
                pl.BlockSpec((2, 1, size, 3 * LANES), lambda b, h, w: (0, b, 0, h)),
                pl.BlockSpec((1, HALO, 3 * LANES), lambda b, h, w: (b, 0, h)),
                pl.BlockSpec((1, 2, size, LANES), lambda b, h, w: (b, 0, 0, 0)),
                pl.BlockSpec((1, 3, 1, 4, LANES), lambda b, h, w: (b, 0, h, 0, 0)),
            ],
            [
                jax.ShapeDtypeStruct((2, seqs, size, 6 * LANES), BF16),
                jax.ShapeDtypeStruct((seqs, HALO, 6 * LANES), BF16),
                jax.ShapeDtypeStruct((seqs, 2, size, LANES), F32),
                jax.ShapeDtypeStruct((seqs, 3, 2, 4, LANES), F32),
            ],
            [
                pltpu.VMEM((3, HALO + 2 * size, LANES), F32),
                pltpu.VMEM((HALO + 2 * size, LANES), F32),
                pltpu.VMEM((3, 2 * size, LANES), F32),
            ],
            flops=LONG,
        )(
            places,
            *(raw,) * 9,
            *rest_args,
            query,
            key,
            value,
            inverse,
            fresh,
            d_low,
            incoming,
            middle,
            d_final,
        )

    return one, two, three, four


def tile_of(extent):
    return 512 if extent % 512 == 0 else extent


def rows_products(pairs, rows, block, add=None, out=BF16):
    columns = pairs[0][1].shape[0]
    tile = tile_of(columns)
    count = len(pairs)

    def kernel(*refs):
        total = None
        for index in range(count):
            part = nt(refs[index][...], refs[count + index][...])
            total = part if total is None else total + part
        if add is not None:
            total = total + refs[2 * count][...].astype(F32)
        refs[-1][...] = total.astype(out)

    lefts = [pl.BlockSpec((rows, left.shape[1]), lambda i: (block, 0)) for left, _ in pairs]
    rights = [pl.BlockSpec((tile, right.shape[1]), lambda i: (i, 0)) for _, right in pairs]
    spec = pl.BlockSpec((rows, tile), lambda i: (0, i))
    extra = () if add is None else (add,)
    return pl.pallas_call(
        kernel,
        grid=(columns // tile,),
        in_specs=lefts + rights + [spec] * len(extra),
        out_specs=spec,
        out_shape=jax.ShapeDtypeStruct((rows, columns), out),
        compiler_params=pltpu.CompilerParams(vmem_limit_bytes=48 << 20),
        cost_estimate=pl.CostEstimate(flops=1000, transcendentals=0, bytes_accessed=1000),
    )(*(left for left, _ in pairs), *(right for _, right in pairs), *extra)


def token_products(pairs, add=None):
    count = len(pairs)
    height, columns = pairs[0][0].shape[1], pairs[0][1].shape[1]
    tile = tile_of(height)

    def kernel(*refs):
        total = None
        for index in range(count):
            part = tn(refs[index][...], refs[count + index][...])
            total = part if total is None else total + part
        if add is not None:
            total = total + refs[2 * count][...].astype(F32)
        refs[-1][...] = total.astype(BF16)

    lefts = [
        pl.BlockSpec((rows, tile), lambda i, block=block: (block, i))
        for _, _, rows, block in pairs
    ]
    rights = [pl.BlockSpec((rows, columns), lambda i: (0, 0)) for _, _, rows, _ in pairs]
    spec = pl.BlockSpec((tile, columns), lambda i: (i, 0))
    extra = () if add is None else (add,)
    return pl.pallas_call(
        kernel,
        grid=(height // tile,),
        in_specs=lefts + rights + [spec] * len(extra),
        out_specs=spec,
        out_shape=jax.ShapeDtypeStruct((height, columns), BF16),
        compiler_params=pltpu.CompilerParams(vmem_limit_bytes=48 << 20),
        cost_estimate=pl.CostEstimate(flops=1000, transcendentals=0, bytes_accessed=1000),
    )(*(item[0] for item in pairs), *(item[1] for item in pairs), *extra)


def feed_forward(rows, grads, gates, ups, downs):
    tokens, width = rows.shape
    units = gates.shape[1]
    tile = 256 if tokens % 256 == 0 else tokens

    def kernel(rows_ref, grads_ref, gates_ref, ups_ref, downs_ref, act, d_gate, d_up):
        gate = nn(rows_ref[...], gates_ref[...])
        up = nn(rows_ref[...], ups_ref[...])
        d_act = nn(grads_ref[...], downs_ref[...]).astype(BF16).astype(F32)
        sig = sigmoid(gate)
        act[...] = (gate * sig * up).astype(BF16)
        d_gate[...] = (d_act * up * sig * (1.0 + gate * (1.0 - sig))).astype(BF16)
        d_up[...] = (d_act * gate * sig).astype(BF16)

    token_spec = pl.BlockSpec((tile, width), lambda i: (i, 0))
    weight_spec = pl.BlockSpec((width, units), lambda i: (0, 0))
    unit_spec = pl.BlockSpec((tile, units), lambda i: (i, 0))
    return pl.pallas_call(
        kernel,
        grid=(tokens // tile,),
        in_specs=[token_spec] * 2 + [weight_spec] * 3,
        out_specs=[unit_spec] * 3,
        out_shape=[jax.ShapeDtypeStruct((tokens, units), BF16)] * 3,
        compiler_params=pltpu.CompilerParams(vmem_limit_bytes=48 << 20),
        cost_estimate=pl.CostEstimate(flops=1000, transcendentals=0, bytes_accessed=1000),
    )(rows, grads, gates, ups, downs)


def dot_nn(left, right):
    return lax.dot_general(left, right, (((1,), (0,)), ((), ())), preferred_element_type=F32)


def dot_nt(left, right):
    return lax.dot_general(left, right, (((1,), (1,)), ((), ())), preferred_element_type=F32)


def dot_tn(left, right):
    return lax.dot_general(left, right, (((0,), (0,)), ((), ())), preferred_element_type=F32)


def rms(values, gain):
    return values * lax.rsqrt(jnp.mean(values * values, axis=1, keepdims=True) + EPSILON) * gain


def tie(value, *after):
    return lax.optimization_barrier((value, after))[0]


class Steps:
    def __init__(self):
        self.last = ()

    def wait(self, *values):
        self.last = (self.last, values)

    def __call__(self, fn, *args):
        traced, static = [], []
        for arg in args:
            leaves = jax.tree.leaves(arg)
            static.append(not leaves or not all(hasattr(leaf, "dtype") for leaf in leaves))
            if not static[-1]:
                traced.append(arg)
        traced = iter(tie(tuple(traced), self.last))
        result = fn(*(arg if fixed else next(traced) for arg, fixed in zip(args, static)))
        self.last = result
        return result


def sum_over(values, axis, hop):
    partners = [(index, index ^ hop) for index in range(lax.axis_size(axis))]
    return (values.astype(F32) + lax.ppermute(values, axis, partners).astype(F32)).astype(BF16)


def shards(
    hidden_in,
    attn_gain,
    query_weight,
    key_weight,
    value_weight,
    conv_weight,
    beta_weight,
    out_gain,
    out_weight,
    ffn_gain,
    gate_weight,
    up_weight,
    down_weight,
    cotangent,
    segment_ids,
):
    count = lax.axis_size("shard")
    places = place_scalars()
    core, cx = places[0], places[1]
    micro, local, size, width = hidden_in.shape
    seqs = micro * local
    own_rows = seqs * size
    heads_tp = conv_weight.shape[2]
    heads = heads_tp // 2
    scale = LANES ** (-0.5)
    first_rows, other_rows = slice(0, own_rows), slice(own_rows, 2 * own_rows)

    def gathered(piece):
        return lax.all_gather(piece, "shard", axis=0, tiled=True)

    def over_shard(total):
        return lax.psum_scatter(total, "shard", scatter_dimension=0, tiled=True)

    def across(part):
        return lax.ppermute(part, "cx", SWAP)

    def to_core(part):
        return lax.ppermute(part, "core", SWAP)

    def with_core(part):
        return jnp.concatenate([part, to_core(part)])

    pack = pack_heads(places, query_weight, key_weight, value_weight, heads)
    joint_own = gathered(pack)

    small = jnp.concatenate(
        [
            attn_gain,
            ffn_gain,
            out_gain,
            conv_weight.reshape(-1),
            beta_weight.reshape(-1),
        ]
    )
    unpadded = small.size
    small = jnp.pad(small, (0, -unpadded % (16 * LANES))).reshape(-1, LANES)
    small = lax.all_gather(small, "shard", axis=0).reshape(count, -1)
    piece_d = attn_gain.shape[0]
    entry = out_gain.shape[0]
    at = 2 * piece_d + entry
    gain_in = small[:, :piece_d].reshape(1, -1).astype(F32)
    gain_ffn = small[:, piece_d : 2 * piece_d].reshape(1, -1).astype(F32)
    gain_head = small[:, 2 * piece_d : at].reshape(1, LANES).astype(F32)
    conv_size = conv_weight.size
    taps = small[:, at : at + conv_size].reshape(count, 4, 3, heads_tp, entry)
    taps = taps.transpose(2, 3, 1, 0, 4).reshape(3, heads_tp, 4, LANES)
    taps = lax.dynamic_slice_in_dim(taps, core * heads, heads, axis=1).astype(F32)
    beta = small[:, at + conv_size : unpadded].reshape(width, heads_tp)
    beta = lax.dynamic_slice_in_dim(beta, core * heads, heads, axis=1)
    beta = jnp.pad(beta, ((0, 0), (0, LANES - heads)))

    hidden_own = hidden_in.reshape(own_rows, width)
    hidden_other = to_core(hidden_own)
    ids_own = segment_ids.reshape(seqs, size)
    ids_other = to_core(ids_own)
    late = jnp.where(core == 1, hidden_own, hidden_other).reshape(seqs, size, width)[:, size - HALO :]
    early_ids = jnp.where(core == 0, ids_own, ids_other)
    late_ids = jnp.where(core == 1, ids_own, ids_other)
    halo = lax.ppermute(late, "cx", [(0, 1)]).reshape(seqs * HALO, width)
    halo_ids = lax.ppermute(late_ids[:, size - HALO :], "cx", [(0, 1)])
    halo_ids = jnp.where(cx == 0, -1, halo_ids)
    ids = jnp.concatenate([halo_ids, early_ids, late_ids], axis=1)[..., None]
    id_rows = jnp.stack([early_ids, late_ids], axis=1)
    hidden_all = jnp.concatenate([hidden_own, hidden_other, halo])
    normed_low = rms(hidden_all.astype(F32), gain_in).astype(BF16)
    rates = sigmoid(dot_nn(normed_low, beta))
    grad_own = cotangent.reshape(own_rows, width)
    grad_near = with_core(grad_own)
    grad_far = with_core(across(grad_own))

    outer_own = gathered(tie(own_heads(places, out_weight).T, pack))
    gates = gathered(tie(own_units(places, gate_weight, 1), pack, hidden_all))
    ups = gathered(tie(own_units(places, up_weight, 1), normed_low, rates))
    downs = gathered(tie(own_units(places, down_weight, 0).T, grad_near, grad_far))
    joint_other = across(tie(joint_own, grad_far, ids, id_rows, normed_low))

    steps = Steps()
    shapes = (rates, ids, id_rows, taps, gain_head, seqs, size, scale)
    own_calls = mixer_calls(places, True, *shapes)
    other_calls = mixer_calls(places, False, *shapes)

    def project(rows, weight):
        return dot_nn(rows, weight).astype(BF16)

    raw_own = steps(project, normed_low, joint_own)
    first_own = steps(own_calls[0], raw_own)
    outer_other = across(tie(outer_own, joint_other, first_own[-1]))
    raw_other = steps(project, normed_low, joint_other)
    first_other = steps(other_calls[0], raw_other)
    in_other = lax.ppermute(first_own[-1], "cx", [(0, 1)])
    in_own = lax.ppermute(first_other[-1], "cx", [(0, 1)])
    head_other, mixed_other, fresh_other, middle_other = steps(
        other_calls[1], *first_other[:4], in_other
    )
    head_own, mixed_own, fresh_own, middle_own = steps(own_calls[1], *first_own[:4], in_own)
    slots = head_own.shape
    head_own, head_other = (part.reshape(2 * own_rows, -1) for part in (head_own, head_other))

    def products(block, lefts, rights, add=None, out=BF16):
        return rows_products(list(zip(lefts, rights)), own_rows, block, add, out)

    def away(*pairs):
        lefts, rights = zip(*pairs)
        return to_core(steps(lambda *args: products(1, *args), lefts, rights))

    def here(arrived, *pairs, out=BF16):
        lefts, rights = zip(*pairs)
        return steps(lambda *args: products(0, *args, out), lefts, rights, arrived)

    def with_tp(part):
        return part, lax.ppermute(part, "tp", SWAP)

    def pair_sum(pair):
        return pair[0].astype(F32) + pair[1].astype(F32)

    pairs = ((head_own, outer_own), (head_other, outer_other))
    mixer_pair = with_tp(here(away(*pairs), *pairs))
    hidden_f32 = hidden_own.astype(F32)

    def resid_step(pair, hidden):
        resid = hidden + pair_sum(pair)
        return resid, rms(resid, gain_ffn).astype(BF16)

    steps.wait(ups)
    resid, ffn_own = steps(resid_step, mixer_pair, hidden_f32)
    ffn_far_own = across(ffn_own)
    ffn_near = with_core(ffn_own)

    weights = (gates, ups, downs)
    act_near, d_gate_near, d_up_near = steps(feed_forward, ffn_near, grad_near, *weights)
    near = ((d_gate_near, gates), (d_up_near, ups))
    near_arrived = away(*near)
    down_near_arrived = away((act_near, downs))
    ffn_far = with_core(tie(ffn_far_own, down_near_arrived))
    act_far, d_gate_far, d_up_far = steps(feed_forward, ffn_far, grad_far, *weights)
    far = ((d_gate_far, gates), (d_up_far, ups))

    def both_grads(near, far, grads_near, grads_far):
        rows = near.shape[0]
        return token_products([(near, grads_near, rows, 0), (far, grads_far, rows, 0)])

    d_ffn_sent = across(here(away(*far), *far))
    grad_down = over_shard(steps(both_grads, grad_near, grad_far, act_near, act_far))
    d_ffn_near = here(near_arrived, *near, out=F32)
    down_far_arrived = away((act_far, downs))
    grad_gate = over_shard(steps(both_grads, ffn_near, ffn_far, d_gate_near, d_gate_far))

    def add_far(near, arrived):
        return (near + arrived.astype(F32)).astype(BF16)

    d_ffn_pair = with_tp(steps(add_far, d_ffn_near, d_ffn_sent))
    grad_up = over_shard(steps(both_grads, ffn_near, ffn_far, d_up_near, d_up_far))
    down_sent = across(here(down_far_arrived, (act_far, downs)))
    down_near = here(down_near_arrived, (act_near, downs), out=F32)

    def resid_back(pair, resid, grads):
        _, pull = jax.vjp(rms, resid, gain_ffn)
        d_resid, sum_ffn_gain = pull(pair_sum(pair))
        d_resid = grads.astype(F32) + d_resid
        return d_resid, sum_ffn_gain, d_resid.astype(BF16)

    d_resid, sum_ffn_gain, resid_own = steps(resid_back, d_ffn_pair, resid, grad_own)
    resid_other = to_core(resid_own)
    resid_low = steps(lambda own, other: jnp.concatenate([own, other]), resid_own, resid_other)

    def grad_of(rows, grads, *arrived):
        return token_products([(rows, grads, 2 * own_rows, 0)], *arrived)

    d_head_own = steps(project, resid_low, outer_own).reshape(slots)
    d_head_other = steps(project, resid_low, outer_other).reshape(slots)
    third_own = steps(own_calls[2], d_head_own, mixed_own, *first_own[:2], first_own[3])
    d_final_other = lax.ppermute(third_own[1], "cx", [(1, 0)])
    third_other = steps(other_calls[2], d_head_other, mixed_other, *first_other[:2], first_other[3])
    d_final_own = lax.ppermute(third_other[1], "cx", [(1, 0)])
    outer_sent = across(steps(grad_of, resid_low, head_other))
    down_pair = with_tp(steps(add_far, down_near, down_sent))
    steps.wait(d_final_own, d_final_other)
    fourth_other = steps(
        other_calls[3],
        raw_other,
        *first_other[:4],
        fresh_other,
        third_other[0],
        in_other,
        middle_other,
        d_final_other,
    )
    edge_own = lax.ppermute(fourth_other[1], "cx", [(1, 0)])
    normed_rows = normed_low[: 2 * own_rows]

    def joint_grad(half, d_raw, d_edge, *arrived):
        lanes = slice(half * 3 * LANES, (half + 1) * 3 * LANES)
        d_raw = d_raw.reshape(2 * own_rows, -1)[:, lanes]
        d_edge = d_edge.reshape(seqs * HALO, -1)[:, lanes]
        pairs = [(normed_low, d_raw, 2 * own_rows, 0)]
        pairs += [(normed_low, d_edge, seqs * HALO, 2 * own_rows // (seqs * HALO))]
        return token_products(pairs, *arrived)

    joint_dots = [
        steps(functools.partial(joint_grad, half), *fourth_other[:2]) for half in range(2)
    ]
    joint_sent = [across(joint_dots[0])]
    steps.wait(outer_sent)
    fourth_own = steps(
        own_calls[3],
        raw_own,
        *first_own[:4],
        fresh_own,
        third_own[0],
        in_own,
        middle_own,
        d_final_own,
    )
    edge_other = lax.ppermute(fourth_own[1], "cx", [(1, 0)])
    joint_sent.append(across(tie(joint_dots[1], edge_other)))
    grad_outer = over_shard(steps(grad_of, resid_low, head_own, outer_sent))
    grad_joint = [
        over_shard(steps(functools.partial(joint_grad, 0), *fourth_own[:2], joint_sent[0]))
    ]

    def with_edge(d_raw, d_edge):
        window = (1 - core, 0, size - HALO, 0)
        edge_rows = lax.dynamic_slice(d_raw, window, (1,) + d_edge.shape)
        return lax.dynamic_update_slice(
            d_raw, (edge_rows.astype(F32) + d_edge.astype(F32)[None]).astype(BF16), window
        ).reshape(2 * own_rows, -1)

    def logit_step(rates, rows):
        d_rates = sum(rates)
        d_logit = jnp.where(core == 0, d_rates, d_rates[:, ::-1]).transpose(1, 0, 2, 3)
        d_logit = d_logit.reshape(2 * own_rows, LANES).astype(BF16)
        return d_logit, dot_tn(rows, d_logit)[:, :heads]

    d_logit, sum_rate = steps(logit_step, [fourth_own[2], fourth_other[2]], normed_rows)
    d_raw_own = steps(with_edge, fourth_own[0], edge_own)
    d_raw_other = steps(with_edge, fourth_other[0], edge_other)

    pairs = ((d_raw_own, joint_own), (d_raw_other, joint_other), (d_logit, beta))
    d_normed_pair = with_tp(here(away(*pairs), *pairs))
    grad_joint.append(
        over_shard(steps(functools.partial(joint_grad, 1), *fourth_own[:2], joint_sent[1]))
    )
    sum_head_gain = sum(
        jnp.sum(third[2][:, :, 0, :], axis=(0, 1)) for third in (third_own, third_other)
    )
    sum_head_gain = sum_over(sum_head_gain.astype(BF16), "tp", 1).astype(F32)

    out_down = steps(lambda pieces: lay_units_turned(places, pieces), pieces_of(grad_down, d_normed_pair[0]))
    out_gate = steps(lambda pieces: lay_units(places, pieces), pieces_of(grad_gate, d_normed_pair[0]))
    out_up = steps(lambda pieces: lay_units(places, pieces), pieces_of(grad_up, d_normed_pair[0]))

    def input_back(pair, d_resid, hidden):
        _, pull = jax.vjp(rms, hidden, gain_in)
        d_hidden, sum_attn_gain = pull(pair_sum(pair))
        return sum_attn_gain, (d_resid + d_hidden).astype(BF16)

    sum_attn_gain, input_rows = steps(input_back, d_normed_pair, d_resid, hidden_f32)
    result_rows = steps(
        lambda pair, resid: (resid + pair_sum(pair)).astype(BF16), down_pair, resid
    )
    out_outer = steps(lambda pieces: lay_heads_turned(places, pieces), pieces_of(grad_outer))

    sum_taps = [jnp.sum(fourth[3], axis=0).transpose(2, 0, 1, 3) for fourth in (fourth_own, fourth_other)]
    sum_taps = jnp.where(
        cx == 0, jnp.concatenate(sum_taps, axis=2), jnp.concatenate(sum_taps[::-1], axis=2)
    )
    gains = jnp.concatenate([sum_attn_gain[0], sum_ffn_gain[0], sum_head_gain]).astype(BF16)
    gains = sum_over(gains, "core", 1)
    packed = jnp.concatenate(
        [gains, sum_taps.reshape(-1).astype(BF16), sum_rate.reshape(-1).astype(BF16)]
    )
    packed = sum_over(packed, "cx", 1)
    hop = 1
    while hop < count:
        packed = sum_over(packed, "shard", hop)
        hop *= 2
    own = lax.axis_index("shard")
    ends = [width, 2 * width, 2 * width + LANES, 2 * width + LANES + sum_taps.size]
    grad_attn_gain = lax.dynamic_slice_in_dim(packed[: ends[0]], own * piece_d, piece_d)
    grad_ffn_gain = lax.dynamic_slice_in_dim(packed[ends[0] : ends[1]], own * piece_d, piece_d)
    grad_out_gain = lax.dynamic_slice_in_dim(packed[ends[1] : ends[2]], own * entry, entry)
    own_conv = lax.dynamic_slice_in_dim(
        packed[ends[2] : ends[3]].reshape(4, 3, heads, LANES), own * entry, entry, axis=3
    )
    own_beta = lax.dynamic_slice_in_dim(
        packed[ends[3] :].reshape(width, heads), own * piece_d, piece_d, axis=0
    )

    def both_cores(values, axis):
        other = to_core(values)
        return jnp.where(
            core == 0,
            jnp.concatenate([values, other], axis=axis),
            jnp.concatenate([other, values], axis=axis),
        ).astype(F32)

    out_query, out_key, out_value = lay_heads(places, [pieces_of(part) for part in grad_joint])
    return (
        result_rows.reshape(hidden_in.shape),
        input_rows.reshape(hidden_in.shape),
        grad_attn_gain.astype(F32),
        out_query,
        out_key,
        out_value,
        both_cores(own_conv, 2),
        both_cores(own_beta, 1),
        grad_out_gain.astype(F32),
        out_outer,
        grad_ffn_gain.astype(F32),
        out_gate,
        out_up,
        out_down,
    )


def solution(mesh):
    shard, ctx, tp = (mesh.shape[name] for name in ("shard", "ctx", "tp"))
    cores = Mesh(
        mesh.devices.reshape(shard, ctx // 2, 2, tp), ("shard", "cx", "core", "tp")
    )
    tokens = P(None, "shard", ("cx", "core"), None)
    outer = P("shard", "tp")
    turned = P("tp", "shard")
    conv = P(None, None, "tp", "shard")
    split = P("shard")
    return jax.shard_map(
        shards,
        mesh=cores,
        in_specs=(
            tokens,
            split,
            outer,
            outer,
            outer,
            conv,
            outer,
            split,
            turned,
            split,
            outer,
            outer,
            turned,
            tokens,
            P(None, "shard", ("cx", "core")),
        ),
        out_specs=(
            tokens,
            tokens,
            split,
            outer,
            outer,
            outer,
            conv,
            outer,
            split,
            turned,
            split,
            outer,
            outer,
            turned,
        ),
        check_vma=False,
    )
```

```python
import functools

import jax
import jax.numpy as jnp
from jax import lax
from jax.experimental import pallas as pl
from jax.experimental.pallas import tpu as pltpu
from jax.sharding import Mesh
from jax.sharding import PartitionSpec as P

EPSILON = 1e-06
F32 = jnp.float32
BF16 = jnp.bfloat16
LANES = 128
HALO = 16
SWAP = [(0, 1), (1, 0)]
LONG = 6 * 10**10


def mm(left, right, left_dim, right_dim):
    return lax.dot_general(
        left.astype(BF16),
        right.astype(BF16),
        (((left_dim,), (right_dim,)), ((), ())),
        preferred_element_type=F32,
    )


def nn(left, right):
    return mm(left, right, 1, 0)


def nt(left, right):
    return mm(left, right, 1, 1)


def tn(left, right):
    return mm(left, right, 0, 0)


def place_scalars():
    return jnp.stack([lax.axis_index("core"), lax.axis_index("cx")]).astype(jnp.int32)


def call(kernel, grid, in_specs, out_specs, out_shape, scratch=(), flops=1000):
    return pl.pallas_call(
        kernel,
        grid_spec=pltpu.PrefetchScalarGridSpec(
            num_scalar_prefetch=1,
            grid=grid,
            in_specs=in_specs,
            out_specs=out_specs,
            scratch_shapes=list(scratch),
        ),
        out_shape=out_shape,
        compiler_params=pltpu.CompilerParams(
            dimension_semantics=("arbitrary",) * len(grid), vmem_limit_bytes=48 << 20
        ),
        cost_estimate=pl.CostEstimate(flops=flops, transcendentals=0, bytes_accessed=1000),
    )


def pack_heads(places, query, key, value, heads):
    rows = query.shape[0]

    def kernel(where, query_ref, key_ref, value_ref, out):
        out[:, :LANES] = query_ref[...]
        out[:, LANES : 2 * LANES] = key_ref[...]
        out[:, 2 * LANES :] = value_ref[...]

    spec = pl.BlockSpec((rows, LANES), lambda h, w: (0, w[0] * heads + 2 * w[1] + h))
    return call(
        kernel,
        (2,),
        [spec] * 3,
        pl.BlockSpec((rows, 3 * LANES), lambda h, w: (0, h)),
        jax.ShapeDtypeStruct((rows, 6 * LANES), query.dtype),
    )(places, query, key, value)


def own_parts(units):
    wide = units // 2
    main = wide // (2 * LANES) * LANES
    return wide, main, wide - 2 * main


def own_units(places, weight, axis):
    wide, main, rest = own_parts(weight.shape[axis])
    first = lax.dynamic_slice_in_dim(weight, places[0] * wide + places[1] * main, main, axis)
    last = lax.dynamic_slice_in_dim(weight, places[0] * wide + 2 * main, rest, axis)
    low, high = jnp.split(last, 2, axis)
    return jnp.concatenate([first, jnp.where(places[1] == 0, low, high)], axis)


def own_heads(places, weight):
    rows = weight.shape[0] // 4
    return lax.dynamic_slice_in_dim(weight, (2 * places[0] + places[1]) * rows, rows, 0)


def pieces_of(own, *after):
    across = lax.ppermute(own, "cx", SWAP)
    late = tie(across, after)
    return [own, across, lax.ppermute(own, "core", SWAP), lax.ppermute(late, "core", SWAP)]


def pick(where, core, cx, refs, store):
    which = 2 * jnp.bitwise_xor(where[0], core) + jnp.bitwise_xor(where[1], cx)
    for index in range(4):

        @pl.when(which == index)
        def _():
            store(refs[index][...].astype(F32))


def lay_heads(places, heads):
    rows = heads[0][0].shape[0]

    def kernel(where, *refs):
        outs = refs[-3:]
        for head in range(2):

            def store(values):
                for index in range(3):
                    outs[index][:, head * LANES : (head + 1) * LANES] = values[
                        :, index * LANES : (index + 1) * LANES
                    ]

            pick(where, pl.program_id(0), pl.program_id(1), refs[4 * head : 4 * head + 4], store)

    return call(
        kernel,
        (2, 2),
        [pl.BlockSpec(heads[0][0].shape, lambda i, j, w: (0, 0))] * 8,
        [pl.BlockSpec((rows, 2 * LANES), lambda i, j, w: (0, 2 * i + j))] * 3,
        [jax.ShapeDtypeStruct((rows, 8 * LANES), F32)] * 3,
    )(places, *heads[0], *heads[1])


def lay_units(places, pieces, turn, flops=1000):
    units, rows = pieces[0].shape
    wide, main, rest = own_parts(4 * units)
    half = rest // 2

    def kernel(where, a, b, c, d, out):
        for side in range(2):

            def store(values):
                at = 2 * main + side * half
                if turn:
                    values = values.T
                    out[:, side * main : (side + 1) * main] = values[:, :main]
                    out[:, at : at + half] = values[:, main:]
                else:
                    out[side * main : (side + 1) * main, :] = values[:main]
                    out[at : at + half, :] = values[main:]

            pick(where, pl.program_id(0), side, (a, b, c, d), store)

    shape = (rows, wide) if turn else (wide, rows)
    return call(
        kernel,
        (2,),
        [pl.BlockSpec((units, rows), lambda i, w: (0, 0))] * 4,
        pl.BlockSpec(shape, (lambda i, w: (0, i)) if turn else (lambda i, w: (i, 0))),
        jax.ShapeDtypeStruct((rows, 2 * wide) if turn else (2 * wide, rows), F32),
        flops=flops,
    )(places, *pieces)


def lay_heads_turned(places, pieces):
    rows, columns = pieces[0].shape

    def kernel(where, a, b, c, d, out):
        def store(values):
            out[...] = values.T

        pick(where, pl.program_id(0), pl.program_id(1), (a, b, c, d), store)

    return call(
        kernel,
        (2, 2),
        [pl.BlockSpec((rows, columns), lambda i, j, w: (0, 0))] * 4,
        pl.BlockSpec((columns, rows), lambda i, j, w: (2 * i + j, 0)),
        jax.ShapeDtypeStruct((4 * columns, rows), F32),
    )(places, *pieces)


def fill_ext(ext, index, halo, first, second, size):
    ext[index, :HALO, :] = halo[...].astype(F32)
    ext[index, HALO : HALO + size, :] = first[...].astype(F32)
    ext[index, HALO + size :, :] = second[...].astype(F32)


def links_of(ids, total):
    own = ids[0, HALO : HALO + total, :]
    return [
        (ids[0, HALO - 3 + tap : HALO - 3 + tap + total, :] == own).astype(F32) for tap in range(4)
    ]


def conv_of(ext, index, taps, links, total):
    result = None
    for tap in range(4):
        term = (
            taps[index, 0, tap : tap + 1, :]
            * ext[index, HALO - 3 + tap : HALO - 3 + tap + total, :]
            * links[tap]
        )
        result = term if result is None else result + term
    return result


def sigmoid(values):
    return 1.0 / (1.0 + jnp.exp(-values))


def first_head(where, own):
    return 2 * (where[1] if own else 1 - where[1])


def head_of(where, own):
    return first_head(where, own) + pl.program_id(1)


def column_of(values, head):
    lane = lax.broadcasted_iota(jnp.int32, values.shape, 1)
    return jnp.sum(jnp.where(lane == head, values, 0.0), axis=1, keepdims=True)


def marks(ids, rows, chunk, size):
    start = HALO + chunk * size
    column = ids[0, start : start + size, :]
    before = ids[0, start - 1 : start, :]
    last = ids[0, start + size - 1 : start + size, :]
    first = (column == before).astype(F32)
    tail = (column == last).astype(F32)
    whole = (last == before).astype(F32)
    same = column == rows[0, chunk : chunk + 1, :]
    row = lax.broadcasted_iota(jnp.int32, (size, size), 0)
    col = lax.broadcasted_iota(jnp.int32, (size, size), 1)
    return first, tail, whole, same & (row > col), same & (row >= col)


def inverse_units(stricts, size):
    row = lax.broadcasted_iota(jnp.int32, (size, size), 0)
    col = lax.broadcasted_iota(jnp.int32, (size, size), 1)
    mixed = jnp.bitwise_xor(row, col)
    results = [
        jnp.where(row == col, 1.0, jnp.where(mixed == 1, -strict, 0.0)) for strict in stricts
    ]
    stricts = [strict.astype(BF16) for strict in stricts]
    block = 2
    while block < size:
        pair = (mixed >= block) & (mixed < 2 * block)
        lows = [result.astype(BF16) for result in results]
        parts = [jnp.where(pair, strict, 0.0) for strict in stricts]
        steps = [nn(part, low).astype(BF16) for part, low in zip(parts, lows)]
        results = [
            result - nn(low, step) for result, low, step in zip(results, lows, steps)
        ]
        block *= 2
    return [result.astype(BF16) for result in results]


def forward_one(where, q0, k0, v0, q1, k1, v1, qh, kh, vh, taps, ids, rows, r0, r1, *rest, size, own):
    query, key, value, inverse, final, ext = rest
    head = head_of(where, own)
    total = 2 * size
    for index, group in enumerate(((qh, q0, q1), (kh, k0, k1), (vh, v0, v1))):
        fill_ext(ext, index, *group, size)
    links = links_of(ids, total)
    out = []
    for index in range(3):
        conv = conv_of(ext, index, taps, links, total)
        act = conv * sigmoid(conv)
        if index < 2:
            act = act * lax.rsqrt(jnp.sum(act * act, axis=1, keepdims=True) + EPSILON)
        out.append(act.astype(BF16))
    for target, values in zip((query, key, value), out):
        target[0, 0] = values[:size]
        target[0, 1] = values[size:]
    chunks = []
    for chunk, rates in enumerate((r0, r1)):
        first, tail, whole, strict, _ = marks(ids, rows, chunk, size)
        rate = column_of(rates[...], head)
        keys = out[1][chunk * size : (chunk + 1) * size]
        chunks.append((first, tail, whole, rate, keys, jnp.where(strict, rate * nt(keys, keys), 0.0)))
    inverses = inverse_units([item[-1] for item in chunks], size)
    state = None
    for chunk, (first, tail, whole, rate, keys, _) in enumerate(chunks):
        fresh = out[2][chunk * size : (chunk + 1) * size].astype(F32)
        inverse[0, 0, chunk] = inverses[chunk]
        if chunk:
            fresh = fresh - first * nt(keys, state)
        fresh = nn(inverses[chunk], rate * fresh)
        added = tn(tail * fresh, keys)
        state = added if state is None else whole * state + added
    final[0, 0] = state.astype(BF16)


def forward_two(where, query, key, value, inverse, ids, rows, r0, r1, incoming, gain, *rest, size, scale, own):
    head_low, mixed_out, fresh_out, middle = rest
    head = head_of(where, own)
    state = incoming[0, 0].astype(F32)
    for chunk, rates in enumerate((r0, r1)):
        first, tail, whole, _, lower = marks(ids, rows, chunk, size)
        rate = column_of(rates[...], head)
        keys, queries = key[0, chunk], query[0, chunk]
        if chunk:
            middle[0, 0] = state.astype(BF16)
        rest_rows = value[0, chunk].astype(F32) - first * nt(keys, state)
        fresh = nn(inverse[0, 0, chunk], rate * rest_rows)
        fresh_out[0, chunk] = fresh.astype(BF16)
        inner = jnp.where(lower, nt(queries, keys), 0.0)
        mixed = scale * (first * nt(queries, state) + nn(inner, fresh))
        mixed_out[0, chunk] = mixed
        normed = mixed * lax.rsqrt(jnp.mean(mixed * mixed, axis=1, keepdims=True) + EPSILON)
        slot = where[0] if chunk == 0 else 1 - where[0]
        head_low[slot, 0] = (normed * gain[...]).astype(BF16)
        if chunk == 0:
            state = whole * state + tn(tail * fresh, keys)


def backward_one(where, d_head, mixed, query, key, inverse, ids, rows, r0, r1, gain, *rest, size, scale, own):
    d_out, d_state_out, d_gain = rest
    head = head_of(where, own)
    total = jnp.zeros((1, LANES), F32)
    d_state = None
    for chunk in (1, 0):
        first, tail, whole, _, lower = marks(ids, rows, chunk, size)
        rate = column_of((r0, r1)[chunk][...], head)
        keys, queries = key[0, chunk], query[0, chunk]
        slot = where[0] if chunk == 0 else 1 - where[0]
        grad = d_head[slot, 0].astype(F32)
        values = mixed[0, chunk]
        inv_rms = lax.rsqrt(jnp.mean(values * values, axis=1, keepdims=True) + EPSILON)
        normed = values * inv_rms
        total = total + jnp.sum(grad * normed, axis=0, keepdims=True)
        scaled = grad * gain[...]
        d_mixed = inv_rms * (scaled - normed * jnp.mean(scaled * normed, axis=1, keepdims=True))
        d_low = (scale * d_mixed).astype(BF16)
        d_out[0, chunk] = d_low
        inner = jnp.where(lower, nt(queries, keys), 0.0)
        d_fresh = tn(inner, d_low)
        if d_state is not None:
            d_fresh = d_fresh + tail * nt(keys, d_state)
        d_rest = rate * tn(inverse[0, 0, chunk], d_fresh)
        change = tn(first * d_low.astype(F32), queries) - tn(first * d_rest, keys)
        d_state = change if d_state is None else whole * d_state + change
    d_state_out[0, 0] = d_state.astype(BF16)
    d_gain[0, 0] = jnp.broadcast_to(total, (8, LANES))


def backward_two(where, q0, k0, v0, q1, k1, v1, qh, kh, vh, taps, ids, rows, r0, r1, *rest, size, own):
    query, key, value, inverse, fresh_in, d_in, incoming, middle, d_final = rest[:9]
    d_raw, d_edge, d_rates, d_taps = rest[9:13]
    ext, d_ext, d_rows = rest[13:]
    head = head_of(where, own)
    total = 2 * size
    for index, group in enumerate(((qh, q0, q1), (kh, k0, k1), (vh, v0, v1))):
        fill_ext(ext, index, *group, size)
    d_state = d_final[0, 0].astype(F32)

    @pl.when(pl.program_id(1) == 0)
    def _():
        d_rates[...] = jnp.zeros_like(d_rates)

    for chunk in (1, 0):
        first, tail, whole, strict, lower = marks(ids, rows, chunk, size)
        rate = column_of((r0, r1)[chunk][...], head)
        keys, queries, fresh = key[0, chunk], query[0, chunk], fresh_in[0, chunk]
        inv, d_low = inverse[0, 0, chunk], d_in[0, chunk]
        state = (middle if chunk else incoming)[0, 0]
        d_mix = d_low.astype(F32)
        inner = jnp.where(lower, nt(queries, keys), 0.0)
        gram = jnp.where(strict, nt(keys, keys), 0.0)
        d_fresh = tn(inner, d_low) + tail * nt(keys, d_state)
        turned = tn(inv, d_fresh)
        d_rest = rate * turned
        rest_rows = value[0, chunk].astype(F32) - first * nt(keys, state)
        error = rest_rows - nn(gram, fresh)
        d_rate = jnp.sum(turned * error, axis=1, keepdims=True) * rate * (1.0 - rate)
        d_inner = jnp.where(lower, nt(d_low, fresh), 0.0)
        d_gram = rate * jnp.where(strict, -nt(turned, fresh), 0.0)
        d_query = first * nn(d_low, state) + nn(d_inner, keys)
        d_key = (
            tn(d_inner, queries)
            + tail * nn(fresh, d_state)
            - nn(first * d_rest, state)
            + nn(d_gram, keys)
            + tn(d_gram, keys)
        )
        for index, values in enumerate((d_query, d_key, d_rest)):
            d_rows[index, chunk * size : (chunk + 1) * size, :] = values
        lane = lax.broadcasted_iota(jnp.int32, (size, LANES), 1)
        d_rates[0, chunk] = d_rates[0, chunk] + jnp.where(lane == head, d_rate, 0.0)
        if chunk:
            d_state = (
                whole * d_state + tn(first * d_mix, queries) - tn(first * d_rest, keys)
            )
    links = links_of(ids, total)
    for index in range(3):
        conv = conv_of(ext, index, taps, links, total)
        sig = sigmoid(conv)
        d_act = d_rows[index].astype(BF16).astype(F32)
        if index < 2:
            act = conv * sig
            inv_norm = lax.rsqrt(jnp.sum(act * act, axis=1, keepdims=True) + EPSILON)
            unit = act * inv_norm
            d_act = (d_act - unit * jnp.sum(unit * d_act, axis=1, keepdims=True)) * inv_norm
        d_conv = d_act * sig * (1.0 + conv * (1.0 - sig))
        d_ext[...] = jnp.zeros_like(d_ext)
        for tap in range(4):
            window = slice(HALO - 3 + tap, HALO - 3 + tap + total)
            linked = d_conv * links[tap]
            d_taps[0, index, 0, tap : tap + 1, :] = jnp.sum(
                linked * ext[index, window, :], axis=0, keepdims=True
            )
            d_ext[window, :] = d_ext[window, :] + taps[index, 0, tap : tap + 1, :] * linked
        lanes = slice(index * LANES, (index + 1) * LANES)
        d_edge[0, :, lanes] = d_ext[:HALO, :].astype(BF16)
        d_raw[where[0], 0, :, lanes] = d_ext[HALO : HALO + size, :].astype(BF16)
        d_raw[1 - where[0], 0, :, lanes] = d_ext[HALO + size :, :].astype(BF16)


def mixer_calls(places, own, rates, ids, rows, taps, gain, seqs, size, scale):
    def slot_of(chunk, w):
        return w[0] if chunk == 0 else 1 - w[0]

    def raw_spec(chunk, part):
        return pl.BlockSpec(
            (size, LANES), lambda b, h, w: (slot_of(chunk, w) * seqs + b, 3 * h + part)
        )

    def rate_spec(chunk):
        return pl.BlockSpec((size, LANES), lambda b, h, w: (slot_of(chunk, w) * seqs + b, 0))

    halo_base = 2 * seqs * size // HALO

    def halo_spec(part):
        return pl.BlockSpec((HALO, LANES), lambda b, h, w: (halo_base + b, 3 * h + part))

    conv_specs = (
        [raw_spec(c, p) for c in range(2) for p in range(3)]
        + [halo_spec(p) for p in range(3)]
        + [
            pl.BlockSpec((3, 1, 4, LANES), lambda b, h, w: (0, first_head(w, own) + h, 0, 0)),
            pl.BlockSpec((1, HALO + 2 * size, 1), lambda b, h, w: (b, 0, 0)),
            pl.BlockSpec((1, 2, size), lambda b, h, w: (b, 0, 0)),
            rate_spec(0),
            rate_spec(1),
        ]
    )
    rest_args = (taps, ids, rows, rates, rates)
    id_specs, id_args = conv_specs[10:], rest_args[1:]
    act_spec = pl.BlockSpec((1, 2, size, LANES), lambda b, h, w: (b, 0, 0, h))
    act_shape = (seqs, 2, size, 2 * LANES)
    state_spec = pl.BlockSpec((1, 1, LANES, LANES), lambda b, h, w: (b, h, 0, 0))
    state_shape = jax.ShapeDtypeStruct((seqs, 2, LANES, LANES), BF16)
    inv_spec = pl.BlockSpec((1, 1, 2, size, size), lambda b, h, w: (b, h, 0, 0, 0))
    inv_shape = jax.ShapeDtypeStruct((seqs, 2, 2, size, size), BF16)
    slot_spec = pl.BlockSpec((2, 1, size, LANES), lambda b, h, w: (0, b, 0, h))
    slot_shape = jax.ShapeDtypeStruct((2, seqs, size, 2 * LANES), BF16)
    gain_spec = pl.BlockSpec((1, LANES), lambda b, h, w: (0, 0))
    low = jax.ShapeDtypeStruct(act_shape, BF16)
    grid = (seqs, 2)

    def one(raw):
        return call(
            functools.partial(forward_one, size=size, own=own),
            grid,
            conv_specs,
            [act_spec] * 3 + [inv_spec, state_spec],
            [low] * 3 + [inv_shape, state_shape],
            [pltpu.VMEM((3, HALO + 2 * size, LANES), F32)],
        )(places, *(raw,) * 9, *rest_args)

    def two(query, key, value, inverse, incoming):
        args = (query, key, value, inverse, *id_args, incoming, gain)
        return call(
            functools.partial(forward_two, size=size, scale=scale, own=own),
            grid,
            [act_spec] * 3
            + [inv_spec]
            + id_specs
            + [state_spec, gain_spec],
            [slot_spec, act_spec, act_spec, state_spec],
            [slot_shape, jax.ShapeDtypeStruct(act_shape, F32), low, state_shape],
        )(places, *args)

    def three(d_head, mixed, query, key, inverse):
        return call(
            functools.partial(backward_one, size=size, scale=scale, own=own),
            grid,
            [slot_spec, act_spec, act_spec, act_spec, inv_spec] + id_specs + [gain_spec],
            [act_spec, state_spec, pl.BlockSpec((1, 1, 8, LANES), lambda b, h, w: (b, h, 0, 0))],
            [low, state_shape, jax.ShapeDtypeStruct((seqs, 2, 8, LANES), F32)],
            flops=int(26 * 1.1e9),
        )(places, d_head, mixed, query, key, inverse, *id_args, gain)

    def four(raw, query, key, value, inverse, fresh, d_low, incoming, middle, d_final):
        return call(
            functools.partial(backward_two, size=size, own=own),
            grid,
            conv_specs + [act_spec] * 3 + [inv_spec, act_spec, act_spec] + [state_spec] * 3,
            [
                pl.BlockSpec((2, 1, size, 3 * LANES), lambda b, h, w: (0, b, 0, h)),
                pl.BlockSpec((1, HALO, 3 * LANES), lambda b, h, w: (b, 0, h)),
                pl.BlockSpec((1, 2, size, LANES), lambda b, h, w: (b, 0, 0, 0)),
                pl.BlockSpec((1, 3, 1, 4, LANES), lambda b, h, w: (b, 0, h, 0, 0)),
            ],
            [
                jax.ShapeDtypeStruct((2, seqs, size, 6 * LANES), BF16),
                jax.ShapeDtypeStruct((seqs, HALO, 6 * LANES), BF16),
                jax.ShapeDtypeStruct((seqs, 2, size, LANES), F32),
                jax.ShapeDtypeStruct((seqs, 3, 2, 4, LANES), F32),
            ],
            [
                pltpu.VMEM((3, HALO + 2 * size, LANES), F32),
                pltpu.VMEM((HALO + 2 * size, LANES), F32),
                pltpu.VMEM((3, 2 * size, LANES), F32),
            ],
            flops=int(26 * 1.1e9),
        )(
            places,
            *(raw,) * 9,
            *rest_args,
            query,
            key,
            value,
            inverse,
            fresh,
            d_low,
            incoming,
            middle,
            d_final,
        )

    return one, two, three, four


def tile_of(extent):
    return 512 if extent % 512 == 0 else extent


def rows_products(pairs, rows, block, add=None, out=BF16, flops=1000):
    columns = pairs[0][1].shape[0]
    tile = tile_of(columns)
    count = len(pairs)

    def kernel(*refs):
        total = None
        for index in range(count):
            part = nt(refs[index][...], refs[count + index][...])
            total = part if total is None else total + part
        if add is not None:
            total = total + refs[2 * count][...].astype(F32)
        refs[-1][...] = total.astype(out)

    lefts = [pl.BlockSpec((rows, left.shape[1]), lambda i: (block, 0)) for left, _ in pairs]
    rights = [pl.BlockSpec((tile, right.shape[1]), lambda i: (i, 0)) for _, right in pairs]
    spec = pl.BlockSpec((rows, tile), lambda i: (0, i))
    extra = () if add is None else (add,)
    return pl.pallas_call(
        kernel,
        grid=(columns // tile,),
        in_specs=lefts + rights + [spec] * len(extra),
        out_specs=spec,
        out_shape=jax.ShapeDtypeStruct((rows, columns), out),
        compiler_params=pltpu.CompilerParams(vmem_limit_bytes=48 << 20),
        cost_estimate=pl.CostEstimate(flops=flops, transcendentals=0, bytes_accessed=1000),
    )(*(left for left, _ in pairs), *(right for _, right in pairs), *extra)


def token_products(pairs, add=None, flops=1000):
    count = len(pairs)
    height, columns = pairs[0][0].shape[1], pairs[0][1].shape[1]
    tile = tile_of(height)

    def kernel(*refs):
        total = None
        for index in range(count):
            part = tn(refs[index][...], refs[count + index][...])
            total = part if total is None else total + part
        if add is not None:
            total = total + refs[2 * count][...].astype(F32)
        refs[-1][...] = total.astype(BF16)

    lefts = [
        pl.BlockSpec((rows, tile), lambda i, block=block: (block, i))
        for _, _, rows, block in pairs
    ]
    rights = [pl.BlockSpec((rows, columns), lambda i: (0, 0)) for _, _, rows, _ in pairs]
    spec = pl.BlockSpec((tile, columns), lambda i: (i, 0))
    extra = () if add is None else (add,)
    return pl.pallas_call(
        kernel,
        grid=(height // tile,),
        in_specs=lefts + rights + [spec] * len(extra),
        out_specs=spec,
        out_shape=jax.ShapeDtypeStruct((height, columns), BF16),
        compiler_params=pltpu.CompilerParams(vmem_limit_bytes=48 << 20),
        cost_estimate=pl.CostEstimate(flops=flops, transcendentals=0, bytes_accessed=1000),
    )(*(item[0] for item in pairs), *(item[1] for item in pairs), *extra)


def feed_forward(rows, grads, gates, ups, downs):
    tokens, width = rows.shape
    units = gates.shape[1]
    tile = 256 if tokens % 256 == 0 else tokens

    def kernel(rows_ref, grads_ref, gates_ref, ups_ref, downs_ref, act, d_gate, d_up):
        gate = nn(rows_ref[...], gates_ref[...])
        up = nn(rows_ref[...], ups_ref[...])
        d_act = nn(grads_ref[...], downs_ref[...]).astype(BF16).astype(F32)
        sig = sigmoid(gate)
        act[...] = (gate * sig * up).astype(BF16)
        d_gate[...] = (d_act * up * sig * (1.0 + gate * (1.0 - sig))).astype(BF16)
        d_up[...] = (d_act * gate * sig).astype(BF16)

    token_spec = pl.BlockSpec((tile, width), lambda i: (i, 0))
    weight_spec = pl.BlockSpec((width, units), lambda i: (0, 0))
    unit_spec = pl.BlockSpec((tile, units), lambda i: (i, 0))
    return pl.pallas_call(
        kernel,
        grid=(tokens // tile,),
        in_specs=[token_spec] * 2 + [weight_spec] * 3,
        out_specs=[unit_spec] * 3,
        out_shape=[jax.ShapeDtypeStruct((tokens, units), BF16)] * 3,
        compiler_params=pltpu.CompilerParams(vmem_limit_bytes=48 << 20),
        cost_estimate=pl.CostEstimate(flops=1000, transcendentals=0, bytes_accessed=1000),
    )(rows, grads, gates, ups, downs)


def dot_nn(left, right):
    return lax.dot_general(left, right, (((1,), (0,)), ((), ())), preferred_element_type=F32)


def dot_nt(left, right):
    return lax.dot_general(left, right, (((1,), (1,)), ((), ())), preferred_element_type=F32)


def dot_tn(left, right):
    return lax.dot_general(left, right, (((0,), (0,)), ((), ())), preferred_element_type=F32)


def rms(values, gain):
    return values * lax.rsqrt(jnp.mean(values * values, axis=1, keepdims=True) + EPSILON) * gain


def tie(value, *after):
    return lax.optimization_barrier((value, after))[0]


class Steps:
    def __init__(self):
        self.last = ()

    def wait(self, *values):
        self.last = (self.last, values)

    def __call__(self, fn, *args):
        traced, static = [], []
        for arg in args:
            leaves = jax.tree.leaves(arg)
            static.append(not leaves or not all(hasattr(leaf, "dtype") for leaf in leaves))
            if not static[-1]:
                traced.append(arg)
        traced = iter(tie(tuple(traced), self.last))
        result = fn(*(arg if fixed else next(traced) for arg, fixed in zip(args, static)))
        self.last = result
        return result


def sum_over(values, axis, hop):
    partners = [(index, index ^ hop) for index in range(lax.axis_size(axis))]
    return (values.astype(F32) + lax.ppermute(values, axis, partners).astype(F32)).astype(BF16)


def shards(
    hidden_in,
    attn_gain,
    query_weight,
    key_weight,
    value_weight,
    conv_weight,
    beta_weight,
    out_gain,
    out_weight,
    ffn_gain,
    gate_weight,
    up_weight,
    down_weight,
    cotangent,
    segment_ids,
):
    count = lax.axis_size("shard")
    places = place_scalars()
    core, cx = places[0], places[1]
    micro, local, size, width = hidden_in.shape
    seqs = micro * local
    own_rows = seqs * size
    heads_tp = conv_weight.shape[2]
    heads = heads_tp // 2
    scale = LANES ** (-0.5)
    first_rows, other_rows = slice(0, own_rows), slice(own_rows, 2 * own_rows)

    def gathered(piece):
        return lax.all_gather(piece, "shard", axis=0, tiled=True)

    def over_shard(total):
        return lax.psum_scatter(total, "shard", scatter_dimension=0, tiled=True)

    def across(part):
        return lax.ppermute(part, "cx", SWAP)

    def to_core(part):
        return lax.ppermute(part, "core", SWAP)

    def with_core(part):
        return jnp.concatenate([part, to_core(part)])

    pack = pack_heads(places, query_weight, key_weight, value_weight, heads)
    joint_own = gathered(pack)

    small = jnp.concatenate(
        [
            attn_gain,
            ffn_gain,
            out_gain,
            conv_weight.reshape(-1),
            beta_weight.reshape(-1),
        ]
    )
    unpadded = small.size
    small = jnp.pad(small, (0, -unpadded % (16 * LANES))).reshape(-1, LANES)
    small = lax.all_gather(small, "shard", axis=0).reshape(count, -1)
    piece_d = attn_gain.shape[0]
    entry = out_gain.shape[0]
    at = 2 * piece_d + entry
    gain_in = small[:, :piece_d].reshape(1, -1).astype(F32)
    gain_ffn = small[:, piece_d : 2 * piece_d].reshape(1, -1).astype(F32)
    gain_head = small[:, 2 * piece_d : at].reshape(1, LANES).astype(F32)
    conv_size = conv_weight.size
    taps = small[:, at : at + conv_size].reshape(count, 4, 3, heads_tp, entry)
    taps = taps.transpose(2, 3, 1, 0, 4).reshape(3, heads_tp, 4, LANES)
    taps = lax.dynamic_slice_in_dim(taps, core * heads, heads, axis=1).astype(F32)
    beta = small[:, at + conv_size : unpadded].reshape(width, heads_tp)
    beta = lax.dynamic_slice_in_dim(beta, core * heads, heads, axis=1)
    beta = jnp.pad(beta, ((0, 0), (0, LANES - heads)))

    hidden_own = hidden_in.reshape(own_rows, width)
    hidden_other = to_core(hidden_own)
    ids_own = segment_ids.reshape(seqs, size)
    ids_other = to_core(ids_own)
    late = jnp.where(core == 1, hidden_own, hidden_other).reshape(seqs, size, width)[:, size - HALO :]
    early_ids = jnp.where(core == 0, ids_own, ids_other)
    late_ids = jnp.where(core == 1, ids_own, ids_other)
    halo = lax.ppermute(late, "cx", [(0, 1)]).reshape(seqs * HALO, width)
    halo_ids = lax.ppermute(late_ids[:, size - HALO :], "cx", [(0, 1)])
    halo_ids = jnp.where(cx == 0, -1, halo_ids)
    ids = jnp.concatenate([halo_ids, early_ids, late_ids], axis=1)[..., None]
    id_rows = jnp.stack([early_ids, late_ids], axis=1)
    hidden_all = jnp.concatenate([hidden_own, hidden_other, halo])
    normed_low = rms(hidden_all.astype(F32), gain_in).astype(BF16)
    rates = sigmoid(dot_nn(normed_low, beta))
    grad_own = cotangent.reshape(own_rows, width)
    grad_near = with_core(grad_own)
    grad_far = with_core(across(grad_own))

    outer_own = gathered(tie(own_heads(places, out_weight).T, pack))
    gates = gathered(tie(own_units(places, gate_weight, 1), pack, hidden_all))
    ups = gathered(tie(own_units(places, up_weight, 1), normed_low, rates))
    downs = gathered(tie(own_units(places, down_weight, 0).T, grad_near, grad_far))
    joint_other = across(tie(joint_own, grad_far, ids, id_rows, normed_low))

    steps = Steps()
    shapes = (rates, ids, id_rows, taps, gain_head, seqs, size, scale)
    own_calls = mixer_calls(places, True, *shapes)
    other_calls = mixer_calls(places, False, *shapes)

    def project(rows, weight):
        return dot_nn(rows, weight).astype(BF16)

    raw_own = steps(project, normed_low, joint_own)
    first_own = steps(own_calls[0], raw_own)
    outer_other = across(tie(outer_own, joint_other, first_own[-1]))
    raw_other = steps(project, normed_low, joint_other)
    first_other = steps(other_calls[0], raw_other)
    in_other = lax.ppermute(first_own[-1], "cx", [(0, 1)])
    in_own = lax.ppermute(first_other[-1], "cx", [(0, 1)])
    head_other, mixed_other, fresh_other, middle_other = steps(
        other_calls[1], *first_other[:4], in_other
    )
    head_own, mixed_own, fresh_own, middle_own = steps(own_calls[1], *first_own[:4], in_own)
    slots = head_own.shape
    head_own, head_other = (part.reshape(2 * own_rows, -1) for part in (head_own, head_other))

    def products(block, lefts, rights, add=None, out=BF16, flops=1000):
        return rows_products(list(zip(lefts, rights)), own_rows, block, add, out, flops)

    def away(*pairs, flops=1000):
        lefts, rights = zip(*pairs)
        return to_core(steps(lambda *args: products(1, *args, flops=flops), lefts, rights))

    def here(arrived, *pairs, out=BF16):
        lefts, rights = zip(*pairs)
        return steps(lambda *args: products(0, *args, out), lefts, rights, arrived)

    def with_tp(part):
        return part, lax.ppermute(part, "tp", SWAP)

    def pair_sum(pair):
        return pair[0].astype(F32) + pair[1].astype(F32)

    pairs = ((head_own, outer_own), (head_other, outer_other))
    mixer_pair = with_tp(here(away(*pairs), *pairs))
    hidden_f32 = hidden_own.astype(F32)

    def resid_step(pair, hidden):
        resid = hidden + pair_sum(pair)
        return resid, rms(resid, gain_ffn).astype(BF16)

    steps.wait(ups)
    resid, ffn_own = steps(resid_step, mixer_pair, hidden_f32)
    ffn_far_own = across(ffn_own)
    ffn_near = with_core(ffn_own)

    weights = (gates, ups, downs)
    act_near, d_gate_near, d_up_near = steps(feed_forward, ffn_near, grad_near, *weights)
    near = ((d_gate_near, gates), (d_up_near, ups))
    near_arrived = away(*near)
    down_near_arrived = away((act_near, downs))
    ffn_far = with_core(tie(ffn_far_own, down_near_arrived))
    act_far, d_gate_far, d_up_far = steps(feed_forward, ffn_far, grad_far, *weights)
    far = ((d_gate_far, gates), (d_up_far, ups))

    def both_grads(near, far, grads_near, grads_far):
        rows = near.shape[0]
        return token_products([(near, grads_near, rows, 0), (far, grads_far, rows, 0)])

    d_ffn_sent = across(here(away(*far), *far))
    grad_down = over_shard(steps(both_grads, grad_near, grad_far, act_near, act_far))
    d_ffn_near = here(near_arrived, *near, out=F32)
    down_far_arrived = away((act_far, downs))
    grad_gate = over_shard(steps(both_grads, ffn_near, ffn_far, d_gate_near, d_gate_far))

    def add_far(near, arrived):
        return (near + arrived.astype(F32)).astype(BF16)

    d_ffn_pair = with_tp(steps(add_far, d_ffn_near, d_ffn_sent))
    grad_up = over_shard(steps(both_grads, ffn_near, ffn_far, d_up_near, d_up_far))
    down_sent = across(here(down_far_arrived, (act_far, downs)))
    down_near = here(down_near_arrived, (act_near, downs), out=F32)

    def resid_back(pair, resid, grads):
        _, pull = jax.vjp(rms, resid, gain_ffn)
        d_resid, sum_ffn_gain = pull(pair_sum(pair))
        d_resid = grads.astype(F32) + d_resid
        return d_resid, sum_ffn_gain, d_resid.astype(BF16)

    d_resid, sum_ffn_gain, resid_own = steps(resid_back, d_ffn_pair, resid, grad_own)
    resid_other = to_core(resid_own)
    resid_low = steps(lambda own, other: jnp.concatenate([own, other]), resid_own, resid_other)

    def grad_of(rows, grads, *arrived, flops=1000):
        return token_products([(rows, grads, 2 * own_rows, 0)], *arrived, flops=flops)

    d_head_own = steps(project, resid_low, outer_own).reshape(slots)
    d_head_other = steps(project, resid_low, outer_other).reshape(slots)
    steps.wait(grad_down)
    third_own = steps(own_calls[2], d_head_own, mixed_own, *first_own[:2], first_own[3])
    d_final_other = lax.ppermute(third_own[1], "cx", [(1, 0)])
    third_other = steps(other_calls[2], d_head_other, mixed_other, *first_other[:2], first_other[3])
    d_final_own = lax.ppermute(third_other[1], "cx", [(1, 0)])
    outer_sent = across(steps(grad_of, resid_low, head_other))
    down_pair = with_tp(steps(add_far, down_near, down_sent))
    sum_head_gain = steps(
        lambda *parts: sum(jnp.sum(part[:, :, 0, :], axis=(0, 1)) for part in parts).astype(BF16),
        third_own[2],
        third_other[2],
    )
    sum_head_gain = sum_over(sum_head_gain, "tp", 1)
    steps.wait(d_final_own, d_final_other, sum_head_gain)
    steps.wait(grad_gate)
    fourth_other = steps(
        other_calls[3],
        raw_other,
        *first_other[:4],
        fresh_other,
        third_other[0],
        in_other,
        middle_other,
        d_final_other,
    )
    edge_own = lax.ppermute(fourth_other[1], "cx", [(1, 0)])
    normed_rows = normed_low[: 2 * own_rows]

    def joint_grad(half, d_raw, d_edge, *arrived, flops=1000):
        lanes = slice(half * 3 * LANES, (half + 1) * 3 * LANES)
        d_raw = d_raw.reshape(2 * own_rows, -1)[:, lanes]
        d_edge = d_edge.reshape(seqs * HALO, -1)[:, lanes]
        pairs = [(normed_low, d_raw, 2 * own_rows, 0)]
        pairs += [(normed_low, d_edge, seqs * HALO, 2 * own_rows // (seqs * HALO))]
        return token_products(pairs, *arrived, flops=flops)

    out_down = steps(
        lambda pieces: lay_units(places, pieces, False, 1000), pieces_of(grad_down.T, fourth_other[1])
    )
    joint_dots = [
        steps(functools.partial(joint_grad, half), *fourth_other[:2]) for half in range(2)
    ]
    joint_sent = [across(joint_dots[0])]
    steps.wait(outer_sent, grad_up)
    fourth_own = steps(
        own_calls[3],
        raw_own,
        *first_own[:4],
        fresh_own,
        third_own[0],
        in_own,
        middle_own,
        d_final_own,
    )
    edge_other = lax.ppermute(fourth_own[1], "cx", [(1, 0)])
    result_rows = steps(
        lambda pair, resid: (resid + pair_sum(pair)).astype(BF16), down_pair, resid
    )
    steps.wait(joint_sent[0])
    joint_sent.append(across(tie(joint_dots[1], edge_other)))
    def with_edge(d_raw, d_edge):
        window = (1 - core, 0, size - HALO, 0)
        edge_rows = lax.dynamic_slice(d_raw, window, (1,) + d_edge.shape)
        return lax.dynamic_update_slice(
            d_raw, (edge_rows.astype(F32) + d_edge.astype(F32)[None]).astype(BF16), window
        ).reshape(2 * own_rows, -1)

    def logit_step(rates, rows):
        d_rates = sum(rates)
        d_logit = jnp.where(core == 0, d_rates, d_rates[:, ::-1]).transpose(1, 0, 2, 3)
        d_logit = d_logit.reshape(2 * own_rows, LANES).astype(BF16)
        return d_logit, dot_tn(rows, d_logit)[:, :heads]

    d_logit, sum_rate = steps(logit_step, [fourth_own[2], fourth_other[2]], normed_rows)
    d_raw_own = steps(with_edge, fourth_own[0], edge_own)
    d_raw_other = steps(with_edge, fourth_other[0], edge_other)

    pairs = ((d_raw_own, joint_own), (d_raw_other, joint_other), (d_logit, beta))
    d_normed_pair = with_tp(here(away(*pairs, flops=LONG), *pairs))
    grad_outer = over_shard(steps(functools.partial(grad_of, flops=LONG), resid_low, head_own, outer_sent))
    grad_joint = [
        over_shard(steps(functools.partial(joint_grad, 0), *fourth_own[:2], joint_sent[0]))
    ]
    joint_total = steps(functools.partial(joint_grad, 1), *fourth_own[:2], joint_sent[1])
    grad_joint.append(over_shard(joint_total))
    steps.wait(grad_joint[0])
    out_gate = steps(
        lambda pieces: lay_units(places, pieces, True, 1000), pieces_of(grad_gate.T, fourth_own[1])
    )

    def input_back(pair, d_resid, hidden):
        _, pull = jax.vjp(rms, hidden, gain_in)
        d_hidden, sum_attn_gain = pull(pair_sum(pair))
        return sum_attn_gain, (d_resid + d_hidden).astype(BF16)

    sum_attn_gain, input_rows = steps(input_back, d_normed_pair, d_resid, hidden_f32)
    out_up = steps(
        lambda pieces: lay_units(places, pieces, True, LONG), pieces_of(grad_up.T, sum_attn_gain)
    )
    out_outer = steps(lambda pieces: lay_heads_turned(places, pieces), pieces_of(grad_outer))

    sum_taps = [jnp.sum(fourth[3], axis=0).transpose(2, 0, 1, 3) for fourth in (fourth_own, fourth_other)]
    sum_taps = jnp.where(
        cx == 0, jnp.concatenate(sum_taps, axis=2), jnp.concatenate(sum_taps[::-1], axis=2)
    )
    gains = jnp.concatenate([sum_attn_gain[0], sum_ffn_gain[0]]).astype(BF16)
    gains = sum_over(jnp.concatenate([gains, sum_head_gain]), "core", 1)
    packed = jnp.concatenate(
        [gains, sum_taps.reshape(-1).astype(BF16), sum_rate.reshape(-1).astype(BF16)]
    )
    packed = sum_over(packed, "cx", 1)
    hop = 1
    while hop < count:
        packed = sum_over(packed, "shard", hop)
        hop *= 2
    own = lax.axis_index("shard")
    ends = [width, 2 * width, 2 * width + LANES, 2 * width + LANES + sum_taps.size]
    grad_attn_gain = lax.dynamic_slice_in_dim(packed[: ends[0]], own * piece_d, piece_d)
    grad_ffn_gain = lax.dynamic_slice_in_dim(packed[ends[0] : ends[1]], own * piece_d, piece_d)
    grad_out_gain = lax.dynamic_slice_in_dim(packed[ends[1] : ends[2]], own * entry, entry)
    own_conv = lax.dynamic_slice_in_dim(
        packed[ends[2] : ends[3]].reshape(4, 3, heads, LANES), own * entry, entry, axis=3
    )
    own_beta = lax.dynamic_slice_in_dim(
        packed[ends[3] :].reshape(width, heads), own * piece_d, piece_d, axis=0
    )

    def both_cores(values, axis):
        other = to_core(values)
        return jnp.where(
            core == 0,
            jnp.concatenate([values, other], axis=axis),
            jnp.concatenate([other, values], axis=axis),
        ).astype(F32)

    out_query, out_key, out_value = lay_heads(places, [pieces_of(part) for part in grad_joint])
    return (
        result_rows.reshape(hidden_in.shape),
        input_rows.reshape(hidden_in.shape),
        grad_attn_gain.astype(F32),
        out_query,
        out_key,
        out_value,
        both_cores(own_conv, 2),
        both_cores(own_beta, 1),
        grad_out_gain.astype(F32),
        out_outer,
        grad_ffn_gain.astype(F32),
        out_gate,
        out_up,
        out_down,
    )


def solution(mesh):
    shard, ctx, tp = (mesh.shape[name] for name in ("shard", "ctx", "tp"))
    cores = Mesh(
        mesh.devices.reshape(shard, ctx // 2, 2, tp), ("shard", "cx", "core", "tp")
    )
    tokens = P(None, "shard", ("cx", "core"), None)
    outer = P("shard", "tp")
    turned = P("tp", "shard")
    conv = P(None, None, "tp", "shard")
    split = P("shard")
    return jax.shard_map(
        shards,
        mesh=cores,
        in_specs=(
            tokens,
            split,
            outer,
            outer,
            outer,
            conv,
            outer,
            split,
            turned,
            split,
            outer,
            outer,
            turned,
            tokens,
            P(None, "shard", ("cx", "core")),
        ),
        out_specs=(
            tokens,
            tokens,
            split,
            outer,
            outer,
            outer,
            conv,
            outer,
            split,
            turned,
            split,
            outer,
            outer,
            turned,
        ),
        check_vma=False,
    )
```

```python
import functools

import jax
import jax.numpy as jnp
from jax import lax
from jax.experimental import pallas as pl
from jax.experimental.pallas import tpu as pltpu
from jax.sharding import Mesh
from jax.sharding import PartitionSpec as P

EPSILON = 1e-06
F32 = jnp.float32
BF16 = jnp.bfloat16
LANES = 128
HALO = 16
SWAP = [(0, 1), (1, 0)]
LONG = 6 * 10**10


def mm(left, right, left_dim, right_dim):
    return lax.dot_general(
        left.astype(BF16),
        right.astype(BF16),
        (((left_dim,), (right_dim,)), ((), ())),
        preferred_element_type=F32,
    )


def nn(left, right):
    return mm(left, right, 1, 0)


def nt(left, right):
    return mm(left, right, 1, 1)


def tn(left, right):
    return mm(left, right, 0, 0)


def place_scalars():
    return jnp.stack([lax.axis_index("core"), lax.axis_index("cx")]).astype(jnp.int32)


def call(kernel, grid, in_specs, out_specs, out_shape, scratch=(), flops=1000):
    return pl.pallas_call(
        kernel,
        grid_spec=pltpu.PrefetchScalarGridSpec(
            num_scalar_prefetch=1,
            grid=grid,
            in_specs=in_specs,
            out_specs=out_specs,
            scratch_shapes=list(scratch),
        ),
        out_shape=out_shape,
        compiler_params=pltpu.CompilerParams(
            dimension_semantics=("arbitrary",) * len(grid), vmem_limit_bytes=48 << 20
        ),
        cost_estimate=pl.CostEstimate(flops=flops, transcendentals=0, bytes_accessed=1000),
    )


def pack_heads(places, query, key, value, heads):
    rows = query.shape[0]

    def kernel(where, query_ref, key_ref, value_ref, out):
        out[:, :LANES] = query_ref[...]
        out[:, LANES : 2 * LANES] = key_ref[...]
        out[:, 2 * LANES :] = value_ref[...]

    spec = pl.BlockSpec((rows, LANES), lambda h, w: (0, w[0] * heads + 2 * w[1] + h))
    return call(
        kernel,
        (2,),
        [spec] * 3,
        pl.BlockSpec((rows, 3 * LANES), lambda h, w: (0, h)),
        jax.ShapeDtypeStruct((rows, 6 * LANES), query.dtype),
    )(places, query, key, value)


def own_parts(units):
    wide = units // 2
    main = wide // (2 * LANES) * LANES
    return wide, main, wide - 2 * main


def own_units(places, weight, axis):
    wide, main, rest = own_parts(weight.shape[axis])
    first = lax.dynamic_slice_in_dim(weight, places[0] * wide + places[1] * main, main, axis)
    last = lax.dynamic_slice_in_dim(weight, places[0] * wide + 2 * main, rest, axis)
    low, high = jnp.split(last, 2, axis)
    return jnp.concatenate([first, jnp.where(places[1] == 0, low, high)], axis)


def own_heads(places, weight):
    rows = weight.shape[0] // 4
    return lax.dynamic_slice_in_dim(weight, (2 * places[0] + places[1]) * rows, rows, 0)


def pieces_of(own, *after):
    across = lax.ppermute(own, "cx", SWAP)
    late = tie(across, after)
    return [own, across, lax.ppermute(own, "core", SWAP), lax.ppermute(late, "core", SWAP)]


def pick(where, core, cx, refs, store):
    which = 2 * jnp.bitwise_xor(where[0], core) + jnp.bitwise_xor(where[1], cx)
    for index in range(4):

        @pl.when(which == index)
        def _():
            store(refs[index][...].astype(F32))


def lay_heads(places, heads):
    rows = heads[0][0].shape[0]

    def kernel(where, *refs):
        outs = refs[-3:]
        for head in range(2):

            def store(values):
                for index in range(3):
                    outs[index][:, head * LANES : (head + 1) * LANES] = values[
                        :, index * LANES : (index + 1) * LANES
                    ]

            pick(where, pl.program_id(0), pl.program_id(1), refs[4 * head : 4 * head + 4], store)

    return call(
        kernel,
        (2, 2),
        [pl.BlockSpec(heads[0][0].shape, lambda i, j, w: (0, 0))] * 8,
        [pl.BlockSpec((rows, 2 * LANES), lambda i, j, w: (0, 2 * i + j))] * 3,
        [jax.ShapeDtypeStruct((rows, 8 * LANES), F32)] * 3,
    )(places, *heads[0], *heads[1])


def lay_units(places, pieces, turn, flops=1000):
    units, rows = pieces[0].shape
    wide, main, rest = own_parts(4 * units)
    half = rest // 2

    def kernel(where, a, b, c, d, out):
        for side in range(2):

            def store(values):
                at = 2 * main + side * half
                if turn:
                    values = values.T
                    out[:, side * main : (side + 1) * main] = values[:, :main]
                    out[:, at : at + half] = values[:, main:]
                else:
                    out[side * main : (side + 1) * main, :] = values[:main]
                    out[at : at + half, :] = values[main:]

            pick(where, pl.program_id(0), side, (a, b, c, d), store)

    shape = (rows, wide) if turn else (wide, rows)
    return call(
        kernel,
        (2,),
        [pl.BlockSpec((units, rows), lambda i, w: (0, 0))] * 4,
        pl.BlockSpec(shape, (lambda i, w: (0, i)) if turn else (lambda i, w: (i, 0))),
        jax.ShapeDtypeStruct((rows, 2 * wide) if turn else (2 * wide, rows), F32),
        flops=flops,
    )(places, *pieces)


def lay_heads_turned(places, pieces):
    rows, columns = pieces[0].shape

    def kernel(where, a, b, c, d, out):
        def store(values):
            out[...] = values.T

        pick(where, pl.program_id(0), pl.program_id(1), (a, b, c, d), store)

    return call(
        kernel,
        (2, 2),
        [pl.BlockSpec((rows, columns), lambda i, j, w: (0, 0))] * 4,
        pl.BlockSpec((columns, rows), lambda i, j, w: (2 * i + j, 0)),
        jax.ShapeDtypeStruct((4 * columns, rows), F32),
    )(places, *pieces)


def fill_ext(ext, index, halo, first, second, size):
    ext[index, :HALO, :] = halo[...].astype(F32)
    ext[index, HALO : HALO + size, :] = first[...].astype(F32)
    ext[index, HALO + size :, :] = second[...].astype(F32)


def links_of(ids, total):
    own = ids[0, HALO : HALO + total, :]
    return [
        (ids[0, HALO - 3 + tap : HALO - 3 + tap + total, :] == own).astype(F32) for tap in range(4)
    ]


def conv_of(ext, index, taps, links, total):
    result = None
    for tap in range(4):
        term = (
            taps[index, 0, tap : tap + 1, :]
            * ext[index, HALO - 3 + tap : HALO - 3 + tap + total, :]
            * links[tap]
        )
        result = term if result is None else result + term
    return result


def sigmoid(values):
    return 1.0 / (1.0 + jnp.exp(-values))


def first_head(where, own):
    return 2 * (where[1] if own else 1 - where[1])


def head_of(where, own):
    return first_head(where, own) + pl.program_id(1)


def column_of(values, head):
    lane = lax.broadcasted_iota(jnp.int32, values.shape, 1)
    return jnp.sum(jnp.where(lane == head, values, 0.0), axis=1, keepdims=True)


def marks(ids, rows, chunk, size):
    start = HALO + chunk * size
    column = ids[0, start : start + size, :]
    before = ids[0, start - 1 : start, :]
    last = ids[0, start + size - 1 : start + size, :]
    first = (column == before).astype(F32)
    tail = (column == last).astype(F32)
    whole = (last == before).astype(F32)
    same = column == rows[0, chunk : chunk + 1, :]
    row = lax.broadcasted_iota(jnp.int32, (size, size), 0)
    col = lax.broadcasted_iota(jnp.int32, (size, size), 1)
    return first, tail, whole, same & (row > col), same & (row >= col)


def inverse_units(stricts, size):
    row = lax.broadcasted_iota(jnp.int32, (size, size), 0)
    col = lax.broadcasted_iota(jnp.int32, (size, size), 1)
    mixed = jnp.bitwise_xor(row, col)
    results = [
        jnp.where(row == col, 1.0, jnp.where(mixed == 1, -strict, 0.0)) for strict in stricts
    ]
    stricts = [strict.astype(BF16) for strict in stricts]
    block = 2
    while block < size:
        pair = (mixed >= block) & (mixed < 2 * block)
        lows = [result.astype(BF16) for result in results]
        parts = [jnp.where(pair, strict, 0.0) for strict in stricts]
        steps = [nn(part, low).astype(BF16) for part, low in zip(parts, lows)]
        results = [
            result - nn(low, step) for result, low, step in zip(results, lows, steps)
        ]
        block *= 2
    return [result.astype(BF16) for result in results]


def forward_one(where, q0, k0, v0, q1, k1, v1, qh, kh, vh, taps, ids, rows, r0, r1, *rest, size, own):
    query, key, value, inverse, final, ext = rest
    head = head_of(where, own)
    total = 2 * size
    for index, group in enumerate(((qh, q0, q1), (kh, k0, k1), (vh, v0, v1))):
        fill_ext(ext, index, *group, size)
    links = links_of(ids, total)
    out = []
    for index in range(3):
        conv = conv_of(ext, index, taps, links, total)
        act = conv * sigmoid(conv)
        if index < 2:
            act = act * lax.rsqrt(jnp.sum(act * act, axis=1, keepdims=True) + EPSILON)
        out.append(act.astype(BF16))
    for target, values in zip((query, key, value), out):
        target[0, 0] = values[:size]
        target[0, 1] = values[size:]
    chunks = []
    for chunk, rates in enumerate((r0, r1)):
        first, tail, whole, strict, _ = marks(ids, rows, chunk, size)
        rate = column_of(rates[...], head)
        keys = out[1][chunk * size : (chunk + 1) * size]
        chunks.append((first, tail, whole, rate, keys, jnp.where(strict, rate * nt(keys, keys), 0.0)))
    inverses = inverse_units([item[-1] for item in chunks], size)
    state = None
    for chunk, (first, tail, whole, rate, keys, _) in enumerate(chunks):
        fresh = out[2][chunk * size : (chunk + 1) * size].astype(F32)
        inverse[0, 0, chunk] = inverses[chunk]
        if chunk:
            fresh = fresh - first * nt(keys, state)
        fresh = nn(inverses[chunk], rate * fresh)
        added = tn(tail * fresh, keys)
        state = added if state is None else whole * state + added
    final[0, 0] = state.astype(BF16)


def forward_two(where, query, key, value, inverse, ids, rows, r0, r1, incoming, gain, *rest, size, scale, own):
    head_low, mixed_out, fresh_out, middle = rest
    head = head_of(where, own)
    state = incoming[0, 0].astype(F32)
    for chunk, rates in enumerate((r0, r1)):
        first, tail, whole, _, lower = marks(ids, rows, chunk, size)
        rate = column_of(rates[...], head)
        keys, queries = key[0, chunk], query[0, chunk]
        if chunk:
            middle[0, 0] = state.astype(BF16)
        rest_rows = value[0, chunk].astype(F32) - first * nt(keys, state)
        fresh = nn(inverse[0, 0, chunk], rate * rest_rows)
        fresh_out[0, chunk] = fresh.astype(BF16)
        inner = jnp.where(lower, nt(queries, keys), 0.0)
        mixed = scale * (first * nt(queries, state) + nn(inner, fresh))
        mixed_out[0, chunk] = mixed
        normed = mixed * lax.rsqrt(jnp.mean(mixed * mixed, axis=1, keepdims=True) + EPSILON)
        slot = where[0] if chunk == 0 else 1 - where[0]
        head_low[slot, 0] = (normed * gain[...]).astype(BF16)
        if chunk == 0:
            state = whole * state + tn(tail * fresh, keys)


def backward_one(where, d_head, mixed, query, key, inverse, ids, rows, r0, r1, gain, *rest, size, scale, own):
    d_out, d_state_out, d_gain = rest
    head = head_of(where, own)
    total = jnp.zeros((1, LANES), F32)
    d_state = None
    for chunk in (1, 0):
        first, tail, whole, _, lower = marks(ids, rows, chunk, size)
        rate = column_of((r0, r1)[chunk][...], head)
        keys, queries = key[0, chunk], query[0, chunk]
        slot = where[0] if chunk == 0 else 1 - where[0]
        grad = d_head[slot, 0].astype(F32)
        values = mixed[0, chunk]
        inv_rms = lax.rsqrt(jnp.mean(values * values, axis=1, keepdims=True) + EPSILON)
        normed = values * inv_rms
        total = total + jnp.sum(grad * normed, axis=0, keepdims=True)
        scaled = grad * gain[...]
        d_mixed = inv_rms * (scaled - normed * jnp.mean(scaled * normed, axis=1, keepdims=True))
        d_low = (scale * d_mixed).astype(BF16)
        d_out[0, chunk] = d_low
        inner = jnp.where(lower, nt(queries, keys), 0.0)
        d_fresh = tn(inner, d_low)
        if d_state is not None:
            d_fresh = d_fresh + tail * nt(keys, d_state)
        d_rest = rate * tn(inverse[0, 0, chunk], d_fresh)
        change = tn(first * d_low.astype(F32), queries) - tn(first * d_rest, keys)
        d_state = change if d_state is None else whole * d_state + change
    d_state_out[0, 0] = d_state.astype(BF16)
    d_gain[0, 0] = jnp.broadcast_to(total, (8, LANES))


def backward_two(where, q0, k0, v0, q1, k1, v1, qh, kh, vh, taps, ids, rows, r0, r1, *rest, size, own):
    query, key, value, inverse, fresh_in, d_in, incoming, middle, d_final = rest[:9]
    d_raw, d_edge, d_rates, d_taps = rest[9:13]
    ext, d_ext, d_rows = rest[13:]
    head = head_of(where, own)
    total = 2 * size
    for index, group in enumerate(((qh, q0, q1), (kh, k0, k1), (vh, v0, v1))):
        fill_ext(ext, index, *group, size)
    d_state = d_final[0, 0].astype(F32)

    @pl.when(pl.program_id(1) == 0)
    def _():
        d_rates[...] = jnp.zeros_like(d_rates)

    for chunk in (1, 0):
        first, tail, whole, strict, lower = marks(ids, rows, chunk, size)
        rate = column_of((r0, r1)[chunk][...], head)
        keys, queries, fresh = key[0, chunk], query[0, chunk], fresh_in[0, chunk]
        inv, d_low = inverse[0, 0, chunk], d_in[0, chunk]
        state = (middle if chunk else incoming)[0, 0]
        d_mix = d_low.astype(F32)
        inner = jnp.where(lower, nt(queries, keys), 0.0)
        gram = jnp.where(strict, nt(keys, keys), 0.0)
        d_fresh = tn(inner, d_low) + tail * nt(keys, d_state)
        turned = tn(inv, d_fresh)
        d_rest = rate * turned
        rest_rows = value[0, chunk].astype(F32) - first * nt(keys, state)
        error = rest_rows - nn(gram, fresh)
        d_rate = jnp.sum(turned * error, axis=1, keepdims=True) * rate * (1.0 - rate)
        d_inner = jnp.where(lower, nt(d_low, fresh), 0.0)
        d_gram = rate * jnp.where(strict, -nt(turned, fresh), 0.0)
        d_query = first * nn(d_low, state) + nn(d_inner, keys)
        d_key = (
            tn(d_inner, queries)
            + tail * nn(fresh, d_state)
            - nn(first * d_rest, state)
            + nn(d_gram, keys)
            + tn(d_gram, keys)
        )
        for index, values in enumerate((d_query, d_key, d_rest)):
            d_rows[index, chunk * size : (chunk + 1) * size, :] = values
        lane = lax.broadcasted_iota(jnp.int32, (size, LANES), 1)
        d_rates[0, chunk] = d_rates[0, chunk] + jnp.where(lane == head, d_rate, 0.0)
        if chunk:
            d_state = (
                whole * d_state + tn(first * d_mix, queries) - tn(first * d_rest, keys)
            )
    links = links_of(ids, total)
    for index in range(3):
        conv = conv_of(ext, index, taps, links, total)
        sig = sigmoid(conv)
        d_act = d_rows[index].astype(BF16).astype(F32)
        if index < 2:
            act = conv * sig
            inv_norm = lax.rsqrt(jnp.sum(act * act, axis=1, keepdims=True) + EPSILON)
            unit = act * inv_norm
            d_act = (d_act - unit * jnp.sum(unit * d_act, axis=1, keepdims=True)) * inv_norm
        d_conv = d_act * sig * (1.0 + conv * (1.0 - sig))
        d_ext[...] = jnp.zeros_like(d_ext)
        for tap in range(4):
            window = slice(HALO - 3 + tap, HALO - 3 + tap + total)
            linked = d_conv * links[tap]
            d_taps[0, index, 0, tap : tap + 1, :] = jnp.sum(
                linked * ext[index, window, :], axis=0, keepdims=True
            )
            d_ext[window, :] = d_ext[window, :] + taps[index, 0, tap : tap + 1, :] * linked
        lanes = slice(index * LANES, (index + 1) * LANES)
        d_edge[0, :, lanes] = d_ext[:HALO, :].astype(BF16)
        d_raw[where[0], 0, :, lanes] = d_ext[HALO : HALO + size, :].astype(BF16)
        d_raw[1 - where[0], 0, :, lanes] = d_ext[HALO + size :, :].astype(BF16)


def mixer_calls(places, own, rates, ids, rows, taps, gain, seqs, size, scale):
    def slot_of(chunk, w):
        return w[0] if chunk == 0 else 1 - w[0]

    def raw_spec(chunk, part):
        return pl.BlockSpec(
            (size, LANES), lambda b, h, w: (slot_of(chunk, w) * seqs + b, 3 * h + part)
        )

    def rate_spec(chunk):
        return pl.BlockSpec((size, LANES), lambda b, h, w: (slot_of(chunk, w) * seqs + b, 0))

    halo_base = 2 * seqs * size // HALO

    def halo_spec(part):
        return pl.BlockSpec((HALO, LANES), lambda b, h, w: (halo_base + b, 3 * h + part))

    conv_specs = (
        [raw_spec(c, p) for c in range(2) for p in range(3)]
        + [halo_spec(p) for p in range(3)]
        + [
            pl.BlockSpec((3, 1, 4, LANES), lambda b, h, w: (0, first_head(w, own) + h, 0, 0)),
            pl.BlockSpec((1, HALO + 2 * size, 1), lambda b, h, w: (b, 0, 0)),
            pl.BlockSpec((1, 2, size), lambda b, h, w: (b, 0, 0)),
            rate_spec(0),
            rate_spec(1),
        ]
    )
    rest_args = (taps, ids, rows, rates, rates)
    id_specs, id_args = conv_specs[10:], rest_args[1:]
    act_spec = pl.BlockSpec((1, 2, size, LANES), lambda b, h, w: (b, 0, 0, h))
    act_shape = (seqs, 2, size, 2 * LANES)
    state_spec = pl.BlockSpec((1, 1, LANES, LANES), lambda b, h, w: (b, h, 0, 0))
    state_shape = jax.ShapeDtypeStruct((seqs, 2, LANES, LANES), BF16)
    inv_spec = pl.BlockSpec((1, 1, 2, size, size), lambda b, h, w: (b, h, 0, 0, 0))
    inv_shape = jax.ShapeDtypeStruct((seqs, 2, 2, size, size), BF16)
    slot_spec = pl.BlockSpec((2, 1, size, LANES), lambda b, h, w: (0, b, 0, h))
    slot_shape = jax.ShapeDtypeStruct((2, seqs, size, 2 * LANES), BF16)
    gain_spec = pl.BlockSpec((1, LANES), lambda b, h, w: (0, 0))
    low = jax.ShapeDtypeStruct(act_shape, BF16)
    grid = (seqs, 2)

    def one(raw):
        return call(
            functools.partial(forward_one, size=size, own=own),
            grid,
            conv_specs,
            [act_spec] * 3 + [inv_spec, state_spec],
            [low] * 3 + [inv_shape, state_shape],
            [pltpu.VMEM((3, HALO + 2 * size, LANES), F32)],
        )(places, *(raw,) * 9, *rest_args)

    def two(query, key, value, inverse, incoming):
        args = (query, key, value, inverse, *id_args, incoming, gain)
        return call(
            functools.partial(forward_two, size=size, scale=scale, own=own),
            grid,
            [act_spec] * 3
            + [inv_spec]
            + id_specs
            + [state_spec, gain_spec],
            [slot_spec, act_spec, act_spec, state_spec],
            [slot_shape, jax.ShapeDtypeStruct(act_shape, F32), low, state_shape],
        )(places, *args)

    def three(d_head, mixed, query, key, inverse):
        return call(
            functools.partial(backward_one, size=size, scale=scale, own=own),
            grid,
            [slot_spec, act_spec, act_spec, act_spec, inv_spec] + id_specs + [gain_spec],
            [act_spec, state_spec, pl.BlockSpec((1, 1, 8, LANES), lambda b, h, w: (b, h, 0, 0))],
            [low, state_shape, jax.ShapeDtypeStruct((seqs, 2, 8, LANES), F32)],
            flops=int(26 * 1.1e9),
        )(places, d_head, mixed, query, key, inverse, *id_args, gain)

    def four(raw, query, key, value, inverse, fresh, d_low, incoming, middle, d_final):
        return call(
            functools.partial(backward_two, size=size, own=own),
            grid,
            conv_specs + [act_spec] * 3 + [inv_spec, act_spec, act_spec] + [state_spec] * 3,
            [
                pl.BlockSpec((2, 1, size, 3 * LANES), lambda b, h, w: (0, b, 0, h)),
                pl.BlockSpec((1, HALO, 3 * LANES), lambda b, h, w: (b, 0, h)),
                pl.BlockSpec((1, 2, size, LANES), lambda b, h, w: (b, 0, 0, 0)),
                pl.BlockSpec((1, 3, 1, 4, LANES), lambda b, h, w: (b, 0, h, 0, 0)),
            ],
            [
                jax.ShapeDtypeStruct((2, seqs, size, 6 * LANES), BF16),
                jax.ShapeDtypeStruct((seqs, HALO, 6 * LANES), BF16),
                jax.ShapeDtypeStruct((seqs, 2, size, LANES), F32),
                jax.ShapeDtypeStruct((seqs, 3, 2, 4, LANES), F32),
            ],
            [
                pltpu.VMEM((3, HALO + 2 * size, LANES), F32),
                pltpu.VMEM((HALO + 2 * size, LANES), F32),
                pltpu.VMEM((3, 2 * size, LANES), F32),
            ],
            flops=int(26 * 1.1e9),
        )(
            places,
            *(raw,) * 9,
            *rest_args,
            query,
            key,
            value,
            inverse,
            fresh,
            d_low,
            incoming,
            middle,
            d_final,
        )

    return one, two, three, four


def tile_of(extent):
    return 512 if extent % 512 == 0 else extent


def rows_products(pairs, rows, block, add=None, out=BF16, flops=1000):
    columns = pairs[0][1].shape[0]
    tile = tile_of(columns)
    count = len(pairs)

    def kernel(*refs):
        total = None
        for index in range(count):
            part = nt(refs[index][...], refs[count + index][...])
            total = part if total is None else total + part
        if add is not None:
            total = total + refs[2 * count][...].astype(F32)
        refs[-1][...] = total.astype(out)

    lefts = [pl.BlockSpec((rows, left.shape[1]), lambda i: (block, 0)) for left, _ in pairs]
    rights = [pl.BlockSpec((tile, right.shape[1]), lambda i: (i, 0)) for _, right in pairs]
    spec = pl.BlockSpec((rows, tile), lambda i: (0, i))
    extra = () if add is None else (add,)
    return pl.pallas_call(
        kernel,
        grid=(columns // tile,),
        in_specs=lefts + rights + [spec] * len(extra),
        out_specs=spec,
        out_shape=jax.ShapeDtypeStruct((rows, columns), out),
        compiler_params=pltpu.CompilerParams(vmem_limit_bytes=48 << 20),
        cost_estimate=pl.CostEstimate(flops=flops, transcendentals=0, bytes_accessed=1000),
    )(*(left for left, _ in pairs), *(right for _, right in pairs), *extra)


def token_products(pairs, add=None, flops=1000):
    count = len(pairs)
    height, columns = pairs[0][0].shape[1], pairs[0][1].shape[1]
    tile = tile_of(height)

    def kernel(*refs):
        total = None
        for index in range(count):
            part = tn(refs[index][...], refs[count + index][...])
            total = part if total is None else total + part
        if add is not None:
            total = total + refs[2 * count][...].astype(F32)
        refs[-1][...] = total.astype(BF16)

    lefts = [
        pl.BlockSpec((rows, tile), lambda i, block=block: (block, i))
        for _, _, rows, block in pairs
    ]
    rights = [pl.BlockSpec((rows, columns), lambda i: (0, 0)) for _, _, rows, _ in pairs]
    spec = pl.BlockSpec((tile, columns), lambda i: (i, 0))
    extra = () if add is None else (add,)
    return pl.pallas_call(
        kernel,
        grid=(height // tile,),
        in_specs=lefts + rights + [spec] * len(extra),
        out_specs=spec,
        out_shape=jax.ShapeDtypeStruct((height, columns), BF16),
        compiler_params=pltpu.CompilerParams(vmem_limit_bytes=48 << 20),
        cost_estimate=pl.CostEstimate(flops=flops, transcendentals=0, bytes_accessed=1000),
    )(*(item[0] for item in pairs), *(item[1] for item in pairs), *extra)


def feed_forward(rows, grads, gates, ups, downs):
    tokens, width = rows.shape
    units = gates.shape[1]
    tile = 256 if tokens % 256 == 0 else tokens

    def kernel(rows_ref, grads_ref, gates_ref, ups_ref, downs_ref, act, d_gate, d_up):
        gate = nn(rows_ref[...], gates_ref[...])
        up = nn(rows_ref[...], ups_ref[...])
        d_act = nn(grads_ref[...], downs_ref[...]).astype(BF16).astype(F32)
        sig = sigmoid(gate)
        act[...] = (gate * sig * up).astype(BF16)
        d_gate[...] = (d_act * up * sig * (1.0 + gate * (1.0 - sig))).astype(BF16)
        d_up[...] = (d_act * gate * sig).astype(BF16)

    token_spec = pl.BlockSpec((tile, width), lambda i: (i, 0))
    weight_spec = pl.BlockSpec((width, units), lambda i: (0, 0))
    unit_spec = pl.BlockSpec((tile, units), lambda i: (i, 0))
    return pl.pallas_call(
        kernel,
        grid=(tokens // tile,),
        in_specs=[token_spec] * 2 + [weight_spec] * 3,
        out_specs=[unit_spec] * 3,
        out_shape=[jax.ShapeDtypeStruct((tokens, units), BF16)] * 3,
        compiler_params=pltpu.CompilerParams(vmem_limit_bytes=48 << 20),
        cost_estimate=pl.CostEstimate(flops=1000, transcendentals=0, bytes_accessed=1000),
    )(rows, grads, gates, ups, downs)


def dot_nn(left, right):
    return lax.dot_general(left, right, (((1,), (0,)), ((), ())), preferred_element_type=F32)


def dot_nt(left, right):
    return lax.dot_general(left, right, (((1,), (1,)), ((), ())), preferred_element_type=F32)


def dot_tn(left, right):
    return lax.dot_general(left, right, (((0,), (0,)), ((), ())), preferred_element_type=F32)


def rms(values, gain):
    return values * lax.rsqrt(jnp.mean(values * values, axis=1, keepdims=True) + EPSILON) * gain


def tie(value, *after):
    return lax.optimization_barrier((value, after))[0]


class Steps:
    def __init__(self):
        self.last = ()

    def wait(self, *values):
        self.last = (self.last, values)

    def __call__(self, fn, *args):
        traced, static = [], []
        for arg in args:
            leaves = jax.tree.leaves(arg)
            static.append(not leaves or not all(hasattr(leaf, "dtype") for leaf in leaves))
            if not static[-1]:
                traced.append(arg)
        traced = iter(tie(tuple(traced), self.last))
        result = fn(*(arg if fixed else next(traced) for arg, fixed in zip(args, static)))
        self.last = result
        return result


def sum_over(values, axis, hop):
    partners = [(index, index ^ hop) for index in range(lax.axis_size(axis))]
    return (values.astype(F32) + lax.ppermute(values, axis, partners).astype(F32)).astype(BF16)


def shards(
    hidden_in,
    attn_gain,
    query_weight,
    key_weight,
    value_weight,
    conv_weight,
    beta_weight,
    out_gain,
    out_weight,
    ffn_gain,
    gate_weight,
    up_weight,
    down_weight,
    cotangent,
    segment_ids,
):
    count = lax.axis_size("shard")
    places = place_scalars()
    core, cx = places[0], places[1]
    micro, local, size, width = hidden_in.shape
    seqs = micro * local
    own_rows = seqs * size
    heads_tp = conv_weight.shape[2]
    heads = heads_tp // 2
    scale = LANES ** (-0.5)
    first_rows, other_rows = slice(0, own_rows), slice(own_rows, 2 * own_rows)

    def gathered(piece):
        return lax.all_gather(piece, "shard", axis=0, tiled=True)

    def over_shard(total):
        return lax.psum_scatter(total, "shard", scatter_dimension=0, tiled=True)

    def across(part):
        return lax.ppermute(part, "cx", SWAP)

    def to_core(part):
        return lax.ppermute(part, "core", SWAP)

    def with_core(part):
        return jnp.concatenate([part, to_core(part)])

    pack = pack_heads(places, query_weight, key_weight, value_weight, heads)
    joint_own = gathered(pack)

    small = jnp.concatenate(
        [
            attn_gain,
            ffn_gain,
            out_gain,
            conv_weight.reshape(-1),
            beta_weight.reshape(-1),
        ]
    )
    unpadded = small.size
    small = jnp.pad(small, (0, -unpadded % (16 * LANES))).reshape(-1, LANES)
    small = lax.all_gather(small, "shard", axis=0).reshape(count, -1)
    piece_d = attn_gain.shape[0]
    entry = out_gain.shape[0]
    at = 2 * piece_d + entry
    gain_in = small[:, :piece_d].reshape(1, -1).astype(F32)
    gain_ffn = small[:, piece_d : 2 * piece_d].reshape(1, -1).astype(F32)
    gain_head = small[:, 2 * piece_d : at].reshape(1, LANES).astype(F32)
    conv_size = conv_weight.size
    taps = small[:, at : at + conv_size].reshape(count, 4, 3, heads_tp, entry)
    taps = taps.transpose(2, 3, 1, 0, 4).reshape(3, heads_tp, 4, LANES)
    taps = lax.dynamic_slice_in_dim(taps, core * heads, heads, axis=1).astype(F32)
    beta = small[:, at + conv_size : unpadded].reshape(width, heads_tp)
    beta = lax.dynamic_slice_in_dim(beta, core * heads, heads, axis=1)
    beta = jnp.pad(beta, ((0, 0), (0, LANES - heads)))

    hidden_own = hidden_in.reshape(own_rows, width)
    hidden_other = to_core(hidden_own)
    ids_own = segment_ids.reshape(seqs, size)
    ids_other = to_core(ids_own)
    late = jnp.where(core == 1, hidden_own, hidden_other).reshape(seqs, size, width)[:, size - HALO :]
    early_ids = jnp.where(core == 0, ids_own, ids_other)
    late_ids = jnp.where(core == 1, ids_own, ids_other)
    halo = lax.ppermute(late, "cx", [(0, 1)]).reshape(seqs * HALO, width)
    halo_ids = lax.ppermute(late_ids[:, size - HALO :], "cx", [(0, 1)])
    halo_ids = jnp.where(cx == 0, -1, halo_ids)
    ids = jnp.concatenate([halo_ids, early_ids, late_ids], axis=1)[..., None]
    id_rows = jnp.stack([early_ids, late_ids], axis=1)
    hidden_all = jnp.concatenate([hidden_own, hidden_other, halo])
    normed_low = rms(hidden_all.astype(F32), gain_in).astype(BF16)
    rates = sigmoid(dot_nn(normed_low, beta))
    grad_own = cotangent.reshape(own_rows, width)
    grad_near = with_core(grad_own)
    grad_far = with_core(across(grad_own))

    outer_own = gathered(tie(own_heads(places, out_weight).T, pack))
    gates = gathered(tie(own_units(places, gate_weight, 1), pack, hidden_all))
    ups = gathered(tie(own_units(places, up_weight, 1), normed_low, rates))
    downs = gathered(tie(own_units(places, down_weight, 0).T, grad_near, grad_far))
    joint_other = across(tie(joint_own, grad_far, ids, id_rows, normed_low))

    steps = Steps()
    shapes = (rates, ids, id_rows, taps, gain_head, seqs, size, scale)
    own_calls = mixer_calls(places, True, *shapes)
    other_calls = mixer_calls(places, False, *shapes)

    def project(rows, weight):
        return dot_nn(rows, weight).astype(BF16)

    raw_own = steps(project, normed_low, joint_own)
    first_own = steps(own_calls[0], raw_own)
    outer_other = across(tie(outer_own, joint_other, first_own[-1]))
    raw_other = steps(project, normed_low, joint_other)
    first_other = steps(other_calls[0], raw_other)
    in_other = lax.ppermute(first_own[-1], "cx", [(0, 1)])
    in_own = lax.ppermute(first_other[-1], "cx", [(0, 1)])
    head_other, mixed_other, fresh_other, middle_other = steps(
        other_calls[1], *first_other[:4], in_other
    )
    head_own, mixed_own, fresh_own, middle_own = steps(own_calls[1], *first_own[:4], in_own)
    slots = head_own.shape
    head_own, head_other = (part.reshape(2 * own_rows, -1) for part in (head_own, head_other))

    def products(block, lefts, rights, add=None, out=BF16, flops=1000):
        return rows_products(list(zip(lefts, rights)), own_rows, block, add, out, flops)

    def away(*pairs, flops=1000):
        lefts, rights = zip(*pairs)
        return to_core(steps(lambda *args: products(1, *args, flops=flops), lefts, rights))

    def here(arrived, *pairs, out=BF16):
        lefts, rights = zip(*pairs)
        return steps(lambda *args: products(0, *args, out), lefts, rights, arrived)

    def with_tp(part):
        return part, lax.ppermute(part, "tp", SWAP)

    def pair_sum(pair):
        return pair[0].astype(F32) + pair[1].astype(F32)

    pairs = ((head_own, outer_own), (head_other, outer_other))
    mixer_pair = with_tp(here(away(*pairs), *pairs))
    hidden_f32 = hidden_own.astype(F32)

    def resid_step(pair, hidden):
        resid = hidden + pair_sum(pair)
        return resid, rms(resid, gain_ffn).astype(BF16)

    steps.wait(ups)
    resid, ffn_own = steps(resid_step, mixer_pair, hidden_f32)
    ffn_far_own = across(ffn_own)
    ffn_near = with_core(ffn_own)

    weights = (gates, ups, downs)
    act_near, d_gate_near, d_up_near = steps(feed_forward, ffn_near, grad_near, *weights)
    near = ((d_gate_near, gates), (d_up_near, ups))
    near_arrived = away(*near)
    down_near_arrived = away((act_near, downs))
    ffn_far = with_core(tie(ffn_far_own, down_near_arrived))
    act_far, d_gate_far, d_up_far = steps(feed_forward, ffn_far, grad_far, *weights)
    far = ((d_gate_far, gates), (d_up_far, ups))

    def both_grads(near, far, grads_near, grads_far):
        rows = near.shape[0]
        return token_products([(near, grads_near, rows, 0), (far, grads_far, rows, 0)])

    d_ffn_sent = across(here(away(*far), *far))
    grad_down = over_shard(steps(both_grads, grad_near, grad_far, act_near, act_far))
    d_ffn_near = here(near_arrived, *near, out=F32)
    down_far_arrived = away((act_far, downs))
    grad_gate = over_shard(steps(both_grads, ffn_near, ffn_far, d_gate_near, d_gate_far))

    def add_far(near, arrived):
        return (near + arrived.astype(F32)).astype(BF16)

    d_ffn_pair = with_tp(steps(add_far, d_ffn_near, d_ffn_sent))
    grad_up = over_shard(steps(both_grads, ffn_near, ffn_far, d_up_near, d_up_far))
    down_sent = across(here(down_far_arrived, (act_far, downs)))
    down_near = here(down_near_arrived, (act_near, downs), out=F32)

    def resid_back(pair, resid, grads):
        _, pull = jax.vjp(rms, resid, gain_ffn)
        d_resid, sum_ffn_gain = pull(pair_sum(pair))
        d_resid = grads.astype(F32) + d_resid
        return d_resid, sum_ffn_gain, d_resid.astype(BF16)

    d_resid, sum_ffn_gain, resid_own = steps(resid_back, d_ffn_pair, resid, grad_own)
    resid_other = to_core(resid_own)
    resid_low = steps(lambda own, other: jnp.concatenate([own, other]), resid_own, resid_other)

    def grad_of(rows, grads, *arrived, flops=1000):
        return token_products([(rows, grads, 2 * own_rows, 0)], *arrived, flops=flops)

    d_head_own = steps(project, resid_low, outer_own).reshape(slots)
    d_head_other = steps(project, resid_low, outer_other).reshape(slots)
    steps.wait(grad_down)
    third_own = steps(own_calls[2], d_head_own, mixed_own, *first_own[:2], first_own[3])
    d_final_other = lax.ppermute(third_own[1], "cx", [(1, 0)])
    third_other = steps(other_calls[2], d_head_other, mixed_other, *first_other[:2], first_other[3])
    d_final_own = lax.ppermute(third_other[1], "cx", [(1, 0)])
    outer_sent = across(steps(grad_of, resid_low, head_other))
    down_pair = with_tp(steps(add_far, down_near, down_sent))
    sum_head_gain = steps(
        lambda *parts: sum(jnp.sum(part[:, :, 0, :], axis=(0, 1)) for part in parts).astype(BF16),
        third_own[2],
        third_other[2],
    )
    sum_head_gain = sum_over(sum_head_gain, "tp", 1)
    steps.wait(d_final_own, d_final_other, sum_head_gain)
    steps.wait(grad_gate)
    fourth_other = steps(
        other_calls[3],
        raw_other,
        *first_other[:4],
        fresh_other,
        third_other[0],
        in_other,
        middle_other,
        d_final_other,
    )
    edge_own = lax.ppermute(fourth_other[1], "cx", [(1, 0)])
    normed_rows = normed_low[: 2 * own_rows]

    def joint_grad(half, d_raw, d_edge, *arrived, flops=1000):
        lanes = slice(half * 3 * LANES, (half + 1) * 3 * LANES)
        d_raw = d_raw.reshape(2 * own_rows, -1)[:, lanes]
        d_edge = d_edge.reshape(seqs * HALO, -1)[:, lanes]
        pairs = [(normed_low, d_raw, 2 * own_rows, 0)]
        pairs += [(normed_low, d_edge, seqs * HALO, 2 * own_rows // (seqs * HALO))]
        return token_products(pairs, *arrived, flops=flops)

    out_down = steps(
        lambda pieces: lay_units(places, pieces, False, 1000), pieces_of(grad_down.T, fourth_other[1])
    )
    joint_dots = [
        steps(functools.partial(joint_grad, half), *fourth_other[:2]) for half in range(2)
    ]
    joint_sent = [across(joint_dots[0])]
    steps.wait(outer_sent, grad_up)
    fourth_own = steps(
        own_calls[3],
        raw_own,
        *first_own[:4],
        fresh_own,
        third_own[0],
        in_own,
        middle_own,
        d_final_own,
    )
    edge_other = lax.ppermute(fourth_own[1], "cx", [(1, 0)])
    result_rows = steps(
        lambda pair, resid: (resid + pair_sum(pair)).astype(BF16), down_pair, resid
    )
    steps.wait(joint_sent[0])
    joint_sent.append(across(tie(joint_dots[1], edge_other)))
    def with_edge(d_raw, d_edge):
        window = (1 - core, 0, size - HALO, 0)
        edge_rows = lax.dynamic_slice(d_raw, window, (1,) + d_edge.shape)
        return lax.dynamic_update_slice(
            d_raw, (edge_rows.astype(F32) + d_edge.astype(F32)[None]).astype(BF16), window
        ).reshape(2 * own_rows, -1)

    def logit_step(rates, rows):
        d_rates = sum(rates)
        d_logit = jnp.where(core == 0, d_rates, d_rates[:, ::-1]).transpose(1, 0, 2, 3)
        d_logit = d_logit.reshape(2 * own_rows, LANES).astype(BF16)
        return d_logit, dot_tn(rows, d_logit)[:, :heads]

    d_logit, sum_rate = steps(logit_step, [fourth_own[2], fourth_other[2]], normed_rows)
    d_raw_own = steps(with_edge, fourth_own[0], edge_own)
    d_raw_other = steps(with_edge, fourth_other[0], edge_other)

    pairs = ((d_raw_own, joint_own), (d_raw_other, joint_other), (d_logit, beta))
    d_normed_pair = with_tp(here(away(*pairs, flops=LONG), *pairs))
    grad_outer = over_shard(steps(functools.partial(grad_of, flops=LONG), resid_low, head_own, outer_sent))
    grad_joint = [
        over_shard(steps(functools.partial(joint_grad, 0), *fourth_own[:2], joint_sent[0]))
    ]
    joint_total = steps(functools.partial(joint_grad, 1), *fourth_own[:2], joint_sent[1])
    grad_joint.append(over_shard(joint_total))
    steps.wait(grad_joint[0])
    out_gate = steps(
        lambda pieces: lay_units(places, pieces, True, 1000), pieces_of(grad_gate.T, joint_total)
    )

    def input_back(pair, d_resid, hidden):
        _, pull = jax.vjp(rms, hidden, gain_in)
        d_hidden, sum_attn_gain = pull(pair_sum(pair))
        return sum_attn_gain, (d_resid + d_hidden).astype(BF16)

    sum_attn_gain, input_rows = steps(input_back, d_normed_pair, d_resid, hidden_f32)
    out_up = steps(
        lambda pieces: lay_units(places, pieces, True, LONG), pieces_of(grad_up.T, sum_attn_gain)
    )
    out_outer = steps(lambda pieces: lay_heads_turned(places, pieces), pieces_of(grad_outer))

    sum_taps = [jnp.sum(fourth[3], axis=0).transpose(2, 0, 1, 3) for fourth in (fourth_own, fourth_other)]
    sum_taps = jnp.where(
        cx == 0, jnp.concatenate(sum_taps, axis=2), jnp.concatenate(sum_taps[::-1], axis=2)
    )
    gains = jnp.concatenate([sum_attn_gain[0], sum_ffn_gain[0]]).astype(BF16)
    gains = sum_over(jnp.concatenate([gains, sum_head_gain]), "core", 1)
    packed = jnp.concatenate(
        [gains, sum_taps.reshape(-1).astype(BF16), sum_rate.reshape(-1).astype(BF16)]
    )
    packed = sum_over(packed, "cx", 1)
    hop = 1
    while hop < count:
        packed = sum_over(packed, "shard", hop)
        hop *= 2
    own = lax.axis_index("shard")
    ends = [width, 2 * width, 2 * width + LANES, 2 * width + LANES + sum_taps.size]
    grad_attn_gain = lax.dynamic_slice_in_dim(packed[: ends[0]], own * piece_d, piece_d)
    grad_ffn_gain = lax.dynamic_slice_in_dim(packed[ends[0] : ends[1]], own * piece_d, piece_d)
    grad_out_gain = lax.dynamic_slice_in_dim(packed[ends[1] : ends[2]], own * entry, entry)
    own_conv = lax.dynamic_slice_in_dim(
        packed[ends[2] : ends[3]].reshape(4, 3, heads, LANES), own * entry, entry, axis=3
    )
    own_beta = lax.dynamic_slice_in_dim(
        packed[ends[3] :].reshape(width, heads), own * piece_d, piece_d, axis=0
    )

    def both_cores(values, axis):
        other = to_core(values)
        return jnp.where(
            core == 0,
            jnp.concatenate([values, other], axis=axis),
            jnp.concatenate([other, values], axis=axis),
        ).astype(F32)

    out_query, out_key, out_value = lay_heads(places, [pieces_of(part) for part in grad_joint])
    return (
        result_rows.reshape(hidden_in.shape),
        input_rows.reshape(hidden_in.shape),
        grad_attn_gain.astype(F32),
        out_query,
        out_key,
        out_value,
        both_cores(own_conv, 2),
        both_cores(own_beta, 1),
        grad_out_gain.astype(F32),
        out_outer,
        grad_ffn_gain.astype(F32),
        out_gate,
        out_up,
        out_down,
    )


def solution(mesh):
    shard, ctx, tp = (mesh.shape[name] for name in ("shard", "ctx", "tp"))
    cores = Mesh(
        mesh.devices.reshape(shard, ctx // 2, 2, tp), ("shard", "cx", "core", "tp")
    )
    tokens = P(None, "shard", ("cx", "core"), None)
    outer = P("shard", "tp")
    turned = P("tp", "shard")
    conv = P(None, None, "tp", "shard")
    split = P("shard")
    return jax.shard_map(
        shards,
        mesh=cores,
        in_specs=(
            tokens,
            split,
            outer,
            outer,
            outer,
            conv,
            outer,
            split,
            turned,
            split,
            outer,
            outer,
            turned,
            tokens,
            P(None, "shard", ("cx", "core")),
        ),
        out_specs=(
            tokens,
            tokens,
            split,
            outer,
            outer,
            outer,
            conv,
            outer,
            split,
            turned,
            split,
            outer,
            outer,
            turned,
        ),
        check_vma=False,
    )
```

```python
import functools

import jax
import jax.numpy as jnp
from jax import lax
from jax.experimental import pallas as pl
from jax.experimental.pallas import tpu as pltpu
from jax.sharding import Mesh
from jax.sharding import PartitionSpec as P

EPSILON = 1e-06
F32 = jnp.float32
BF16 = jnp.bfloat16
LANES = 128
HALO = 16
SWAP = [(0, 1), (1, 0)]
LONG = 6 * 10**10


def mm(left, right, left_dim, right_dim):
    return lax.dot_general(
        left.astype(BF16),
        right.astype(BF16),
        (((left_dim,), (right_dim,)), ((), ())),
        preferred_element_type=F32,
    )


def nn(left, right):
    return mm(left, right, 1, 0)


def nt(left, right):
    return mm(left, right, 1, 1)


def tn(left, right):
    return mm(left, right, 0, 0)


def place_scalars():
    return jnp.stack([lax.axis_index("core"), lax.axis_index("cx")]).astype(jnp.int32)


def call(kernel, grid, in_specs, out_specs, out_shape, scratch=(), flops=1000):
    return pl.pallas_call(
        kernel,
        grid_spec=pltpu.PrefetchScalarGridSpec(
            num_scalar_prefetch=1,
            grid=grid,
            in_specs=in_specs,
            out_specs=out_specs,
            scratch_shapes=list(scratch),
        ),
        out_shape=out_shape,
        compiler_params=pltpu.CompilerParams(
            dimension_semantics=("arbitrary",) * len(grid), vmem_limit_bytes=48 << 20
        ),
        cost_estimate=pl.CostEstimate(flops=flops, transcendentals=0, bytes_accessed=1000),
    )


def pack_heads(places, query, key, value, heads):
    rows = query.shape[0]

    def kernel(where, query_ref, key_ref, value_ref, out):
        out[:, :LANES] = query_ref[...]
        out[:, LANES : 2 * LANES] = key_ref[...]
        out[:, 2 * LANES :] = value_ref[...]

    spec = pl.BlockSpec((rows, LANES), lambda h, w: (0, w[0] * heads + 2 * w[1] + h))
    return call(
        kernel,
        (2,),
        [spec] * 3,
        pl.BlockSpec((rows, 3 * LANES), lambda h, w: (0, h)),
        jax.ShapeDtypeStruct((rows, 6 * LANES), query.dtype),
    )(places, query, key, value)


def own_parts(units):
    wide = units // 2
    main = wide // (2 * LANES) * LANES
    return wide, main, wide - 2 * main


def own_units(places, weight, axis):
    wide, main, rest = own_parts(weight.shape[axis])
    first = lax.dynamic_slice_in_dim(weight, places[0] * wide + places[1] * main, main, axis)
    last = lax.dynamic_slice_in_dim(weight, places[0] * wide + 2 * main, rest, axis)
    low, high = jnp.split(last, 2, axis)
    return jnp.concatenate([first, jnp.where(places[1] == 0, low, high)], axis)


def own_heads(places, weight):
    rows = weight.shape[0] // 4
    return lax.dynamic_slice_in_dim(weight, (2 * places[0] + places[1]) * rows, rows, 0)


def pieces_of(own, *after):
    across = lax.ppermute(own, "cx", SWAP)
    late = tie(across, after)
    return [own, across, lax.ppermute(own, "core", SWAP), lax.ppermute(late, "core", SWAP)]


def pick(where, core, cx, refs, store):
    which = 2 * jnp.bitwise_xor(where[0], core) + jnp.bitwise_xor(where[1], cx)
    for index in range(4):

        @pl.when(which == index)
        def _():
            store(refs[index][...].astype(F32))


def lay_heads(places, heads):
    rows = heads[0][0].shape[0]

    def kernel(where, *refs):
        outs = refs[-3:]
        for head in range(2):

            def store(values):
                for index in range(3):
                    outs[index][:, head * LANES : (head + 1) * LANES] = values[
                        :, index * LANES : (index + 1) * LANES
                    ]

            pick(where, pl.program_id(0), pl.program_id(1), refs[4 * head : 4 * head + 4], store)

    return call(
        kernel,
        (2, 2),
        [pl.BlockSpec(heads[0][0].shape, lambda i, j, w: (0, 0))] * 8,
        [pl.BlockSpec((rows, 2 * LANES), lambda i, j, w: (0, 2 * i + j))] * 3,
        [jax.ShapeDtypeStruct((rows, 8 * LANES), F32)] * 3,
    )(places, *heads[0], *heads[1])


def lay_units(places, pieces, turn, flops=1000):
    units, rows = pieces[0].shape
    wide, main, rest = own_parts(4 * units)
    half = rest // 2

    def kernel(where, a, b, c, d, out):
        for side in range(2):

            def store(values):
                at = 2 * main + side * half
                if turn:
                    values = values.T
                    out[:, side * main : (side + 1) * main] = values[:, :main]
                    out[:, at : at + half] = values[:, main:]
                else:
                    out[side * main : (side + 1) * main, :] = values[:main]
                    out[at : at + half, :] = values[main:]

            pick(where, pl.program_id(0), side, (a, b, c, d), store)

    shape = (rows, wide) if turn else (wide, rows)
    return call(
        kernel,
        (2,),
        [pl.BlockSpec((units, rows), lambda i, w: (0, 0))] * 4,
        pl.BlockSpec(shape, (lambda i, w: (0, i)) if turn else (lambda i, w: (i, 0))),
        jax.ShapeDtypeStruct((rows, 2 * wide) if turn else (2 * wide, rows), F32),
        flops=flops,
    )(places, *pieces)


def lay_heads_turned(places, pieces):
    rows, columns = pieces[0].shape

    def kernel(where, a, b, c, d, out):
        def store(values):
            out[...] = values.T

        pick(where, pl.program_id(0), pl.program_id(1), (a, b, c, d), store)

    return call(
        kernel,
        (2, 2),
        [pl.BlockSpec((rows, columns), lambda i, j, w: (0, 0))] * 4,
        pl.BlockSpec((columns, rows), lambda i, j, w: (2 * i + j, 0)),
        jax.ShapeDtypeStruct((4 * columns, rows), F32),
    )(places, *pieces)


def fill_ext(ext, index, halo, first, second, size):
    ext[index, :HALO, :] = halo[...].astype(F32)
    ext[index, HALO : HALO + size, :] = first[...].astype(F32)
    ext[index, HALO + size :, :] = second[...].astype(F32)


def links_of(ids, total):
    own = ids[0, HALO : HALO + total, :]
    return [
        (ids[0, HALO - 3 + tap : HALO - 3 + tap + total, :] == own).astype(F32) for tap in range(4)
    ]


def conv_of(ext, index, taps, links, total):
    result = None
    for tap in range(4):
        term = (
            taps[index, 0, tap : tap + 1, :]
            * ext[index, HALO - 3 + tap : HALO - 3 + tap + total, :]
            * links[tap]
        )
        result = term if result is None else result + term
    return result


def sigmoid(values):
    return 1.0 / (1.0 + jnp.exp(-values))


def first_head(where, own):
    return 2 * (where[1] if own else 1 - where[1])


def head_of(where, own):
    return first_head(where, own) + pl.program_id(1)


def column_of(values, head):
    lane = lax.broadcasted_iota(jnp.int32, values.shape, 1)
    return jnp.sum(jnp.where(lane == head, values, 0.0), axis=1, keepdims=True)


def marks(ids, rows, chunk, size):
    start = HALO + chunk * size
    column = ids[0, start : start + size, :]
    before = ids[0, start - 1 : start, :]
    last = ids[0, start + size - 1 : start + size, :]
    first = (column == before).astype(F32)
    tail = (column == last).astype(F32)
    whole = (last == before).astype(F32)
    same = column == rows[0, chunk : chunk + 1, :]
    row = lax.broadcasted_iota(jnp.int32, (size, size), 0)
    col = lax.broadcasted_iota(jnp.int32, (size, size), 1)
    return first, tail, whole, same & (row > col), same & (row >= col)


def inverse_units(stricts, size):
    row = lax.broadcasted_iota(jnp.int32, (size, size), 0)
    col = lax.broadcasted_iota(jnp.int32, (size, size), 1)
    mixed = jnp.bitwise_xor(row, col)
    results = [
        jnp.where(row == col, 1.0, jnp.where(mixed == 1, -strict, 0.0)) for strict in stricts
    ]
    stricts = [strict.astype(BF16) for strict in stricts]
    block = 2
    while block < size:
        pair = (mixed >= block) & (mixed < 2 * block)
        lows = [result.astype(BF16) for result in results]
        parts = [jnp.where(pair, strict, 0.0) for strict in stricts]
        steps = [nn(part, low).astype(BF16) for part, low in zip(parts, lows)]
        results = [
            result - nn(low, step) for result, low, step in zip(results, lows, steps)
        ]
        block *= 2
    return [result.astype(BF16) for result in results]


def forward_one(where, q0, k0, v0, q1, k1, v1, qh, kh, vh, taps, ids, rows, r0, r1, *rest, size, own):
    query, key, value, inverse, final, ext = rest
    head = head_of(where, own)
    total = 2 * size
    for index, group in enumerate(((qh, q0, q1), (kh, k0, k1), (vh, v0, v1))):
        fill_ext(ext, index, *group, size)
    links = links_of(ids, total)
    out = []
    for index in range(3):
        conv = conv_of(ext, index, taps, links, total)
        act = conv * sigmoid(conv)
        if index < 2:
            act = act * lax.rsqrt(jnp.sum(act * act, axis=1, keepdims=True) + EPSILON)
        out.append(act.astype(BF16))
    for target, values in zip((query, key, value), out):
        target[0, 0] = values[:size]
        target[0, 1] = values[size:]
    chunks = []
    for chunk, rates in enumerate((r0, r1)):
        first, tail, whole, strict, _ = marks(ids, rows, chunk, size)
        rate = column_of(rates[...], head)
        keys = out[1][chunk * size : (chunk + 1) * size]
        chunks.append((first, tail, whole, rate, keys, jnp.where(strict, rate * nt(keys, keys), 0.0)))
    inverses = inverse_units([item[-1] for item in chunks], size)
    state = None
    for chunk, (first, tail, whole, rate, keys, _) in enumerate(chunks):
        fresh = out[2][chunk * size : (chunk + 1) * size].astype(F32)
        inverse[0, 0, chunk] = inverses[chunk]
        if chunk:
            fresh = fresh - first * nt(keys, state)
        fresh = nn(inverses[chunk], rate * fresh)
        added = tn(tail * fresh, keys)
        state = added if state is None else whole * state + added
    final[0, 0] = state.astype(BF16)


def forward_two(where, query, key, value, inverse, ids, rows, r0, r1, incoming, gain, *rest, size, scale, own):
    head_low, mixed_out, fresh_out, middle = rest
    head = head_of(where, own)
    state = incoming[0, 0].astype(F32)
    for chunk, rates in enumerate((r0, r1)):
        first, tail, whole, _, lower = marks(ids, rows, chunk, size)
        rate = column_of(rates[...], head)
        keys, queries = key[0, chunk], query[0, chunk]
        if chunk:
            middle[0, 0] = state.astype(BF16)
        rest_rows = value[0, chunk].astype(F32) - first * nt(keys, state)
        fresh = nn(inverse[0, 0, chunk], rate * rest_rows)
        fresh_out[0, chunk] = fresh.astype(BF16)
        inner = jnp.where(lower, nt(queries, keys), 0.0)
        mixed = scale * (first * nt(queries, state) + nn(inner, fresh))
        mixed_out[0, chunk] = mixed
        normed = mixed * lax.rsqrt(jnp.mean(mixed * mixed, axis=1, keepdims=True) + EPSILON)
        slot = where[0] if chunk == 0 else 1 - where[0]
        head_low[slot, 0] = (normed * gain[...]).astype(BF16)
        if chunk == 0:
            state = whole * state + tn(tail * fresh, keys)


def backward_one(where, d_head, mixed, query, key, inverse, ids, rows, r0, r1, gain, *rest, size, scale, own):
    d_out, d_state_out, d_gain = rest
    head = head_of(where, own)
    total = jnp.zeros((1, LANES), F32)
    d_state = None
    for chunk in (1, 0):
        first, tail, whole, _, lower = marks(ids, rows, chunk, size)
        rate = column_of((r0, r1)[chunk][...], head)
        keys, queries = key[0, chunk], query[0, chunk]
        slot = where[0] if chunk == 0 else 1 - where[0]
        grad = d_head[slot, 0].astype(F32)
        values = mixed[0, chunk]
        inv_rms = lax.rsqrt(jnp.mean(values * values, axis=1, keepdims=True) + EPSILON)
        normed = values * inv_rms
        total = total + jnp.sum(grad * normed, axis=0, keepdims=True)
        scaled = grad * gain[...]
        d_mixed = inv_rms * (scaled - normed * jnp.mean(scaled * normed, axis=1, keepdims=True))
        d_low = (scale * d_mixed).astype(BF16)
        d_out[0, chunk] = d_low
        inner = jnp.where(lower, nt(queries, keys), 0.0)
        d_fresh = tn(inner, d_low)
        if d_state is not None:
            d_fresh = d_fresh + tail * nt(keys, d_state)
        d_rest = rate * tn(inverse[0, 0, chunk], d_fresh)
        change = tn(first * d_low.astype(F32), queries) - tn(first * d_rest, keys)
        d_state = change if d_state is None else whole * d_state + change
    d_state_out[0, 0] = d_state.astype(BF16)
    d_gain[0, 0] = jnp.broadcast_to(total, (8, LANES))


def backward_two(where, q0, k0, v0, q1, k1, v1, qh, kh, vh, taps, ids, rows, r0, r1, *rest, size, own):
    query, key, value, inverse, fresh_in, d_in, incoming, middle, d_final = rest[:9]
    d_raw, d_edge, d_rates, d_taps = rest[9:13]
    ext, d_ext, d_rows = rest[13:]
    head = head_of(where, own)
    total = 2 * size
    for index, group in enumerate(((qh, q0, q1), (kh, k0, k1), (vh, v0, v1))):
        fill_ext(ext, index, *group, size)
    d_state = d_final[0, 0].astype(F32)

    @pl.when(pl.program_id(1) == 0)
    def _():
        d_rates[...] = jnp.zeros_like(d_rates)

    for chunk in (1, 0):
        first, tail, whole, strict, lower = marks(ids, rows, chunk, size)
        rate = column_of((r0, r1)[chunk][...], head)
        keys, queries, fresh = key[0, chunk], query[0, chunk], fresh_in[0, chunk]
        inv, d_low = inverse[0, 0, chunk], d_in[0, chunk]
        state = (middle if chunk else incoming)[0, 0]
        d_mix = d_low.astype(F32)
        inner = jnp.where(lower, nt(queries, keys), 0.0)
        gram = jnp.where(strict, nt(keys, keys), 0.0)
        d_fresh = tn(inner, d_low) + tail * nt(keys, d_state)
        turned = tn(inv, d_fresh)
        d_rest = rate * turned
        rest_rows = value[0, chunk].astype(F32) - first * nt(keys, state)
        error = rest_rows - nn(gram, fresh)
        d_rate = jnp.sum(turned * error, axis=1, keepdims=True) * rate * (1.0 - rate)
        d_inner = jnp.where(lower, nt(d_low, fresh), 0.0)
        d_gram = rate * jnp.where(strict, -nt(turned, fresh), 0.0)
        d_query = first * nn(d_low, state) + nn(d_inner, keys)
        d_key = (
            tn(d_inner, queries)
            + tail * nn(fresh, d_state)
            - nn(first * d_rest, state)
            + nn(d_gram, keys)
            + tn(d_gram, keys)
        )
        for index, values in enumerate((d_query, d_key, d_rest)):
            d_rows[index, chunk * size : (chunk + 1) * size, :] = values
        lane = lax.broadcasted_iota(jnp.int32, (size, LANES), 1)
        d_rates[0, chunk] = d_rates[0, chunk] + jnp.where(lane == head, d_rate, 0.0)
        if chunk:
            d_state = (
                whole * d_state + tn(first * d_mix, queries) - tn(first * d_rest, keys)
            )
    links = links_of(ids, total)
    for index in range(3):
        conv = conv_of(ext, index, taps, links, total)
        sig = sigmoid(conv)
        d_act = d_rows[index].astype(BF16).astype(F32)
        if index < 2:
            act = conv * sig
            inv_norm = lax.rsqrt(jnp.sum(act * act, axis=1, keepdims=True) + EPSILON)
            unit = act * inv_norm
            d_act = (d_act - unit * jnp.sum(unit * d_act, axis=1, keepdims=True)) * inv_norm
        d_conv = d_act * sig * (1.0 + conv * (1.0 - sig))
        d_ext[...] = jnp.zeros_like(d_ext)
        for tap in range(4):
            window = slice(HALO - 3 + tap, HALO - 3 + tap + total)
            linked = d_conv * links[tap]
            d_taps[0, index, 0, tap : tap + 1, :] = jnp.sum(
                linked * ext[index, window, :], axis=0, keepdims=True
            )
            d_ext[window, :] = d_ext[window, :] + taps[index, 0, tap : tap + 1, :] * linked
        lanes = slice(index * LANES, (index + 1) * LANES)
        d_edge[0, :, lanes] = d_ext[:HALO, :].astype(BF16)
        d_raw[where[0], 0, :, lanes] = d_ext[HALO : HALO + size, :].astype(BF16)
        d_raw[1 - where[0], 0, :, lanes] = d_ext[HALO + size :, :].astype(BF16)


def mixer_calls(places, own, rates, ids, rows, taps, gain, seqs, size, scale):
    def slot_of(chunk, w):
        return w[0] if chunk == 0 else 1 - w[0]

    def raw_spec(chunk, part):
        return pl.BlockSpec(
            (size, LANES), lambda b, h, w: (slot_of(chunk, w) * seqs + b, 3 * h + part)
        )

    def rate_spec(chunk):
        return pl.BlockSpec((size, LANES), lambda b, h, w: (slot_of(chunk, w) * seqs + b, 0))

    halo_base = 2 * seqs * size // HALO

    def halo_spec(part):
        return pl.BlockSpec((HALO, LANES), lambda b, h, w: (halo_base + b, 3 * h + part))

    conv_specs = (
        [raw_spec(c, p) for c in range(2) for p in range(3)]
        + [halo_spec(p) for p in range(3)]
        + [
            pl.BlockSpec((3, 1, 4, LANES), lambda b, h, w: (0, first_head(w, own) + h, 0, 0)),
            pl.BlockSpec((1, HALO + 2 * size, 1), lambda b, h, w: (b, 0, 0)),
            pl.BlockSpec((1, 2, size), lambda b, h, w: (b, 0, 0)),
            rate_spec(0),
            rate_spec(1),
        ]
    )
    rest_args = (taps, ids, rows, rates, rates)
    id_specs, id_args = conv_specs[10:], rest_args[1:]
    act_spec = pl.BlockSpec((1, 2, size, LANES), lambda b, h, w: (b, 0, 0, h))
    act_shape = (seqs, 2, size, 2 * LANES)
    state_spec = pl.BlockSpec((1, 1, LANES, LANES), lambda b, h, w: (b, h, 0, 0))
    state_shape = jax.ShapeDtypeStruct((seqs, 2, LANES, LANES), BF16)
    inv_spec = pl.BlockSpec((1, 1, 2, size, size), lambda b, h, w: (b, h, 0, 0, 0))
    inv_shape = jax.ShapeDtypeStruct((seqs, 2, 2, size, size), BF16)
    slot_spec = pl.BlockSpec((2, 1, size, LANES), lambda b, h, w: (0, b, 0, h))
    slot_shape = jax.ShapeDtypeStruct((2, seqs, size, 2 * LANES), BF16)
    gain_spec = pl.BlockSpec((1, LANES), lambda b, h, w: (0, 0))
    low = jax.ShapeDtypeStruct(act_shape, BF16)
    grid = (seqs, 2)

    def one(raw):
        return call(
            functools.partial(forward_one, size=size, own=own),
            grid,
            conv_specs,
            [act_spec] * 3 + [inv_spec, state_spec],
            [low] * 3 + [inv_shape, state_shape],
            [pltpu.VMEM((3, HALO + 2 * size, LANES), F32)],
        )(places, *(raw,) * 9, *rest_args)

    def two(query, key, value, inverse, incoming):
        args = (query, key, value, inverse, *id_args, incoming, gain)
        return call(
            functools.partial(forward_two, size=size, scale=scale, own=own),
            grid,
            [act_spec] * 3
            + [inv_spec]
            + id_specs
            + [state_spec, gain_spec],
            [slot_spec, act_spec, act_spec, state_spec],
            [slot_shape, jax.ShapeDtypeStruct(act_shape, F32), low, state_shape],
        )(places, *args)

    def three(d_head, mixed, query, key, inverse):
        return call(
            functools.partial(backward_one, size=size, scale=scale, own=own),
            grid,
            [slot_spec, act_spec, act_spec, act_spec, inv_spec] + id_specs + [gain_spec],
            [act_spec, state_spec, pl.BlockSpec((1, 1, 8, LANES), lambda b, h, w: (b, h, 0, 0))],
            [low, state_shape, jax.ShapeDtypeStruct((seqs, 2, 8, LANES), F32)],
            flops=int(26 * 1.1e9),
        )(places, d_head, mixed, query, key, inverse, *id_args, gain)

    def four(raw, query, key, value, inverse, fresh, d_low, incoming, middle, d_final):
        return call(
            functools.partial(backward_two, size=size, own=own),
            grid,
            conv_specs + [act_spec] * 3 + [inv_spec, act_spec, act_spec] + [state_spec] * 3,
            [
                pl.BlockSpec((2, 1, size, 3 * LANES), lambda b, h, w: (0, b, 0, h)),
                pl.BlockSpec((1, HALO, 3 * LANES), lambda b, h, w: (b, 0, h)),
                pl.BlockSpec((1, 2, size, LANES), lambda b, h, w: (b, 0, 0, 0)),
                pl.BlockSpec((1, 3, 1, 4, LANES), lambda b, h, w: (b, 0, h, 0, 0)),
            ],
            [
                jax.ShapeDtypeStruct((2, seqs, size, 6 * LANES), BF16),
                jax.ShapeDtypeStruct((seqs, HALO, 6 * LANES), BF16),
                jax.ShapeDtypeStruct((seqs, 2, size, LANES), F32),
                jax.ShapeDtypeStruct((seqs, 3, 2, 4, LANES), F32),
            ],
            [
                pltpu.VMEM((3, HALO + 2 * size, LANES), F32),
                pltpu.VMEM((HALO + 2 * size, LANES), F32),
                pltpu.VMEM((3, 2 * size, LANES), F32),
            ],
            flops=int(26 * 1.1e9),
        )(
            places,
            *(raw,) * 9,
            *rest_args,
            query,
            key,
            value,
            inverse,
            fresh,
            d_low,
            incoming,
            middle,
            d_final,
        )

    return one, two, three, four


def tile_of(extent):
    return 512 if extent % 512 == 0 else extent


def rows_products(pairs, rows, block, add=None, out=BF16, flops=1000):
    columns = pairs[0][1].shape[0]
    tile = tile_of(columns)
    count = len(pairs)

    def kernel(*refs):
        total = None
        for index in range(count):
            part = nt(refs[index][...], refs[count + index][...])
            total = part if total is None else total + part
        if add is not None:
            total = total + refs[2 * count][...].astype(F32)
        refs[-1][...] = total.astype(out)

    lefts = [pl.BlockSpec((rows, left.shape[1]), lambda i: (block, 0)) for left, _ in pairs]
    rights = [pl.BlockSpec((tile, right.shape[1]), lambda i: (i, 0)) for _, right in pairs]
    spec = pl.BlockSpec((rows, tile), lambda i: (0, i))
    extra = () if add is None else (add,)
    return pl.pallas_call(
        kernel,
        grid=(columns // tile,),
        in_specs=lefts + rights + [spec] * len(extra),
        out_specs=spec,
        out_shape=jax.ShapeDtypeStruct((rows, columns), out),
        compiler_params=pltpu.CompilerParams(vmem_limit_bytes=48 << 20),
        cost_estimate=pl.CostEstimate(flops=flops, transcendentals=0, bytes_accessed=1000),
    )(*(left for left, _ in pairs), *(right for _, right in pairs), *extra)


def token_products(pairs, add=None, flops=1000):
    count = len(pairs)
    height, columns = pairs[0][0].shape[1], pairs[0][1].shape[1]
    tile = tile_of(height)

    def kernel(*refs):
        total = None
        for index in range(count):
            part = tn(refs[index][...], refs[count + index][...])
            total = part if total is None else total + part
        if add is not None:
            total = total + refs[2 * count][...].astype(F32)
        refs[-1][...] = total.astype(BF16)

    lefts = [
        pl.BlockSpec((rows, tile), lambda i, block=block: (block, i))
        for _, _, rows, block in pairs
    ]
    rights = [pl.BlockSpec((rows, columns), lambda i: (0, 0)) for _, _, rows, _ in pairs]
    spec = pl.BlockSpec((tile, columns), lambda i: (i, 0))
    extra = () if add is None else (add,)
    return pl.pallas_call(
        kernel,
        grid=(height // tile,),
        in_specs=lefts + rights + [spec] * len(extra),
        out_specs=spec,
        out_shape=jax.ShapeDtypeStruct((height, columns), BF16),
        compiler_params=pltpu.CompilerParams(vmem_limit_bytes=48 << 20),
        cost_estimate=pl.CostEstimate(flops=flops, transcendentals=0, bytes_accessed=1000),
    )(*(item[0] for item in pairs), *(item[1] for item in pairs), *extra)


def feed_forward(rows, grads, gates, ups, downs):
    tokens, width = rows.shape
    units = gates.shape[1]
    tile = 256 if tokens % 256 == 0 else tokens

    def kernel(rows_ref, grads_ref, gates_ref, ups_ref, downs_ref, act, d_gate, d_up):
        gate = nn(rows_ref[...], gates_ref[...])
        up = nn(rows_ref[...], ups_ref[...])
        d_act = nn(grads_ref[...], downs_ref[...]).astype(BF16).astype(F32)
        sig = sigmoid(gate)
        act[...] = (gate * sig * up).astype(BF16)
        d_gate[...] = (d_act * up * sig * (1.0 + gate * (1.0 - sig))).astype(BF16)
        d_up[...] = (d_act * gate * sig).astype(BF16)

    token_spec = pl.BlockSpec((tile, width), lambda i: (i, 0))
    weight_spec = pl.BlockSpec((width, units), lambda i: (0, 0))
    unit_spec = pl.BlockSpec((tile, units), lambda i: (i, 0))
    return pl.pallas_call(
        kernel,
        grid=(tokens // tile,),
        in_specs=[token_spec] * 2 + [weight_spec] * 3,
        out_specs=[unit_spec] * 3,
        out_shape=[jax.ShapeDtypeStruct((tokens, units), BF16)] * 3,
        compiler_params=pltpu.CompilerParams(vmem_limit_bytes=48 << 20),
        cost_estimate=pl.CostEstimate(flops=1000, transcendentals=0, bytes_accessed=1000),
    )(rows, grads, gates, ups, downs)


def dot_nn(left, right):
    return lax.dot_general(left, right, (((1,), (0,)), ((), ())), preferred_element_type=F32)


def dot_nt(left, right):
    return lax.dot_general(left, right, (((1,), (1,)), ((), ())), preferred_element_type=F32)


def dot_tn(left, right):
    return lax.dot_general(left, right, (((0,), (0,)), ((), ())), preferred_element_type=F32)


def rms(values, gain):
    return values * lax.rsqrt(jnp.mean(values * values, axis=1, keepdims=True) + EPSILON) * gain


def tie(value, *after):
    return lax.optimization_barrier((value, after))[0]


class Steps:
    def __init__(self):
        self.last = ()

    def wait(self, *values):
        self.last = (self.last, values)

    def __call__(self, fn, *args):
        traced, static = [], []
        for arg in args:
            leaves = jax.tree.leaves(arg)
            static.append(not leaves or not all(hasattr(leaf, "dtype") for leaf in leaves))
            if not static[-1]:
                traced.append(arg)
        traced = iter(tie(tuple(traced), self.last))
        result = fn(*(arg if fixed else next(traced) for arg, fixed in zip(args, static)))
        self.last = result
        return result


def sum_over(values, axis, hop):
    partners = [(index, index ^ hop) for index in range(lax.axis_size(axis))]
    return (values.astype(F32) + lax.ppermute(values, axis, partners).astype(F32)).astype(BF16)


def shards(
    hidden_in,
    attn_gain,
    query_weight,
    key_weight,
    value_weight,
    conv_weight,
    beta_weight,
    out_gain,
    out_weight,
    ffn_gain,
    gate_weight,
    up_weight,
    down_weight,
    cotangent,
    segment_ids,
):
    count = lax.axis_size("shard")
    places = place_scalars()
    core, cx = places[0], places[1]
    micro, local, size, width = hidden_in.shape
    seqs = micro * local
    own_rows = seqs * size
    heads_tp = conv_weight.shape[2]
    heads = heads_tp // 2
    scale = LANES ** (-0.5)
    first_rows, other_rows = slice(0, own_rows), slice(own_rows, 2 * own_rows)

    def gathered(piece):
        return lax.all_gather(piece, "shard", axis=0, tiled=True)

    def over_shard(total):
        return lax.psum_scatter(total, "shard", scatter_dimension=0, tiled=True)

    def across(part):
        return lax.ppermute(part, "cx", SWAP)

    def to_core(part):
        return lax.ppermute(part, "core", SWAP)

    def with_core(part):
        return jnp.concatenate([part, to_core(part)])

    pack = pack_heads(places, query_weight, key_weight, value_weight, heads)
    joint_own = gathered(pack)

    small = jnp.concatenate(
        [
            attn_gain,
            ffn_gain,
            out_gain,
            conv_weight.reshape(-1),
            beta_weight.reshape(-1),
        ]
    )
    unpadded = small.size
    small = jnp.pad(small, (0, -unpadded % (16 * LANES))).reshape(-1, LANES)
    small = lax.all_gather(small, "shard", axis=0).reshape(count, -1)
    piece_d = attn_gain.shape[0]
    entry = out_gain.shape[0]
    at = 2 * piece_d + entry
    gain_in = small[:, :piece_d].reshape(1, -1).astype(F32)
    gain_ffn = small[:, piece_d : 2 * piece_d].reshape(1, -1).astype(F32)
    gain_head = small[:, 2 * piece_d : at].reshape(1, LANES).astype(F32)
    conv_size = conv_weight.size
    taps = small[:, at : at + conv_size].reshape(count, 4, 3, heads_tp, entry)
    taps = taps.transpose(2, 3, 1, 0, 4).reshape(3, heads_tp, 4, LANES)
    taps = lax.dynamic_slice_in_dim(taps, core * heads, heads, axis=1).astype(F32)
    beta = small[:, at + conv_size : unpadded].reshape(width, heads_tp)
    beta = lax.dynamic_slice_in_dim(beta, core * heads, heads, axis=1)
    beta = jnp.pad(beta, ((0, 0), (0, LANES - heads)))

    hidden_own = hidden_in.reshape(own_rows, width)
    hidden_other = to_core(hidden_own)
    ids_own = segment_ids.reshape(seqs, size)
    ids_other = to_core(ids_own)
    late = jnp.where(core == 1, hidden_own, hidden_other).reshape(seqs, size, width)[:, size - HALO :]
    early_ids = jnp.where(core == 0, ids_own, ids_other)
    late_ids = jnp.where(core == 1, ids_own, ids_other)
    halo = lax.ppermute(late, "cx", [(0, 1)]).reshape(seqs * HALO, width)
    halo_ids = lax.ppermute(late_ids[:, size - HALO :], "cx", [(0, 1)])
    halo_ids = jnp.where(cx == 0, -1, halo_ids)
    ids = jnp.concatenate([halo_ids, early_ids, late_ids], axis=1)[..., None]
    id_rows = jnp.stack([early_ids, late_ids], axis=1)
    hidden_all = jnp.concatenate([hidden_own, hidden_other, halo])
    normed_low = rms(hidden_all.astype(F32), gain_in).astype(BF16)
    rates = sigmoid(dot_nn(normed_low, beta))
    grad_own = cotangent.reshape(own_rows, width)
    grad_near = with_core(grad_own)
    grad_far = with_core(across(grad_own))

    outer_own = gathered(tie(own_heads(places, out_weight).T, pack))
    gates = gathered(tie(own_units(places, gate_weight, 1), pack, hidden_all))
    ups = gathered(tie(own_units(places, up_weight, 1), normed_low, rates))
    downs = gathered(tie(own_units(places, down_weight, 0).T, grad_near, grad_far))
    joint_other = across(tie(joint_own, grad_far, ids, id_rows, normed_low))

    steps = Steps()
    shapes = (rates, ids, id_rows, taps, gain_head, seqs, size, scale)
    own_calls = mixer_calls(places, True, *shapes)
    other_calls = mixer_calls(places, False, *shapes)

    def project(rows, weight):
        return dot_nn(rows, weight).astype(BF16)

    raw_own = steps(project, normed_low, joint_own)
    first_own = steps(own_calls[0], raw_own)
    outer_other = across(tie(outer_own, joint_other, first_own[-1]))
    raw_other = steps(project, normed_low, joint_other)
    first_other = steps(other_calls[0], raw_other)
    in_other = lax.ppermute(first_own[-1], "cx", [(0, 1)])
    in_own = lax.ppermute(first_other[-1], "cx", [(0, 1)])
    head_other, mixed_other, fresh_other, middle_other = steps(
        other_calls[1], *first_other[:4], in_other
    )
    head_own, mixed_own, fresh_own, middle_own = steps(own_calls[1], *first_own[:4], in_own)
    slots = head_own.shape
    head_own, head_other = (part.reshape(2 * own_rows, -1) for part in (head_own, head_other))

    def products(block, lefts, rights, add=None, out=BF16, flops=1000):
        return rows_products(list(zip(lefts, rights)), own_rows, block, add, out, flops)

    def away(*pairs, flops=1000):
        lefts, rights = zip(*pairs)
        return to_core(steps(lambda *args: products(1, *args, flops=flops), lefts, rights))

    def here(arrived, *pairs, out=BF16):
        lefts, rights = zip(*pairs)
        return steps(lambda *args: products(0, *args, out), lefts, rights, arrived)

    def with_tp(part):
        return part, lax.ppermute(part, "tp", SWAP)

    def pair_sum(pair):
        return pair[0].astype(F32) + pair[1].astype(F32)

    pairs = ((head_own, outer_own), (head_other, outer_other))
    mixer_pair = with_tp(here(away(*pairs), *pairs))
    hidden_f32 = hidden_own.astype(F32)

    def resid_step(pair, hidden):
        resid = hidden + pair_sum(pair)
        return resid, rms(resid, gain_ffn).astype(BF16)

    steps.wait(ups)
    resid, ffn_own = steps(resid_step, mixer_pair, hidden_f32)
    ffn_far_own = across(ffn_own)
    ffn_near = with_core(ffn_own)

    weights = (gates, ups, downs)
    act_near, d_gate_near, d_up_near = steps(feed_forward, ffn_near, grad_near, *weights)
    near = ((d_gate_near, gates), (d_up_near, ups))
    near_arrived = away(*near)
    down_near_arrived = away((act_near, downs))
    ffn_far = with_core(tie(ffn_far_own, down_near_arrived))
    act_far, d_gate_far, d_up_far = steps(feed_forward, ffn_far, grad_far, *weights)
    far = ((d_gate_far, gates), (d_up_far, ups))

    def both_grads(near, far, grads_near, grads_far):
        rows = near.shape[0]
        return token_products([(near, grads_near, rows, 0), (far, grads_far, rows, 0)])

    d_ffn_sent = across(here(away(*far), *far))
    grad_down = over_shard(steps(both_grads, grad_near, grad_far, act_near, act_far))
    d_ffn_near = here(near_arrived, *near, out=F32)
    down_far_arrived = away((act_far, downs))
    grad_gate = over_shard(steps(both_grads, ffn_near, ffn_far, d_gate_near, d_gate_far))

    def add_far(near, arrived):
        return (near + arrived.astype(F32)).astype(BF16)

    d_ffn_pair = with_tp(steps(add_far, d_ffn_near, d_ffn_sent))
    grad_up = over_shard(steps(both_grads, ffn_near, ffn_far, d_up_near, d_up_far))
    down_sent = across(here(down_far_arrived, (act_far, downs)))
    down_near = here(down_near_arrived, (act_near, downs), out=F32)

    def resid_back(pair, resid, grads):
        _, pull = jax.vjp(rms, resid, gain_ffn)
        d_resid, sum_ffn_gain = pull(pair_sum(pair))
        d_resid = grads.astype(F32) + d_resid
        return d_resid, sum_ffn_gain, d_resid.astype(BF16)

    d_resid, sum_ffn_gain, resid_own = steps(resid_back, d_ffn_pair, resid, grad_own)
    resid_other = to_core(resid_own)
    resid_low = steps(lambda own, other: jnp.concatenate([own, other]), resid_own, resid_other)

    def grad_of(rows, grads, *arrived, flops=1000):
        return token_products([(rows, grads, 2 * own_rows, 0)], *arrived, flops=flops)

    d_head_own = steps(project, resid_low, outer_own).reshape(slots)
    d_head_other = steps(project, resid_low, outer_other).reshape(slots)
    steps.wait(grad_down)
    third_own = steps(own_calls[2], d_head_own, mixed_own, *first_own[:2], first_own[3])
    d_final_other = lax.ppermute(third_own[1], "cx", [(1, 0)])
    third_other = steps(other_calls[2], d_head_other, mixed_other, *first_other[:2], first_other[3])
    d_final_own = lax.ppermute(third_other[1], "cx", [(1, 0)])
    outer_sent = across(steps(grad_of, resid_low, head_other))
    down_pair = with_tp(steps(add_far, down_near, down_sent))
    sum_head_gain = steps(
        lambda *parts: sum(jnp.sum(part[:, :, 0, :], axis=(0, 1)) for part in parts).astype(BF16),
        third_own[2],
        third_other[2],
    )
    sum_head_gain = sum_over(sum_head_gain, "tp", 1)
    steps.wait(d_final_own, d_final_other, sum_head_gain)
    steps.wait(grad_gate)
    fourth_other = steps(
        other_calls[3],
        raw_other,
        *first_other[:4],
        fresh_other,
        third_other[0],
        in_other,
        middle_other,
        d_final_other,
    )
    edge_own = lax.ppermute(fourth_other[1], "cx", [(1, 0)])
    normed_rows = normed_low[: 2 * own_rows]

    def joint_grad(half, d_raw, d_edge, *arrived, flops=1000):
        lanes = slice(half * 3 * LANES, (half + 1) * 3 * LANES)
        d_raw = d_raw.reshape(2 * own_rows, -1)[:, lanes]
        d_edge = d_edge.reshape(seqs * HALO, -1)[:, lanes]
        pairs = [(normed_low, d_raw, 2 * own_rows, 0)]
        pairs += [(normed_low, d_edge, seqs * HALO, 2 * own_rows // (seqs * HALO))]
        return token_products(pairs, *arrived, flops=flops)

    out_down = steps(
        lambda pieces: lay_units(places, pieces, False, 1000), pieces_of(grad_down.T, fourth_other[1])
    )
    joint_dots = [
        steps(functools.partial(joint_grad, half), *fourth_other[:2]) for half in range(2)
    ]
    joint_sent = [across(joint_dots[0])]
    steps.wait(outer_sent, grad_up)
    fourth_own = steps(
        own_calls[3],
        raw_own,
        *first_own[:4],
        fresh_own,
        third_own[0],
        in_own,
        middle_own,
        d_final_own,
    )
    edge_other = lax.ppermute(fourth_own[1], "cx", [(1, 0)])
    result_rows = steps(
        lambda pair, resid: (resid + pair_sum(pair)).astype(BF16), down_pair, resid
    )
    steps.wait(joint_sent[0])
    joint_sent.append(across(tie(joint_dots[1], edge_other)))
    def with_edge(d_raw, d_edge):
        window = (1 - core, 0, size - HALO, 0)
        edge_rows = lax.dynamic_slice(d_raw, window, (1,) + d_edge.shape)
        return lax.dynamic_update_slice(
            d_raw, (edge_rows.astype(F32) + d_edge.astype(F32)[None]).astype(BF16), window
        ).reshape(2 * own_rows, -1)

    def logit_step(rates, rows):
        d_rates = sum(rates)
        d_logit = jnp.where(core == 0, d_rates, d_rates[:, ::-1]).transpose(1, 0, 2, 3)
        d_logit = d_logit.reshape(2 * own_rows, LANES).astype(BF16)
        return d_logit, dot_tn(rows, d_logit)[:, :heads]

    d_logit, sum_rate = steps(logit_step, [fourth_own[2], fourth_other[2]], normed_rows)
    d_raw_own = steps(with_edge, fourth_own[0], edge_own)
    d_raw_other = steps(with_edge, fourth_other[0], edge_other)

    pairs = ((d_raw_own, joint_own), (d_raw_other, joint_other), (d_logit, beta))
    d_normed_pair = with_tp(here(away(*pairs, flops=LONG), *pairs))
    grad_outer = over_shard(steps(functools.partial(grad_of, flops=LONG), resid_low, head_own, outer_sent))
    grad_joint = [
        over_shard(steps(functools.partial(joint_grad, 0), *fourth_own[:2], joint_sent[0]))
    ]
    joint_total = steps(functools.partial(joint_grad, 1), *fourth_own[:2], joint_sent[1])
    grad_joint.append(over_shard(joint_total))
    steps.wait(grad_joint[0])
    out_gate = steps(
        lambda pieces: lay_units(places, pieces, True, 1000), pieces_of(grad_gate.T, grad_joint[0])
    )

    def input_back(pair, d_resid, hidden):
        _, pull = jax.vjp(rms, hidden, gain_in)
        d_hidden, sum_attn_gain = pull(pair_sum(pair))
        return sum_attn_gain, (d_resid + d_hidden).astype(BF16)

    sum_attn_gain, input_rows = steps(input_back, d_normed_pair, d_resid, hidden_f32)
    out_up = steps(
        lambda pieces: lay_units(places, pieces, True, LONG), pieces_of(grad_up.T, sum_attn_gain)
    )
    out_outer = steps(lambda pieces: lay_heads_turned(places, pieces), pieces_of(grad_outer))

    sum_taps = [jnp.sum(fourth[3], axis=0).transpose(2, 0, 1, 3) for fourth in (fourth_own, fourth_other)]
    sum_taps = jnp.where(
        cx == 0, jnp.concatenate(sum_taps, axis=2), jnp.concatenate(sum_taps[::-1], axis=2)
    )
    gains = jnp.concatenate([sum_attn_gain[0], sum_ffn_gain[0]]).astype(BF16)
    gains = sum_over(jnp.concatenate([gains, sum_head_gain]), "core", 1)
    packed = jnp.concatenate(
        [gains, sum_taps.reshape(-1).astype(BF16), sum_rate.reshape(-1).astype(BF16)]
    )
    packed = sum_over(packed, "cx", 1)
    hop = 1
    while hop < count:
        packed = sum_over(packed, "shard", hop)
        hop *= 2
    own = lax.axis_index("shard")
    ends = [width, 2 * width, 2 * width + LANES, 2 * width + LANES + sum_taps.size]
    grad_attn_gain = lax.dynamic_slice_in_dim(packed[: ends[0]], own * piece_d, piece_d)
    grad_ffn_gain = lax.dynamic_slice_in_dim(packed[ends[0] : ends[1]], own * piece_d, piece_d)
    grad_out_gain = lax.dynamic_slice_in_dim(packed[ends[1] : ends[2]], own * entry, entry)
    own_conv = lax.dynamic_slice_in_dim(
        packed[ends[2] : ends[3]].reshape(4, 3, heads, LANES), own * entry, entry, axis=3
    )
    own_beta = lax.dynamic_slice_in_dim(
        packed[ends[3] :].reshape(width, heads), own * piece_d, piece_d, axis=0
    )

    def both_cores(values, axis):
        other = to_core(values)
        return jnp.where(
            core == 0,
            jnp.concatenate([values, other], axis=axis),
            jnp.concatenate([other, values], axis=axis),
        ).astype(F32)

    out_query, out_key, out_value = lay_heads(places, [pieces_of(part) for part in grad_joint])
    return (
        result_rows.reshape(hidden_in.shape),
        input_rows.reshape(hidden_in.shape),
        grad_attn_gain.astype(F32),
        out_query,
        out_key,
        out_value,
        both_cores(own_conv, 2),
        both_cores(own_beta, 1),
        grad_out_gain.astype(F32),
        out_outer,
        grad_ffn_gain.astype(F32),
        out_gate,
        out_up,
        out_down,
    )


def solution(mesh):
    shard, ctx, tp = (mesh.shape[name] for name in ("shard", "ctx", "tp"))
    cores = Mesh(
        mesh.devices.reshape(shard, ctx // 2, 2, tp), ("shard", "cx", "core", "tp")
    )
    tokens = P(None, "shard", ("cx", "core"), None)
    outer = P("shard", "tp")
    turned = P("tp", "shard")
    conv = P(None, None, "tp", "shard")
    split = P("shard")
    return jax.shard_map(
        shards,
        mesh=cores,
        in_specs=(
            tokens,
            split,
            outer,
            outer,
            outer,
            conv,
            outer,
            split,
            turned,
            split,
            outer,
            outer,
            turned,
            tokens,
            P(None, "shard", ("cx", "core")),
        ),
        out_specs=(
            tokens,
            tokens,
            split,
            outer,
            outer,
            outer,
            conv,
            outer,
            split,
            turned,
            split,
            outer,
            outer,
            turned,
        ),
        check_vma=False,
    )
```
